512 devices in a mesh: fsdp: 64 (over x, y, z_hi, core), ctx: 8 (over z_lo).
Axes of the slice: x: 4, y: 4, z: 16 (z_hi: 2, z_lo: 8; z = z_hi * 8 + z_lo), core: 2. Of those that a mesh axis runs over, the one named last changes fastest.
Arguments:
- token_ids: int32 [1024], P('ctx'), may hold values from 0 to 511
- embed: bfloat16 [512, 8192], P(None, 'fsdp'), may hold values from -6 to 6
- w_in: bfloat16 [8192, 3, 8192], P('ctx', None, 'fsdp'), may hold values from -0.1875 to 0.1875
- taps: float32 [7, 3, 8192], P(None, None, 'fsdp'), may hold values from -2 to 2
- rates: float32 [16, 8192], P(None, 'fsdp'), may hold values from 9.765625e-05 to 0.08, as said below
- residues: float32 [16, 8192], P(None, 'fsdp'), may hold values from -0.15 to 0.15
- cotangent: bfloat16 [1024, 8192], P('ctx', 'fsdp'), may hold values from -6 to 6
Outputs:
- mixed: bfloat16 [1024, 8192], P('ctx', 'fsdp')
- input_grad: bfloat16 [1024, 8192], P('ctx', 'fsdp')
The draws below stay inside these ranges and needn't reach their ends.
Inputs may be any that keep to these rules, and one draw needn't show every extreme that they name: `rates`: every rate lies between 0.1 / 1024 and 0.08.
All inputs are finite; a program needn't handle non-finite values.
Results may differ from the reference program's by a relative error of at most 0.0064.
Values may be sent and summed in bfloat16 or wider, within the bound.
A program may use at most 64 MiB of HBM per device.

```python
import math
import jax
import jax.numpy as jnp
from jax import lax

D = 8192
VOCAB = 512
MODES = 16
KSHORT = 7
SEQ = 1024


def draw_rates(key, part):
    spread = jax.random.uniform(key, (MODES, D), jnp.float32)
    lowest = math.log(0.1 / SEQ)
    highest = math.log(0.08)
    return jnp.exp(lowest + (highest - lowest) * spread).astype(jnp.float32)


def set_ends(values, stream_key, smallest, top_value):
    place = [jax.random.randint(jax.random.fold_in(stream_key, axis), (), 0, length) for axis, length in enumerate(values.shape)]
    main_axis = values.shape.index(max(values.shape))
    beside = place[:main_axis] + [(place[main_axis] + 1) % values.shape[main_axis]] + place[main_axis + 1:]
    return values.at[tuple(place)].set(smallest).at[tuple(beside)].set(top_value)


def with_spikes(drawn, key, source, target, parts, factor):
    def block_of(axis_at):
        return (jnp.arange(drawn.shape[axis_at]) // (drawn.shape[axis_at] // parts)).reshape((-1,) + (1,) * (drawn.ndim - 1 - axis_at))

    near = jax.random.permutation(key, parts)[block_of(target)]
    second = (block_of(target) + parts // 2) % parts
    return jnp.where((block_of(source) == near) | (block_of(source) == second), factor * drawn, drawn)


def steps_of(own_key, dims, cuts, least, top_value):
    def one(position, shards_of):
        heights = jax.random.uniform(jax.random.fold_in(jax.random.fold_in(own_key, 6), position), (shards_of,), jnp.float32, least / len(cuts), top_value / len(cuts))
        return jnp.repeat(jnp.exp(heights), dims[position] // shards_of).reshape((-1,) + (1,) * (len(dims) - position - 1))

    gain = one(*cuts[0])
    for cut in cuts[1:]:
        gain = gain * one(*cut)
    return gain


def centred(rng, extent, deviation, limit, shards=(), kind=jnp.bfloat16):
    factor_of = steps_of(rng, extent, shards, -0.22, 0.18) if shards else 1.0
    values = jax.random.normal(rng, extent, jnp.float32) * deviation * factor_of
    return jnp.minimum(jnp.maximum(values, -limit), limit).astype(kind)


def gaussian_with(own_key, extent, scale, limit, cuts, heavy, kind=jnp.bfloat16):
    array = scale * jax.random.normal(own_key, extent, jnp.float32)
    if cuts:
        array = array * steps_of(own_key, extent, cuts, -0.22, 0.18)
    return jnp.clip(with_spikes(array, jax.random.fold_in(own_key, 3), *heavy), -limit, limit).astype(kind)


def setup_inputs(seed: int = 0) -> dict:
    keys = jax.random.split(jax.random.key(seed), 8)
    return {
        "token_ids": set_ends(jax.random.randint(keys[0], (SEQ,), 0, VOCAB), jax.random.fold_in(keys[0], 1), 0, VOCAB - 1).astype(jnp.int32),
        "embed": centred(keys[1], (VOCAB, D), 1.0, 6.0, ((1, 64),)),
        "w_in": gaussian_with(keys[2], (D, 3, D), D ** -0.5, 0.1875, ((0, 8), (2, 64)), (2, 0, 64, 4.0)),
        "taps": centred(keys[3], (KSHORT, 3, D), 0.4, 2.0, ((2, 64),), jnp.float32),
        "rates": draw_rates(jax.random.fold_in(keys[7], 71), 0),
        "residues": centred(keys[5], (MODES, D), 0.03, 0.15, ((1, 64),), jnp.float32),
        "cotangent": centred(keys[6], (SEQ, D), 1.0, 6.0, ((0, 8), (1, 64))),
    }


def pair_combine(earlier, later):
    return (earlier[0] * later[0], later[0] * earlier[1] + later[1])


def modal_states(drive, step_decay):
    tok_count = drive.shape[0]
    factors = jnp.broadcast_to(step_decay[None], (tok_count,) + step_decay.shape)
    inputs = jnp.broadcast_to(drive[:, None, :], factors.shape)
    return lax.associative_scan(pair_combine, (factors, inputs), axis=0)[1]


def short_filter(extended, taps, tok_count):
    rim_width = taps.shape[0] - 1
    filtered = taps[0] * extended[rim_width:rim_width + tok_count]
    for shift_lag in range(1, rim_width + 1):
        filtered = filtered + taps[shift_lag] * extended[rim_width - shift_lag:rim_width - shift_lag + tok_count]
    return filtered


def short_adjoint(extended, taps, tok_count):
    rim_width = taps.shape[0] - 1
    result = taps[0] * extended[:tok_count]
    for shift_lag in range(1, rim_width + 1):
        result = result + taps[shift_lag] * extended[shift_lag:shift_lag + tok_count]
    return result


def block_mix(stored, grad_out, taps, rates, residues):
    tok_count = stored.shape[0]
    rim_width = taps.shape[0] - 1
    leading = jnp.zeros((rim_width,) + stored.shape[1:], jnp.bfloat16)
    extended = jnp.concatenate([leading, stored], axis=0).astype(jnp.float32)
    filtered = short_filter(extended, taps, tok_count)
    query_part = filtered[:, 0]
    key_part = filtered[:, 1]
    value_part = filtered[:, 2]
    drive = key_part * value_part
    step_decay = jnp.exp(-rates)
    states = modal_states(drive, step_decay)
    long_out = jnp.sum(residues[None] * states, axis=1)
    mixed = (query_part * long_out).astype(jnp.bfloat16)
    incoming = grad_out.astype(jnp.float32)
    grad_long = incoming * query_part
    grad_query = incoming * long_out
    adjoint = jnp.flip(modal_states(jnp.flip(grad_long, 0), step_decay), 0)
    grad_drive = jnp.sum(residues[None] * adjoint, axis=1)
    grad_filtered = jnp.stack([grad_query, grad_drive * value_part, grad_drive * key_part], axis=1)
    trailing = jnp.zeros((rim_width,) + grad_filtered.shape[1:], jnp.float32)
    ext_grad = jnp.concatenate([grad_filtered, trailing], axis=0)
    grad_stored = short_adjoint(ext_grad, taps, tok_count).astype(jnp.bfloat16)
    return mixed, grad_stored


def reference(token_ids, embed, w_in, taps, rates, residues, cotangent):
    embedded = embed[token_ids]
    flat_w = w_in.reshape(D, 3 * D)
    stored = lax.optimization_barrier(jnp.dot(embedded, flat_w, preferred_element_type=jnp.float32).astype(jnp.bfloat16))
    stored = stored.reshape(SEQ, 3, D)
    blocks = 16
    block_width = D // blocks

    def one_block(block_index):
        first = block_index * block_width
        return block_mix(
            lax.dynamic_slice_in_dim(stored, first, block_width, 2),
            lax.dynamic_slice_in_dim(cotangent, first, block_width, 1),
            lax.dynamic_slice_in_dim(taps, first, block_width, 2),
            lax.dynamic_slice_in_dim(rates, first, block_width, 1),
            lax.dynamic_slice_in_dim(residues, first, block_width, 1),
        )

    mixed_blocks, grad_blocks = lax.map(one_block, jnp.arange(blocks, dtype=jnp.int32))
    mixed = jnp.moveaxis(mixed_blocks, 0, 1).reshape(SEQ, D)
    grad_rows = jnp.moveaxis(grad_blocks, 0, 2).reshape(SEQ, 3 * D)
    input_grad = jnp.dot(grad_rows, flat_w.T, preferred_element_type=jnp.float32).astype(jnp.bfloat16)
    return (mixed, input_grad)
```

```python
import functools

import jax
import jax.numpy as jnp
from jax import lax
from jax.experimental import pallas as pl
from jax.experimental.pallas import tpu as pltpu
from jax.sharding import PartitionSpec as P

MESH = pl.DeviceIdType.MESH
VMEM = pl.BlockSpec(memory_space=pltpu.VMEM)
ANY = pl.BlockSpec(memory_space=pl.ANY)
LIMIT = 60 * 1024 * 1024
NX, NY, NC = 4, 4, 8
CHUNKS = 8
LAG = 2
VOCAB = 512
MODES = 16
TAPS = 7


def place():
    f = lax.axis_index("fsdp")
    c = lax.axis_index("ctx")
    return f // 16, (f // 4) % 4, (f // 2) % 2, f % 2, c


def flat(x, y, h, k):
    return (x % 4) * 16 + (y % 4) * 4 + h * 2 + k


def greet(devices, count):
    barrier = pltpu.get_barrier_semaphore()
    for device, wanted in devices:
        if wanted is None:
            pl.semaphore_signal(barrier, inc=1, device_id=device, device_id_type=MESH)
        else:

            @pl.when(wanted)
            def _():
                pl.semaphore_signal(barrier, inc=1, device_id=device, device_id_type=MESH)

    pl.semaphore_wait(barrier, count)


def table_kernel(
    embed_ref, w_ref, tok_ref, cot_ref,
    p_ref, tokall_ref, cotall_ref,
    emb, acc, pre_in, suf_in, pre_out, suf_out, toks, cots,
    local_sem, a_send, a_recv, k_send, pre_send, pre_recv, suf_send, suf_recv,
    cot_send, cot_recv, tok_send, tok_recv,
):
    x, y, h, k, c = place()
    x0, y0 = c // 2, (c % 2) * 2
    dx, dy = (x - x0 + 4) % 4, (y - y0 + 4) % 4
    on_row = dy < 2
    source = jnp.logical_and(on_row, dx == 0)
    near = jnp.where(jnp.logical_or(dy == 0, dy == 3), 0, 1)
    own = near * 4 + h * 2 + k

    local = pltpu.make_async_copy(embed_ref, emb.at[own], local_sem)

    @pl.when(source)
    def _():
        local.start()

    me = flat(x, y, h, k)
    plane = [
        flat(x, y, 1 - h, k), flat(x + 1, y, h, k), flat(x + 3, y, h, k),
        flat(x, y + 1, h, k), flat(x, y + 3, h, k), flat(x, y, h, 1 - k),
    ]
    greet(
        [((d, c), None) for d in plane] + [((me, (c + o) % NC), None) for o in range(1, NC)],
        len(plane) + NC - 1,
    )

    def block_copy(slot, target, sem):
        return pltpu.make_async_remote_copy(
            src_ref=emb.at[slot], dst_ref=emb.at[slot], send_sem=sem, recv_sem=a_recv.at[slot],
            device_id=(target, c), device_id_type=MESH,
        )

    def arrived(slot):
        block_copy(slot, plane[0], a_send.at[0]).wait_recv()

    sends = []

    def send(slot, target, sem, when):
        copy = block_copy(slot, target, sem)
        sends.append((copy, when))
        if when is None:
            copy.start()
        else:

            @pl.when(when)
            def _():
                copy.start()

    @pl.when(source)
    def _():
        local.wait()

    send(own, plane[0], a_send.at[0], source)
    off_row = jnp.logical_not(on_row)
    extra = []
    for b in range(2):
        hb = h if b == 0 else 1 - h
        slot = near * 4 + hb * 2 + k
        if b == 0:

            @pl.when(jnp.logical_not(source))
            def _():
                arrived(slot)

        else:
            arrived(slot)
        base = 1 + b * 5
        send(slot, plane[1], a_send.at[base], jnp.logical_and(on_row, jnp.logical_or(dx == 0, dx == 1) if b == 0 else dx == 0))
        send(slot, plane[2], a_send.at[base + 1], jnp.logical_and(on_row, dx == 0 if b == 0 else jnp.logical_or(dx == 0, dx == 3)))
        send(slot, plane[3], a_send.at[base + 2], jnp.logical_or(on_row, dy == 2))
        send(slot, plane[4], a_send.at[base + 3], jnp.logical_or(on_row, dy == 3))
        send(slot, plane[5], k_send.at[b], None)
        if b == 0:
            for o in range(1, NC):
                target = (me, (c + o) % NC)
                cot_copy = pltpu.make_async_remote_copy(
                    src_ref=cot_ref, dst_ref=cots.at[c], send_sem=cot_send.at[o - 1], recv_sem=cot_recv.at[o - 1],
                    device_id=target, device_id_type=MESH,
                )
                tok_copy = pltpu.make_async_remote_copy(
                    src_ref=tok_ref, dst_ref=toks.at[c], send_sem=tok_send.at[o - 1], recv_sem=tok_recv.at[o - 1],
                    device_id=target, device_id_type=MESH,
                )
                cot_copy.start()
                tok_copy.start()
                extra += [cot_copy, tok_copy]
    for b in range(2):
        hb = h if b == 0 else 1 - h
        slot = (1 - near) * 4 + hb * 2 + k
        arrived(slot)
        send(slot, plane[5], k_send.at[2 + b], None)
    for q in range(4):
        arrived(q * 2 + 1 - k)

    total = None
    for q in range(4):
        left = jnp.concatenate([emb[2 * q], emb[2 * q + 1]], axis=1)
        right = jnp.concatenate([w_ref[g, pl.ds(q * 256, 256), :] for g in range(3)], axis=1)
        part = jnp.dot(left, right, preferred_element_type=jnp.float32)
        total = part if total is None else total + part
    acc[...] = total.reshape(acc.shape)

    rows = acc.shape[1]

    @pl.when(c == 0)
    def _():
        pre_in[...] = jnp.zeros_like(pre_in)

    @pl.when(c == NC - 1)
    def _():
        suf_in[...] = jnp.zeros_like(suf_in)

    def chain(i, inbox, outbox, send_sem, recv_sem, to):
        return pltpu.make_async_remote_copy(
            src_ref=outbox.at[i], dst_ref=inbox.at[i], send_sem=send_sem.at[i], recv_sem=recv_sem.at[i],
            device_id=(me, to), device_id_type=MESH,
        )

    up = (c + 1) % NC
    down = (c + NC - 1) % NC

    def turn(s, _):
        i = s - LAG * c

        @pl.when(jnp.logical_and(i >= 0, i < CHUNKS))
        def _():
            @pl.when(c > 0)
            def _():
                chain(i, pre_in, pre_out, pre_send, pre_recv, up).wait_recv()

            @pl.when(c < NC - 1)
            def _():
                pre_out[i] = acc[i] + pre_in[i]
                chain(i, pre_in, pre_out, pre_send, pre_recv, up).start()

        e = s - LAG * (NC - 1 - c)

        @pl.when(jnp.logical_and(e >= 0, e < CHUNKS))
        def _():
            @pl.when(c < NC - 1)
            def _():
                chain(e, suf_in, suf_out, suf_send, suf_recv, down).wait_recv()

            @pl.when(c > 0)
            def _():
                suf_out[e] = acc[e] + suf_in[e]
                chain(e, suf_in, suf_out, suf_send, suf_recv, down).start()

        return 0

    lax.fori_loop(0, LAG * (NC - 1) + CHUNKS, turn, 0)

    def finish(i, _):
        both = acc[i] + pre_in[i] + suf_in[i]
        p_ref[pl.ds(pl.multiple_of(i * rows, rows), rows), :] = both.astype(jnp.bfloat16)

        @pl.when(c < NC - 1)
        def _():
            chain(i, pre_in, pre_out, pre_send, pre_recv, up).wait_send()

        @pl.when(c > 0)
        def _():
            chain(i, suf_in, suf_out, suf_send, suf_recv, down).wait_send()

        return 0

    lax.fori_loop(0, CHUNKS, finish, 0)

    cots[c] = cot_ref[...]
    toks[c] = tok_ref[...]
    for copy in extra:
        copy.wait()
    for i in range(NC):
        cotall_ref[i] = cots[i]
        tokall_ref[pl.ds(i, 1), :] = toks[i]
    for copy, when in sends:
        if when is None:
            copy.wait_send()
        else:

            @pl.when(when)
            def _():
                copy.wait_send()


def shifted_up(value, by, row):
    return jnp.where(row >= by, pltpu.roll(value, by, 0), 0.0)


def shifted_down(value, by, row):
    return jnp.where(row < 8 - by, pltpu.roll(value, 8 - by, 0), 0.0)


def scan_modes(drive_at, out_ref, rates_ref, res_ref, backward):
    row = lax.broadcasted_iota(jnp.int32, (8, 128), 0)
    shifted = shifted_down if backward else shifted_up
    length = 128

    def spread(ref, m):
        return jnp.broadcast_to(ref[m : m + 1, :], (8, 128))

    def at(j):
        j = length - 1 - j if backward else j
        return pl.ds(pl.multiple_of(j * 8, 8), 8)

    decay = [jnp.exp(-spread(rates_ref, m)) for m in range(MODES)]

    def ends(j, state):
        drive = drive_at(at(j))
        return tuple(decay[m] * state[m] + drive for m in range(MODES))

    zero = jnp.zeros((8, 128), jnp.float32)
    state = lax.fori_loop(0, length, ends, (zero,) * MODES, unroll=4)
    entering = []
    for m in range(MODES):
        rate = spread(rates_ref, m)
        whole = state[m]
        for by in (1, 2, 4):
            whole = whole + jnp.exp(-rate * float(length * by)) * shifted(whole, by, row)
        entering.append(shifted(whole, 1, row))
    weight = [spread(res_ref, m) for m in range(MODES)]

    def outs(j, state):
        where = at(j)
        drive = drive_at(where)
        state = tuple(decay[m] * state[m] + drive for m in range(MODES))
        terms = [weight[m] * state[m] for m in range(MODES)]
        while len(terms) > 1:
            terms = [a + b for a, b in zip(terms[::2], terms[1::2])]
        out_ref[where, :] = terms[0]
        return state

    lax.fori_loop(0, length, outs, tuple(entering), unroll=4)


def mix_kernel(
    p_ref, tok_ref, cot_ref, taps_ref, rates_ref, res_ref, w_ref,
    mixed_ref, part_ref,
    z, filt, cot, drive, glong, lo, gd, gz, lhs,
):
    c = lax.axis_index("ctx")
    halo = 8
    row = lax.broadcasted_iota(jnp.int32, (8, 128), 0)
    lane = lax.broadcasted_iota(jnp.int32, (8, VOCAB), 1)

    for s in range(NC):
        cot[pl.ds(s, 128, stride=8), :] = cot_ref[s].astype(jnp.float32)

    def pick(i, toks):
        rows = []
        for j in range(0, 16, 2):
            two = [jnp.where(toks[:, j + e : j + e + 1] == lane, 1.0, 0.0) for e in range(2)]
            rows.append(jnp.concatenate(two, axis=0).astype(jnp.bfloat16))
        hot = jnp.concatenate(rows, axis=0)
        found = jnp.dot(hot, p_ref[...], preferred_element_type=jnp.float32)
        start = pl.ds(pl.multiple_of((halo + i * 16) * 8, 128 // 2), 128)
        for g in range(3):
            z[g, start, :] = found[:, g * 128 : (g + 1) * 128]
        return pltpu.roll(toks, 112, 1)

    lax.fori_loop(0, 8, pick, tok_ref[...])
    for g in range(3):
        for d in range(1, TAPS):
            z[g, pl.ds((halo - d) * 8, 8), :] = shifted_up(z[g, pl.ds((halo + 128 - d) * 8, 8), :], 1, row)

    def filter_rows(i, _):
        base = i * 64
        for g in range(3):
            value = None
            for d in range(TAPS):
                term = taps_ref[g, d : d + 1, :] * z[g, pl.ds(pl.multiple_of(base + (halo - d) * 8, 8), 64), :]
                value = term if value is None else value + term
            filt[g, pl.ds(pl.multiple_of(base, 64), 64), :] = value
        here = pl.ds(pl.multiple_of(base, 64), 64)
        drive[here, :] = filt[1, here, :] * filt[2, here, :]
        glong[here, :] = cot[here, :] * filt[0, here, :]
        return 0

    lax.fori_loop(0, 16, filter_rows, 0)
    scan_modes(lambda at: drive[at, :], lo, rates_ref, res_ref, False)
    scan_modes(lambda at: glong[at, :], gd, rates_ref, res_ref, True)

    def grads(i, _):
        here = pl.ds(pl.multiple_of(i * 64, 64), 64)
        long_out, grad_drive = lo[here, :], gd[here, :]
        z[0, here, :] = cot[here, :] * long_out
        z[1, here, :] = grad_drive * filt[2, here, :]
        z[2, here, :] = grad_drive * filt[1, here, :]
        lo[here, :] = filt[0, here, :] * long_out
        return 0

    lax.fori_loop(0, 16, grads, 0)
    mixed_ref[...] = lo[pl.ds(c, 128, stride=8), :].astype(jnp.bfloat16)
    for g in range(3):
        for d in range(TAPS - 1):
            z[g, pl.ds((128 + d) * 8, 8), :] = shifted_down(z[g, pl.ds(d * 8, 8), :], 1, row)

    def adjoint_rows(i, _):
        base = i * 64
        for g in range(3):
            value = None
            for d in range(TAPS):
                term = taps_ref[g, d : d + 1, :] * z[g, pl.ds(pl.multiple_of(base + d * 8, 8), 64), :]
                value = term if value is None else value + term
            gz[g, pl.ds(pl.multiple_of(base, 64), 64), :] = value
        return 0

    lax.fori_loop(0, 16, adjoint_rows, 0)
    for s in range(NC):
        for g in range(3):
            lhs[pl.ds(s * 128, 128), pl.ds(g * 128, 128)] = gz[g, pl.ds(s, 128, stride=8), :].astype(jnp.bfloat16)
    for n in range(4):
        yb, hh = n // 2, n % 2
        right = jnp.concatenate([w_ref[g, pl.ds(n * 256, 256), :] for g in range(3)], axis=1)
        out = lax.dot_general(
            lhs[...], right, (((1,), (1,)), ((), ())), preferred_element_type=jnp.float32
        ).astype(jnp.bfloat16)
        for s in range(NC):
            xo, yo = s // 2, yb * 2 + s % 2
            a, b = (xo, yo) if hh == 0 else (yo, xo)
            for kk in range(2):
                part_ref[kk, hh, a, b] = out[s * 128 : (s + 1) * 128, kk * 128 : (kk + 1) * 128]


def sum_kernel(
    part_ref, out_ref,
    core_in, first_out, first_in, second_out, second_in, last_out, last_in,
    core_send, core_recv, first_send, first_recv, second_send, second_recv, last_send, last_recv,
):
    x, y, h, k, c = place()
    x0, y0 = c // 2, (c % 2) * 2
    partner = (flat(x, y, h, 1 - k), c)
    xs = [(flat(x + o, y, h, k), c) for o in range(1, 4)]
    ys = [(flat(x, y + o, h, k), c) for o in range(1, 4)]
    owner = [(flat(x0, y0 + y // 2, e, k), 2 * x + y % 2) for e in range(2)]
    from_c = 2 * x + y // 2
    givers = [(flat(c // 2, (y % 2) * 2 + c % 2, e, k), from_c) for e in range(2)]
    loop = jnp.logical_and(jnp.logical_and(x == x0, y == y0 + y // 2), c == 2 * x + y % 2)
    foreign = [jnp.logical_not(jnp.logical_and(loop, h == e)) for e in range(2)]
    greet(
        [(d, None) for d in [partner] + xs + ys] + [(givers[e], foreign[e]) for e in range(2)],
        9 - loop.astype(jnp.int32),
    )

    def core_copy(e, a):
        return pltpu.make_async_remote_copy(
            src_ref=part_ref.at[1 - k, e, a], dst_ref=core_in.at[e, a],
            send_sem=core_send.at[e, a], recv_sem=core_recv.at[e, a], device_id=partner, device_id_type=MESH,
        )

    spots = [x, y]
    lines = [xs, ys]

    def first_copy(e, o):
        return pltpu.make_async_remote_copy(
            src_ref=first_out.at[e, o], dst_ref=first_in.at[e, o - 1],
            send_sem=first_send.at[e, o - 1], recv_sem=first_recv.at[e, o - 1],
            device_id=lines[e][o - 1], device_id_type=MESH,
        )

    def second_copy(e, o):
        return pltpu.make_async_remote_copy(
            src_ref=second_out.at[e, o], dst_ref=second_in.at[e, o - 1],
            send_sem=second_send.at[e, o - 1], recv_sem=second_recv.at[e, o - 1],
            device_id=lines[1 - e][o - 1], device_id_type=MESH,
        )

    def last_copy(e):
        return pltpu.make_async_remote_copy(
            src_ref=last_out.at[e], dst_ref=last_in.at[h],
            send_sem=last_send.at[e], recv_sem=last_recv.at[h], device_id=owner[e], device_id_type=MESH,
        )

    def last_wait(e):
        pltpu.make_async_remote_copy(
            src_ref=last_out.at[e], dst_ref=last_in.at[e],
            send_sem=last_send.at[e], recv_sem=last_recv.at[e], device_id=partner, device_id_type=MESH,
        ).wait_recv()

    order = [2, 1, 3, 0]
    for o in order:
        for e in range(2):
            core_copy(e, (spots[e] + o) % 4).start()
    for o in order:
        for e in range(2):
            a = (spots[e] + o) % 4
            core_copy(e, a).wait_recv()
            both = part_ref[k, e, a].astype(jnp.float32) + core_in[e, a].astype(jnp.float32)
            first_out[e, o] = both.astype(jnp.bfloat16)
            if o:
                first_copy(e, o).start()
    for e in range(2):
        for o in range(1, 4):
            first_copy(e, o).wait_recv()
    for o in order:
        for e in range(2):
            b = (spots[1 - e] + o) % 4
            both = first_out[e, 0, b].astype(jnp.float32)
            for i in range(3):
                both = both + first_in[e, i, b].astype(jnp.float32)
            second_out[e, o] = both.astype(jnp.bfloat16)
            if o:
                second_copy(e, o).start()
    for e in range(2):
        both = second_out[e, 0].astype(jnp.float32)
        for o in range(1, 4):
            second_copy(e, o).wait_recv()
            both = both + second_in[e, o - 1].astype(jnp.float32)
        last_out[e] = both.astype(jnp.bfloat16)

        @pl.when(foreign[e])
        def _():
            last_copy(e).start()

        @pl.when(jnp.logical_not(foreign[e]))
        def _():
            last_in[e] = last_out[e]

    for e in range(2):

        @pl.when(foreign[e])
        def _():
            last_wait(e)

    out_ref[...] = (last_in[0].astype(jnp.float32) + last_in[1].astype(jnp.float32)).astype(jnp.bfloat16)
    for e in range(2):
        for a in range(4):
            core_copy(e, (spots[e] + a) % 4).wait_send()
        for o in range(1, 4):
            first_copy(e, o).wait_send()
            second_copy(e, o).wait_send()

        @pl.when(foreign[e])
        def _():
            last_copy(e).wait_send()


def on_device(token_ids, embed, w_in, taps, rates, residues, cotangent):
    bf16, f32, i32 = jnp.bfloat16, jnp.float32, jnp.int32
    dma = pltpu.SemaphoreType.DMA
    w = w_in.transpose(1, 0, 2)
    taps = taps.transpose(1, 0, 2)
    rows = VOCAB // CHUNKS
    p, toks, cots = pl.pallas_call(
        table_kernel,
        out_shape=(
            jax.ShapeDtypeStruct((VOCAB, 384), bf16),
            jax.ShapeDtypeStruct((NC, 128), i32),
            jax.ShapeDtypeStruct((NC, 128, 128), bf16),
        ),
        in_specs=[ANY, VMEM, VMEM, VMEM],
        out_specs=(VMEM, VMEM, VMEM),
        scratch_shapes=[
            pltpu.VMEM((8, VOCAB, 128), bf16),
            pltpu.VMEM((CHUNKS, rows, 384), f32),
            pltpu.VMEM((CHUNKS, rows, 384), f32),
            pltpu.VMEM((CHUNKS, rows, 384), f32),
            pltpu.VMEM((CHUNKS, rows, 384), f32),
            pltpu.VMEM((CHUNKS, rows, 384), f32),
            pltpu.VMEM((NC, 1, 128), i32),
            pltpu.VMEM((NC, 128, 128), bf16),
            dma, dma((11,)), dma((8,)), dma((4,)),
            dma((CHUNKS,)), dma((CHUNKS,)), dma((CHUNKS,)), dma((CHUNKS,)),
            dma((NC - 1,)), dma((NC - 1,)), dma((NC - 1,)), dma((NC - 1,)),
        ],
        compiler_params=pltpu.CompilerParams(collective_id=0, has_side_effects=True, vmem_limit_bytes=LIMIT),
        name="table",
    )(embed, w, token_ids.reshape(1, 128), cotangent)
    wide = pltpu.VMEM((1024, 128), f32)
    mixed, part = pl.pallas_call(
        mix_kernel,
        out_shape=(
            jax.ShapeDtypeStruct((128, 128), bf16),
            jax.ShapeDtypeStruct((2, 2, 4, 4, 128, 128), bf16),
        ),
        in_specs=[VMEM] * 7,
        out_specs=(VMEM, VMEM),
        scratch_shapes=[
            pltpu.VMEM((3, 136 * 8, 128), f32), pltpu.VMEM((3, 1024, 128), f32),
            wide, wide, wide, wide, wide,
            pltpu.VMEM((3, 1024, 128), f32), pltpu.VMEM((1024, 384), bf16),
        ],
        compiler_params=pltpu.CompilerParams(vmem_limit_bytes=LIMIT),
        name="mix",
    )(p, toks, cots, taps, rates, residues, w)
    own = pl.pallas_call(
        sum_kernel,
        out_shape=jax.ShapeDtypeStruct((128, 128), bf16),
        in_specs=[VMEM],
        out_specs=VMEM,
        scratch_shapes=[
            pltpu.VMEM((2, 4, 4, 128, 128), bf16), pltpu.VMEM((2, 4, 4, 128, 128), bf16),
            pltpu.VMEM((2, 3, 4, 128, 128), bf16), pltpu.VMEM((2, 4, 128, 128), bf16),
            pltpu.VMEM((2, 3, 128, 128), bf16), pltpu.VMEM((2, 128, 128), bf16), pltpu.VMEM((2, 128, 128), bf16),
            dma((2, 4)), dma((2, 4)), dma((2, 3)), dma((2, 3)), dma((2, 3)), dma((2, 3)), dma((2,)), dma((2,)),
        ],
        compiler_params=pltpu.CompilerParams(collective_id=1, has_side_effects=True, vmem_limit_bytes=LIMIT),
        name="sums",
    )(part)
    return mixed, own


def solution(mesh):
    in_specs = (
        P("ctx"),
        P(None, "fsdp"),
        P("ctx", None, "fsdp"),
        P(None, None, "fsdp"),
        P(None, "fsdp"),
        P(None, "fsdp"),
        P("ctx", "fsdp"),
    )
    out_specs = (P("ctx", "fsdp"), P("ctx", "fsdp"))
    return jax.shard_map(on_device, mesh=mesh, in_specs=in_specs, out_specs=out_specs, check_vma=False)
```

```python
import functools

import jax
import jax.numpy as jnp
from jax import lax
from jax.experimental import pallas as pl
from jax.experimental.pallas import tpu as pltpu
from jax.sharding import PartitionSpec as P

MESH = pl.DeviceIdType.MESH
VMEM = pl.BlockSpec(memory_space=pltpu.VMEM)
ANY = pl.BlockSpec(memory_space=pl.ANY)
LIMIT = 60 * 1024 * 1024
NC = 8
VOCAB = 512
MODES = 16
TAPS = 7


def place():
    f = lax.axis_index("fsdp")
    c = lax.axis_index("ctx")
    return f // 16, (f // 4) % 4, (f // 2) % 2, f % 2, c


def flat(x, y, h, k):
    return (x % 4) * 16 + (y % 4) * 4 + h * 2 + k


def greet(devices, count):
    barrier = pltpu.get_barrier_semaphore()
    for device, wanted in devices:
        if wanted is None:
            pl.semaphore_signal(barrier, inc=1, device_id=device, device_id_type=MESH)
        else:

            @pl.when(wanted)
            def _():
                pl.semaphore_signal(barrier, inc=1, device_id=device, device_id_type=MESH)

    pl.semaphore_wait(barrier, count)


def table_kernel(
    embed_ref, w_ref, tok_ref, cot_ref,
    p_ref, tokall_ref, cotall_ref,
    emb, acc, part_out, part_in, pair_out, pair_in, table, toks, cots,
    local_sem, half_send, x_send, y_send, k_send, a_recv,
    part_send, part_recv, pair_send, pair_recv, done_send, done_recv,
    cot_send, cot_recv, tok_send, tok_recv,
):
    f32, bf16 = jnp.float32, jnp.bfloat16
    x, y, h, k, c = place()
    me = flat(x, y, h, k)
    mine = 2 * x + y // 2
    yb = y % 2
    edge = jnp.where(mine < NC // 2, NC - 1, 0)
    x0, y0 = c // 2, (c % 2) * 2
    dy = (y - y0 + 4) % 4
    on_row = dy < 2
    source = mine == c
    near = jnp.where(dy == 1, 1, 0)
    own = yb * 4 + h * 2 + k

    xs = [flat(x + o, y, h, k) for o in range(1, 4)]
    ys = [flat(x, y + o, h, k) for o in range(1, 4)]
    partner = flat(x, y, h, 1 - k)
    other = flat(x, y, 1 - h, k)
    gives = c == edge
    greet(
        [((d, c), None) for d in xs + ys + [partner]]
        + [((me, (c + o) % NC), None) for o in range(1, NC)]
        + [((other, edge), source)],
        7 + NC - 1 + gives.astype(jnp.int32),
    )

    local = pltpu.make_async_copy(embed_ref, emb.at[own], local_sem)

    def block_copy(slot, target, sem, src=None, to=c):
        return pltpu.make_async_remote_copy(
            src_ref=emb.at[slot] if src is None else src, dst_ref=emb.at[slot], send_sem=sem,
            recv_sem=a_recv.at[slot], device_id=(target, to), device_id_type=MESH,
        )

    def arrived(slot):
        block_copy(slot, partner, k_send.at[0]).wait_recv()

    sends = []

    def send(copy, when):
        sends.append((copy, when))
        if when is None:
            copy.start()
        else:

            @pl.when(when)
            def _():
                copy.start()

    send(block_copy(own, other, half_send, embed_ref, mine), gives)

    @pl.when(source)
    def _():
        local.start()

    for o in (2, 1, 3):
        send(block_copy(own, xs[o - 1], x_send.at[0, o - 1], embed_ref), source)

    @pl.when(source)
    def _():
        local.wait()

    def slot_of(row, b):
        return row * 4 + (h if b == 0 else 1 - h) * 2 + k

    extra = []
    for b in range(2):
        slot = slot_of(near, b)
        if b == 0:

            @pl.when(jnp.logical_not(source))
            def _():
                arrived(slot)

        else:
            arrived(slot)
            for o in (2, 1, 3):
                send(block_copy(slot, xs[o - 1], x_send.at[1, o - 1]), source)
        for o in (2, 1, 3):
            send(block_copy(slot, ys[o - 1], y_send.at[b, o - 1]), on_row)
        send(block_copy(slot, partner, k_send.at[b]), None)
        if b == 0:
            for o in range(1, NC):
                target = (me, (c + o) % NC)
                for src, dst, ss, rs in (
                    (cot_ref, cots, cot_send, cot_recv), (tok_ref, toks, tok_send, tok_recv)
                ):
                    copy = pltpu.make_async_remote_copy(
                        src_ref=src, dst_ref=dst.at[c], send_sem=ss.at[o - 1], recv_sem=rs.at[o - 1],
                        device_id=target, device_id_type=MESH,
                    )
                    copy.start()
                    extra.append(copy)
            far = slot_of(1 - near, 0)
            arrived(far)
            send(block_copy(far, partner, k_send.at[2]), None)

    def lane(e, b):
        return e * 4 + (h if b == 0 else 1 - h) * 2

    def product(rows, b):
        total = None
        for e in range(2):
            j = lane(e, b)
            left = jnp.concatenate([emb[j, rows, :], emb[j + 1, rows, :]], axis=1)
            at = pl.ds(pl.multiple_of(j * 128, 256), 256)
            right = jnp.concatenate([w_ref[g, at, :] for g in range(3)], axis=1)
            part = jnp.dot(left, right, preferred_element_type=f32)
            total = part if total is None else total + part
        return total

    for e in range(2):
        arrived(lane(e, 0) + 1 - k)
    for q in range(4):
        rows = pl.ds(q * 128, 128)
        acc[q] = product(rows, 0)
    far = slot_of(1 - near, 1)
    arrived(far)
    send(block_copy(far, partner, k_send.at[3]), None)
    for e in range(2):
        arrived(lane(e, 1) + 1 - k)

    q = c % 4
    base = c - q

    def part_copy(o, s):
        return pltpu.make_async_remote_copy(
            src_ref=part_out.at[o - 1, s], dst_ref=part_in.at[o - 1, s], send_sem=part_send.at[o - 1, s],
            recv_sem=part_recv.at[o - 1, s], device_id=(me, base + (q + o) % 4), device_id_type=MESH,
        )

    def pair_copy(s):
        return pltpu.make_async_remote_copy(
            src_ref=pair_out.at[s], dst_ref=pair_in.at[s], send_sem=pair_send.at[s], recv_sem=pair_recv.at[s],
            device_id=(me, (c + 4) % NC), device_id_type=MESH,
        )

    def done_copy(o, s):
        return pltpu.make_async_remote_copy(
            src_ref=table.at[q, s], dst_ref=table.at[q, s], send_sem=done_send.at[o - 1, s],
            recv_sem=done_recv.at[o - 1, s], device_id=(me, base + (q + o) % 4), device_id_type=MESH,
        )

    for s in range(2):
        for o in (3, 1, 2, 0):
            group = (q + o) % 4
            rows = pl.ds(pl.multiple_of(group * 128 + s * 64, 64), 64)
            half = pl.ds(s * 64, 64)
            total = acc[group, half, :] + product(rows, 1)
            if o:
                part_out[o - 1, s] = total.astype(bf16)
                part_copy(o, s).start()
            else:
                acc[group, half, :] = total
    for s in range(2):
        half = pl.ds(s * 64, 64)
        total = acc[q, half, :]
        for o in range(1, 4):
            part_copy(o, s).wait_recv()
            total = total + part_in[o - 1, s].astype(f32)
        acc[q, half, :] = total
        pair_out[s] = total.astype(bf16)
        pair_copy(s).start()
    for s in range(2):
        half = pl.ds(s * 64, 64)
        pair_copy(s).wait_recv()
        table[q, s] = (acc[q, half, :] + pair_in[s].astype(f32)).astype(bf16)
        for o in (3, 1, 2):
            done_copy(o, s).start()

    cots[c] = cot_ref[...]
    toks[c] = tok_ref[...]
    for copy in extra:
        copy.wait()
    for i in range(NC):
        cotall_ref[i] = cots[i]
        tokall_ref[pl.ds(i, 1), :] = toks[i]
    for copy, when in sends:
        if when is None:
            copy.wait_send()
        else:

            @pl.when(when)
            def _():
                copy.wait_send()

    for s in range(2):
        pair_copy(s).wait_send()
        for o in range(1, 4):
            part_copy(o, s).wait_send()
            done_copy(o, s).wait()
    for i in range(4):
        for s in range(2):
            p_ref[pl.ds(i * 128 + s * 64, 64), :] = table[i, s]


def shifted_up(value, by, row):
    return jnp.where(row >= by, pltpu.roll(value, by, 0), 0.0)


def shifted_down(value, by, row):
    return jnp.where(row < 8 - by, pltpu.roll(value, 8 - by, 0), 0.0)


def scan_modes(drive_at, out_ref, rates_ref, res_ref, backward):
    row = lax.broadcasted_iota(jnp.int32, (8, 128), 0)
    shifted = shifted_down if backward else shifted_up
    length = 128

    def spread(ref, m):
        return jnp.broadcast_to(ref[m : m + 1, :], (8, 128))

    def at(j):
        j = length - 1 - j if backward else j
        return pl.ds(pl.multiple_of(j * 8, 8), 8)

    decay = [jnp.exp(-spread(rates_ref, m)) for m in range(MODES)]

    def ends(j, state):
        drive = drive_at(at(j))
        return tuple(decay[m] * state[m] + drive for m in range(MODES))

    zero = jnp.zeros((8, 128), jnp.float32)
    state = lax.fori_loop(0, length, ends, (zero,) * MODES, unroll=4)
    entering = []
    for m in range(MODES):
        rate = spread(rates_ref, m)
        whole = state[m]
        for by in (1, 2, 4):
            whole = whole + jnp.exp(-rate * float(length * by)) * shifted(whole, by, row)
        entering.append(shifted(whole, 1, row))
    weight = [spread(res_ref, m) for m in range(MODES)]

    def outs(j, state):
        where = at(j)
        drive = drive_at(where)
        state = tuple(decay[m] * state[m] + drive for m in range(MODES))
        terms = [weight[m] * state[m] for m in range(MODES)]
        while len(terms) > 1:
            terms = [a + b for a, b in zip(terms[::2], terms[1::2])]
        out_ref[where, :] = terms[0]
        return state

    lax.fori_loop(0, length, outs, tuple(entering), unroll=4)


def mix_kernel(
    p_ref, tok_ref, cot_ref, taps_ref, rates_ref, res_ref,
    mixed_ref, lhs_ref,
    z, filt, cot, drive, glong, lo, gd, gz,
):
    c = lax.axis_index("ctx")
    halo = 8
    row = lax.broadcasted_iota(jnp.int32, (8, 128), 0)
    lane = lax.broadcasted_iota(jnp.int32, (8, VOCAB), 1)

    for s in range(NC):
        cot[pl.ds(s, 128, stride=8), :] = cot_ref[s].astype(jnp.float32)

    def pick(i, toks):
        rows = []
        for j in range(0, 16, 2):
            two = [jnp.where(toks[:, j + e : j + e + 1] == lane, 1.0, 0.0) for e in range(2)]
            rows.append(jnp.concatenate(two, axis=0).astype(jnp.bfloat16))
        hot = jnp.concatenate(rows, axis=0)
        found = jnp.dot(hot, p_ref[...], preferred_element_type=jnp.float32)
        start = pl.ds(pl.multiple_of((halo + i * 16) * 8, 128 // 2), 128)
        for g in range(3):
            z[g, start, :] = found[:, g * 128 : (g + 1) * 128]
        return pltpu.roll(toks, 112, 1)

    lax.fori_loop(0, 8, pick, tok_ref[...])
    for g in range(3):
        for d in range(1, TAPS):
            z[g, pl.ds((halo - d) * 8, 8), :] = shifted_up(z[g, pl.ds((halo + 128 - d) * 8, 8), :], 1, row)

    def filter_rows(i, _):
        base = i * 64
        for g in range(3):
            value = None
            for d in range(TAPS):
                term = taps_ref[g, d : d + 1, :] * z[g, pl.ds(pl.multiple_of(base + (halo - d) * 8, 8), 64), :]
                value = term if value is None else value + term
            filt[g, pl.ds(pl.multiple_of(base, 64), 64), :] = value
        here = pl.ds(pl.multiple_of(base, 64), 64)
        drive[here, :] = filt[1, here, :] * filt[2, here, :]
        glong[here, :] = cot[here, :] * filt[0, here, :]
        return 0

    lax.fori_loop(0, 16, filter_rows, 0)
    scan_modes(lambda at: drive[at, :], lo, rates_ref, res_ref, False)
    scan_modes(lambda at: glong[at, :], gd, rates_ref, res_ref, True)

    def grads(i, _):
        here = pl.ds(pl.multiple_of(i * 64, 64), 64)
        long_out, grad_drive = lo[here, :], gd[here, :]
        z[0, here, :] = cot[here, :] * long_out
        z[1, here, :] = grad_drive * filt[2, here, :]
        z[2, here, :] = grad_drive * filt[1, here, :]
        lo[here, :] = filt[0, here, :] * long_out
        return 0

    lax.fori_loop(0, 16, grads, 0)
    mixed_ref[...] = lo[pl.ds(c, 128, stride=8), :].astype(jnp.bfloat16)
    for g in range(3):
        for d in range(TAPS - 1):
            z[g, pl.ds((128 + d) * 8, 8), :] = shifted_down(z[g, pl.ds(d * 8, 8), :], 1, row)

    def adjoint_rows(i, _):
        base = i * 64
        for g in range(3):
            value = None
            for d in range(TAPS):
                term = taps_ref[g, d : d + 1, :] * z[g, pl.ds(pl.multiple_of(base + d * 8, 8), 64), :]
                value = term if value is None else value + term
            gz[g, pl.ds(pl.multiple_of(base, 64), 64), :] = value
        return 0

    lax.fori_loop(0, 16, adjoint_rows, 0)
    for s in range(NC):
        start = (c + s) % NC
        for g in range(3):
            lhs_ref[pl.ds(s * 128, 128), pl.ds(g * 128, 128)] = gz[g, pl.ds(start, 128, stride=8), :].astype(jnp.bfloat16)


SPOT = {0: (0, 0), 1: (1, 0), 2: (0, 1), 3: (1, 1), 4: (2, 1), 5: (3, 1), 6: (2, 0), 7: (3, 0)}


def sum_kernel(
    lhs_ref, w_ref, out_ref,
    own, core_out, core_in, first_out, first_in, second_own, second_out, second_in, last_out, last_in,
    core_send, core_recv, first_send, first_recv, second_send, second_recv, last_send, last_recv,
):
    f32, bf16 = jnp.float32, jnp.bfloat16
    x, y, h, k, c = place()
    x0, y0 = c // 2, (c % 2) * 2
    dx, dy = (x - x0 + 4) % 4, (y - y0 + 4) % 4
    partner = (flat(x, y, h, 1 - k), c)
    xs = [(flat(x + o, y, h, k), c) for o in range(1, 4)]
    ys = [(flat(x, y + o, h, k), c) for o in range(1, 4)]
    yb = jnp.where(jnp.logical_or(dy == 1, dy == 2), 1, 0)
    far = jnp.where(dy >= 2, 1, 0)
    step = jnp.where(dx < 2, dx + 2 * far, dx + 4 - 2 * far)
    owner = [(flat(x0, y0 + yb, e, k), (c + step) % NC) for e in range(2)]
    from_c = 2 * x + y // 2
    back = (c - from_c + NC) % NC
    back_x = jnp.where(back < 4, back % 2, 2 + back % 2)
    back_far = jnp.where(back < 4, back // 2, 3 - back // 2)
    back_y = jnp.where(y % 2 == 0, 3 * back_far, 1 + back_far)
    givers = [(flat(x + back_x, (y // 2) * 2 + back_y, e, k), from_c) for e in range(2)]
    loop = jnp.logical_and(dx == 0, dy < 2)
    foreign = [jnp.logical_not(jnp.logical_and(loop, h == e)) for e in range(2)]
    greet(
        [(d, None) for d in [partner] + xs + ys] + [(givers[e], foreign[e]) for e in range(2)],
        9 - loop.astype(jnp.int32),
    )

    def core_copy(e, a):
        return pltpu.make_async_remote_copy(
            src_ref=core_out.at[e, a], dst_ref=core_in.at[e, a],
            send_sem=core_send.at[e, a], recv_sem=core_recv.at[e, a], device_id=partner, device_id_type=MESH,
        )

    spots = [dx, dy]
    lines = [xs, ys]

    def first_copy(e, o):
        return pltpu.make_async_remote_copy(
            src_ref=first_out.at[e, o - 1], dst_ref=first_in.at[e, o - 1],
            send_sem=first_send.at[e, o - 1], recv_sem=first_recv.at[e, o - 1],
            device_id=lines[e][o - 1], device_id_type=MESH,
        )

    def second_copy(e, o):
        return pltpu.make_async_remote_copy(
            src_ref=second_out.at[e, o - 1], dst_ref=second_in.at[e, o - 1],
            send_sem=second_send.at[e, o - 1], recv_sem=second_recv.at[e, o - 1],
            device_id=lines[1 - e][o - 1], device_id_type=MESH,
        )

    def last_copy(e):
        return pltpu.make_async_remote_copy(
            src_ref=last_out.at[e], dst_ref=last_in.at[h],
            send_sem=last_send.at[e], recv_sem=last_recv.at[h], device_id=owner[e], device_id_type=MESH,
        )

    def last_wait(e):
        pltpu.make_async_remote_copy(
            src_ref=last_out.at[e], dst_ref=last_in.at[e],
            send_sem=last_send.at[e], recv_sem=last_recv.at[e], device_id=partner, device_id_type=MESH,
        ).wait_recv()

    def tile(e, kk, store):
        starts = [pl.multiple_of(r * 512 + e * 256 + kk * 128, 128) for r in range(2)]
        right = jnp.concatenate(
            [jnp.concatenate([w_ref[g, pl.ds(at, 128), :] for g in range(3)], axis=1) for at in starts], axis=0
        )
        out = lax.dot_general(lhs_ref[...], right, (((1,), (1,)), ((), ())), preferred_element_type=f32)
        for s in range(NC):
            sx, sfar = SPOT[s]
            for r in range(2):
                sy = 3 * sfar if r == 0 else 1 + sfar
                a, b = (sx, sy) if e == 0 else (sy, sx)
                store(e, a, b, out[s * 128 : (s + 1) * 128, r * 128 : (r + 1) * 128])

    def to_core(e, a, b, value):
        core_out[e, a, b] = value.astype(bf16)

    def to_own(e, a, b, value):
        own[e, a, b] = value

    for e in range(2):
        tile(e, 1 - k, to_core)
        for a in range(4):
            core_copy(e, a).start()
    for e in range(2):
        tile(e, k, to_own)
    order = [2, 1, 3, 0]
    for o in order:
        for e in range(2):
            a = (spots[e] + o) % 4
            core_copy(e, a).wait_recv()
            both = own[e, a] + core_in[e, a].astype(f32)
            if o:
                first_out[e, o - 1] = both.astype(bf16)
                first_copy(e, o).start()
            else:
                own[e, a] = both
    for e in range(2):
        for o in range(1, 4):
            first_copy(e, o).wait_recv()
    for o in order:
        for e in range(2):
            b = (spots[1 - e] + o) % 4
            both = own[e, spots[e], b]
            for i in range(3):
                both = both + first_in[e, i, b].astype(f32)
            if o:
                second_out[e, o - 1] = both.astype(bf16)
                second_copy(e, o).start()
            else:
                second_own[e] = both
    for e in range(2):
        both = second_own[e]
        for o in range(1, 4):
            second_copy(e, o).wait_recv()
            both = both + second_in[e, o - 1].astype(f32)
        last_out[e] = both.astype(bf16)

        @pl.when(foreign[e])
        def _():
            last_copy(e).start()

        @pl.when(jnp.logical_not(foreign[e]))
        def _():
            last_in[e] = last_out[e]

    for e in range(2):

        @pl.when(foreign[e])
        def _():
            last_wait(e)

    out_ref[...] = (last_in[0].astype(f32) + last_in[1].astype(f32)).astype(bf16)
    for e in range(2):
        for a in range(4):
            core_copy(e, a).wait_send()
        for o in range(1, 4):
            first_copy(e, o).wait_send()
            second_copy(e, o).wait_send()

        @pl.when(foreign[e])
        def _():
            last_copy(e).wait_send()


def on_device(token_ids, embed, w_in, taps, rates, residues, cotangent):
    bf16, f32, i32 = jnp.bfloat16, jnp.float32, jnp.int32
    dma = pltpu.SemaphoreType.DMA
    w = w_in.transpose(1, 0, 2)
    taps = taps.transpose(1, 0, 2)
    p, toks, cots = pl.pallas_call(
        table_kernel,
        out_shape=(
            jax.ShapeDtypeStruct((VOCAB, 384), bf16),
            jax.ShapeDtypeStruct((NC, 128), i32),
            jax.ShapeDtypeStruct((NC, 128, 128), bf16),
        ),
        in_specs=[ANY, VMEM, VMEM, VMEM],
        out_specs=(VMEM, VMEM, VMEM),
        scratch_shapes=[
            pltpu.VMEM((8, VOCAB, 128), bf16),
            pltpu.VMEM((4, 128, 384), f32),
            pltpu.VMEM((3, 2, 64, 384), bf16), pltpu.VMEM((3, 2, 64, 384), bf16),
            pltpu.VMEM((2, 64, 384), bf16), pltpu.VMEM((2, 64, 384), bf16),
            pltpu.VMEM((4, 2, 64, 384), bf16),
            pltpu.VMEM((NC, 1, 128), i32),
            pltpu.VMEM((NC, 128, 128), bf16),
            dma, dma, dma((2, 3)), dma((2, 3)), dma((4,)), dma((8,)),
            dma((3, 2)), dma((3, 2)), dma((2,)), dma((2,)), dma((3, 2)), dma((3, 2)),
            dma((NC - 1,)), dma((NC - 1,)), dma((NC - 1,)), dma((NC - 1,)),
        ],
        compiler_params=pltpu.CompilerParams(collective_id=0, has_side_effects=True, vmem_limit_bytes=LIMIT),
        name="table",
    )(embed, w, token_ids.reshape(1, 128), cotangent)
    wide = pltpu.VMEM((1024, 128), f32)
    mixed, lhs = pl.pallas_call(
        mix_kernel,
        out_shape=(
            jax.ShapeDtypeStruct((128, 128), bf16),
            jax.ShapeDtypeStruct((1024, 384), bf16),
        ),
        in_specs=[VMEM] * 6,
        out_specs=(VMEM, VMEM),
        scratch_shapes=[
            pltpu.VMEM((3, 136 * 8, 128), f32), pltpu.VMEM((3, 1024, 128), f32),
            wide, wide, wide, wide, wide,
            pltpu.VMEM((3, 1024, 128), f32),
        ],
        compiler_params=pltpu.CompilerParams(vmem_limit_bytes=LIMIT),
        name="mix",
    )(p, toks, cots, taps, rates, residues)
    own = pl.pallas_call(
        sum_kernel,
        out_shape=jax.ShapeDtypeStruct((128, 128), bf16),
        in_specs=[VMEM, VMEM],
        out_specs=VMEM,
        scratch_shapes=[
            pltpu.VMEM((2, 4, 4, 128, 128), f32),
            pltpu.VMEM((2, 4, 4, 128, 128), bf16), pltpu.VMEM((2, 4, 4, 128, 128), bf16),
            pltpu.VMEM((2, 3, 4, 128, 128), bf16), pltpu.VMEM((2, 3, 4, 128, 128), bf16),
            pltpu.VMEM((2, 128, 128), f32),
            pltpu.VMEM((2, 3, 128, 128), bf16), pltpu.VMEM((2, 3, 128, 128), bf16),
            pltpu.VMEM((2, 128, 128), bf16), pltpu.VMEM((2, 128, 128), bf16),
            dma((2, 4)), dma((2, 4)), dma((2, 3)), dma((2, 3)), dma((2, 3)), dma((2, 3)), dma((2,)), dma((2,)),
        ],
        compiler_params=pltpu.CompilerParams(collective_id=1, has_side_effects=True, vmem_limit_bytes=LIMIT),
        name="sums",
    )(lhs, w)
    return mixed, own


def solution(mesh):
    in_specs = (
        P("ctx"),
        P(None, "fsdp"),
        P("ctx", None, "fsdp"),
        P(None, None, "fsdp"),
        P(None, "fsdp"),
        P(None, "fsdp"),
        P("ctx", "fsdp"),
    )
    out_specs = (P("ctx", "fsdp"), P("ctx", "fsdp"))
    return jax.shard_map(on_device, mesh=mesh, in_specs=in_specs, out_specs=out_specs, check_vma=False)
```

```python
import functools

import jax
import jax.numpy as jnp
from jax import lax
from jax.experimental import pallas as pl
from jax.experimental.pallas import tpu as pltpu
from jax.sharding import PartitionSpec as P

MESH = pl.DeviceIdType.MESH
VMEM = pl.BlockSpec(memory_space=pltpu.VMEM)
ANY = pl.BlockSpec(memory_space=pl.ANY)
LIMIT = 60 * 1024 * 1024
NC = 8
PIECES = 2
PIECE = 256
VOCAB = 512
MODES = 16
TAPS = 7


def place():
    f = lax.axis_index("fsdp")
    c = lax.axis_index("ctx")
    return f // 16, (f // 4) % 4, (f // 2) % 2, f % 2, c


def flat(x, y, h, k):
    return (x % 4) * 16 + (y % 4) * 4 + h * 2 + k


def hail(devices):
    barrier = pltpu.get_barrier_semaphore()
    for device, wanted in devices:
        if wanted is None:
            pl.semaphore_signal(barrier, inc=1, device_id=device, device_id_type=MESH)
        else:

            @pl.when(wanted)
            def _():
                pl.semaphore_signal(barrier, inc=1, device_id=device, device_id_type=MESH)


def greet(devices, count):
    hail(devices)
    pl.semaphore_wait(pltpu.get_barrier_semaphore(), count)


def table_kernel(
    embed_ref, w_ref, tok_ref, cot_ref,
    p_ref, tokall_ref, cotall_ref,
    emb, acc, part_out, part_in, pair_out, pair_in, table, toks, cots,
    local_sem, half_send, x_send, y_send, k_send, a_recv,
    part_send, part_recv, pair_send, pair_recv, done_send, done_recv,
    cot_send, cot_recv, tok_send, tok_recv,
):
    f32, bf16 = jnp.float32, jnp.bfloat16
    x, y, h, k, c = place()
    me = flat(x, y, h, k)
    mine = 2 * x + y // 2
    yb = y % 2
    edge = jnp.where(mine < NC // 2, NC - 1, 0)
    x0, y0 = c // 2, (c % 2) * 2
    dy = (y - y0 + 4) % 4
    on_row = dy < 2
    source = mine == c
    near = jnp.where(dy == 1, 1, 0)
    own = yb * 4 + h * 2 + k

    xs = [flat(x + o, y, h, k) for o in range(1, 4)]
    ys = [flat(x, y + o, h, k) for o in range(1, 4)]
    partner = flat(x, y, h, 1 - k)
    other = flat(x, y, 1 - h, k)
    gives = c == edge
    q = c % 4
    base = c - q
    across = (c + 4) % NC
    group = [(me, base + (q + o) % 4) for o in range(1, 4)]
    greet(
        [((d, c), None) for d in xs + ys + [partner]]
        + [(d, None) for d in group + [(me, across)]]
        + [((other, edge), source)],
        11 + gives.astype(jnp.int32),
    )

    local = pltpu.make_async_copy(embed_ref, emb.at[own], local_sem)

    def block_copy(slot, p, target, sem, src=None, to=c):
        rows = pl.ds(p * PIECE, PIECE)
        return pltpu.make_async_remote_copy(
            src_ref=emb.at[slot, rows] if src is None else src.at[rows], dst_ref=emb.at[slot, rows], send_sem=sem,
            recv_sem=a_recv.at[slot, p], device_id=(target, to), device_id_type=MESH,
        )

    def arrived(slot, p):
        block_copy(slot, p, partner, k_send.at[0, 0]).wait_recv()

    sends = []

    def send(copy, when):
        sends.append((copy, when))
        if when is None:
            copy.start()
        else:

            @pl.when(when)
            def _():
                copy.start()

    for p in range(PIECES):
        send(block_copy(own, p, other, half_send.at[p], embed_ref, mine), gives)
    for p in range(PIECES):
        for o in (2, 1, 3):
            send(block_copy(own, p, xs[o - 1], x_send.at[0, o - 1, p], embed_ref), source)

    @pl.when(source)
    def _():
        local.start()
        local.wait()

    def slot_of(row, b):
        return row * 4 + (h if b == 0 else 1 - h) * 2 + k

    extra = []

    def spread(index, target, sem):
        for src, dst, ss, rs in ((cot_ref, cots, cot_send, cot_recv), (tok_ref, toks, tok_send, tok_recv)):
            copy = pltpu.make_async_remote_copy(
                src_ref=src if sem < 4 else dst.at[index], dst_ref=dst.at[index], send_sem=ss.at[sem],
                recv_sem=rs.at[sem], device_id=target, device_id_type=MESH,
            )
            copy.start()
            extra.append(copy)

    for b in range(2):
        slot = slot_of(near, b)
        for p in range(PIECES):
            if b == 0:

                @pl.when(jnp.logical_not(source))
                def _():
                    arrived(slot, p)

            else:
                arrived(slot, p)
                for o in (2, 1, 3):
                    send(block_copy(slot, p, xs[o - 1], x_send.at[1, o - 1, p]), source)
            for o in (2, 1, 3):
                send(block_copy(slot, p, ys[o - 1], y_send.at[b, o - 1, p]), on_row)
            send(block_copy(slot, p, partner, k_send.at[b, p]), None)
        if b == 0:
            for o in range(1, 4):
                spread(c, group[o - 1], o - 1)
            spread(c, (me, across), 3)
            far = slot_of(1 - near, 0)
            for p in range(PIECES):
                arrived(far, p)
                send(block_copy(far, p, partner, k_send.at[2, p]), None)

    for copy in extra[6:8]:
        copy.wait_recv()
    for o in range(1, 4):
        spread(across, group[o - 1], 3 + o)

    def lane(e, b):
        return e * 4 + (h if b == 0 else 1 - h) * 2

    def product(s, b):
        total = None
        for e in range(2):
            j = lane(e, b)
            left = jnp.concatenate(
                [jnp.concatenate([emb[j + i, pl.ds(r * 128 + s * 64, 64), :] for i in range(2)], axis=1) for r in range(4)],
                axis=0,
            )
            at = pl.ds(pl.multiple_of(j * 128, 256), 256)
            right = jnp.concatenate([w_ref[g, at, :] for g in range(3)], axis=1)
            part = jnp.dot(left, right, preferred_element_type=f32)
            total = part if total is None else total + part
        return total.reshape(4, 64, 384)

    for e in range(2):
        for p in range(PIECES):
            arrived(lane(e, 0) + 1 - k, p)
    for s in range(2):
        acc[s] = product(s, 0)
    far = slot_of(1 - near, 1)
    for p in range(PIECES):
        arrived(far, p)
        send(block_copy(far, p, partner, k_send.at[3, p]), None)
    for e in range(2):
        for p in range(PIECES):
            arrived(lane(e, 1) + 1 - k, p)

    def part_copy(o, s):
        return pltpu.make_async_remote_copy(
            src_ref=part_out.at[o - 1, s], dst_ref=part_in.at[o - 1, s], send_sem=part_send.at[o - 1, s],
            recv_sem=part_recv.at[o - 1, s], device_id=(me, base + (q + o) % 4), device_id_type=MESH,
        )

    def pair_copy(s):
        return pltpu.make_async_remote_copy(
            src_ref=pair_out.at[s], dst_ref=pair_in.at[s], send_sem=pair_send.at[s], recv_sem=pair_recv.at[s],
            device_id=(me, (c + 4) % NC), device_id_type=MESH,
        )

    def done_copy(o, s):
        return pltpu.make_async_remote_copy(
            src_ref=table.at[q, s], dst_ref=table.at[q, s], send_sem=done_send.at[o - 1, s],
            recv_sem=done_recv.at[o - 1, s], device_id=(me, base + (q + o) % 4), device_id_type=MESH,
        )

    for s in range(2):
        acc[s] = acc[s] + product(s, 1)
        for o in (3, 1, 2):
            part_out[o - 1, s] = acc[s, (q + o) % 4].astype(bf16)
            part_copy(o, s).start()
    for s in range(2):
        total = acc[s, q]
        for o in range(1, 4):
            part_copy(o, s).wait_recv()
            total = total + part_in[o - 1, s].astype(f32)
        acc[s, q] = total
        pair_out[s] = total.astype(bf16)
        pair_copy(s).start()
    for s in range(2):
        pair_copy(s).wait_recv()
        table[q, s] = (acc[s, q] + pair_in[s].astype(f32)).astype(bf16)
        for o in (3, 1, 2):
            done_copy(o, s).start()

    cots[c] = cot_ref[...]
    toks[c] = tok_ref[...]
    for i, copy in enumerate(extra):
        if 6 <= i < 8:
            copy.wait_send()
        else:
            copy.wait()
    for i in range(NC):
        cotall_ref[i] = cots[i]
        tokall_ref[pl.ds(i, 1), :] = toks[i]
    for copy, when in sends:
        if when is None:
            copy.wait_send()
        else:

            @pl.when(when)
            def _():
                copy.wait_send()

    for s in range(2):
        pair_copy(s).wait_send()
        for o in range(1, 4):
            part_copy(o, s).wait_send()
            done_copy(o, s).wait()
    for i in range(4):
        for s in range(2):
            p_ref[pl.ds(i * 128 + s * 64, 64), :] = table[i, s]


def shifted_up(value, by, row):
    return jnp.where(row >= by, pltpu.roll(value, by, 0), 0.0)


def shifted_down(value, by, row):
    return jnp.where(row < 8 - by, pltpu.roll(value, 8 - by, 0), 0.0)


def scan_modes(drive_at, out_ref, rates_ref, res_ref, backward):
    row = lax.broadcasted_iota(jnp.int32, (8, 128), 0)
    shifted = shifted_down if backward else shifted_up
    length = 128

    def spread(ref, m):
        return jnp.broadcast_to(ref[m : m + 1, :], (8, 128))

    def at(j):
        j = length - 1 - j if backward else j
        return pl.ds(pl.multiple_of(j * 8, 8), 8)

    decay = [jnp.exp(-spread(rates_ref, m)) for m in range(MODES)]

    def ends(j, state):
        drive = drive_at(at(j))
        return tuple(decay[m] * state[m] + drive for m in range(MODES))

    zero = jnp.zeros((8, 128), jnp.float32)
    state = lax.fori_loop(0, length, ends, (zero,) * MODES, unroll=4)
    entering = []
    for m in range(MODES):
        rate = spread(rates_ref, m)
        whole = state[m]
        for by in (1, 2, 4):
            whole = whole + jnp.exp(-rate * float(length * by)) * shifted(whole, by, row)
        entering.append(shifted(whole, 1, row))
    weight = [spread(res_ref, m) for m in range(MODES)]

    def outs(j, state):
        where = at(j)
        drive = drive_at(where)
        state = tuple(decay[m] * state[m] + drive for m in range(MODES))
        terms = [weight[m] * state[m] for m in range(MODES)]
        while len(terms) > 1:
            terms = [a + b for a, b in zip(terms[::2], terms[1::2])]
        out_ref[where, :] = terms[0]
        return state

    lax.fori_loop(0, length, outs, tuple(entering), unroll=4)


def mix(
    p_ref, tok_ref, cot_ref, taps_ref, rates_ref, res_ref,
    mixed_ref, lhs_ref,
    z, filt, cot, drive, glong, lo, gd, gz,
):
    c = lax.axis_index("ctx")
    halo = 8
    row = lax.broadcasted_iota(jnp.int32, (8, 128), 0)
    lane = lax.broadcasted_iota(jnp.int32, (8, VOCAB), 1)

    for s in range(NC):
        cot[pl.ds(s, 128, stride=8), :] = cot_ref[s].astype(jnp.float32)

    def pick(i, toks):
        rows = []
        for j in range(0, 16, 2):
            two = [jnp.where(toks[:, j + e : j + e + 1] == lane, 1.0, 0.0) for e in range(2)]
            rows.append(jnp.concatenate(two, axis=0).astype(jnp.bfloat16))
        hot = jnp.concatenate(rows, axis=0)
        found = jnp.dot(hot, p_ref[...], preferred_element_type=jnp.float32)
        start = pl.ds(pl.multiple_of((halo + i * 16) * 8, 128 // 2), 128)
        for g in range(3):
            z[g, start, :] = found[:, g * 128 : (g + 1) * 128]
        return pltpu.roll(toks, 112, 1)

    lax.fori_loop(0, 8, pick, tok_ref[...])
    for g in range(3):
        for d in range(1, TAPS):
            z[g, pl.ds((halo - d) * 8, 8), :] = shifted_up(z[g, pl.ds((halo + 128 - d) * 8, 8), :], 1, row)

    def filter_rows(i, _):
        base = i * 64
        for g in range(3):
            value = None
            for d in range(TAPS):
                term = taps_ref[g, d : d + 1, :] * z[g, pl.ds(pl.multiple_of(base + (halo - d) * 8, 8), 64), :]
                value = term if value is None else value + term
            filt[g, pl.ds(pl.multiple_of(base, 64), 64), :] = value
        here = pl.ds(pl.multiple_of(base, 64), 64)
        drive[here, :] = filt[1, here, :] * filt[2, here, :]
        glong[here, :] = cot[here, :] * filt[0, here, :]
        return 0

    lax.fori_loop(0, 16, filter_rows, 0)
    scan_modes(lambda at: drive[at, :], lo, rates_ref, res_ref, False)
    scan_modes(lambda at: glong[at, :], gd, rates_ref, res_ref, True)

    def grads(i, _):
        here = pl.ds(pl.multiple_of(i * 64, 64), 64)
        long_out, grad_drive = lo[here, :], gd[here, :]
        z[0, here, :] = cot[here, :] * long_out
        z[1, here, :] = grad_drive * filt[2, here, :]
        z[2, here, :] = grad_drive * filt[1, here, :]
        lo[here, :] = filt[0, here, :] * long_out
        return 0

    lax.fori_loop(0, 16, grads, 0)
    mixed_ref[...] = lo[pl.ds(c, 128, stride=8), :].astype(jnp.bfloat16)
    for g in range(3):
        for d in range(TAPS - 1):
            z[g, pl.ds((128 + d) * 8, 8), :] = shifted_down(z[g, pl.ds(d * 8, 8), :], 1, row)

    def adjoint_rows(i, _):
        base = i * 64
        for g in range(3):
            value = None
            for d in range(TAPS):
                term = taps_ref[g, d : d + 1, :] * z[g, pl.ds(pl.multiple_of(base + d * 8, 8), 64), :]
                value = term if value is None else value + term
            gz[g, pl.ds(pl.multiple_of(base, 64), 64), :] = value
        return 0

    lax.fori_loop(0, 16, adjoint_rows, 0)
    for s in range(NC):
        start = (c + s) % NC
        for g in range(3):
            lhs_ref[pl.ds(s * 128, 128), pl.ds(g * 128, 128)] = gz[g, pl.ds(start, 128, stride=8), :].astype(jnp.bfloat16)


SPOT = {0: (0, 0), 1: (1, 0), 2: (0, 1), 3: (1, 1), 4: (2, 1), 5: (3, 1), 6: (2, 0), 7: (3, 0)}


def mix_kernel(
    p_ref, tok_ref, cot_ref, taps_ref, rates_ref, res_ref, w_ref,
    mixed_ref, pair_ref,
    z, filt, cot, drive, glong, lo, gd, gz, lhs_ref,
    own, core_out, core_in, first_out, first_in, second_own, second_out, second_in, last_out, last_in,
    core_send, core_recv, first_send, first_recv, second_send, second_recv, last_send, last_recv,
):
    f32, bf16 = jnp.float32, jnp.bfloat16
    x, y, h, k, c = place()
    x0, y0 = c // 2, (c % 2) * 2
    dx, dy = (x - x0 + 4) % 4, (y - y0 + 4) % 4
    partner = (flat(x, y, h, 1 - k), c)
    xs = [(flat(x + o, y, h, k), c) for o in range(1, 4)]
    ys = [(flat(x, y + o, h, k), c) for o in range(1, 4)]
    yb = jnp.where(jnp.logical_or(dy == 1, dy == 2), 1, 0)
    far = jnp.where(dy >= 2, 1, 0)
    step = jnp.where(dx < 2, dx + 2 * far, dx + 4 - 2 * far)
    owner = [(flat(x0, y0 + yb, e, k), (c + step) % NC) for e in range(2)]
    from_c = 2 * x + y // 2
    back = (c - from_c + NC) % NC
    back_x = jnp.where(back < 4, back % 2, 2 + back % 2)
    back_far = jnp.where(back < 4, back // 2, 3 - back // 2)
    back_y = jnp.where(y % 2 == 0, 3 * back_far, 1 + back_far)
    givers = [(flat(x + back_x, (y // 2) * 2 + back_y, e, k), from_c) for e in range(2)]
    loop = jnp.logical_and(dx == 0, dy < 2)
    foreign = [jnp.logical_not(jnp.logical_and(loop, h == e)) for e in range(2)]
    hail([(d, None) for d in [partner] + xs + ys] + [(givers[e], foreign[e]) for e in range(2)])
    mix(
        p_ref, tok_ref, cot_ref, taps_ref, rates_ref, res_ref, mixed_ref, lhs_ref,
        z, filt, cot, drive, glong, lo, gd, gz,
    )
    pl.semaphore_wait(pltpu.get_barrier_semaphore(), 9 - loop.astype(jnp.int32))

    def core_copy(e, a):
        return pltpu.make_async_remote_copy(
            src_ref=core_out.at[e, a], dst_ref=core_in.at[e, a],
            send_sem=core_send.at[e, a], recv_sem=core_recv.at[e, a], device_id=partner, device_id_type=MESH,
        )

    spots = [dx, dy]
    lines = [xs, ys]

    def first_copy(e, o):
        return pltpu.make_async_remote_copy(
            src_ref=first_out.at[e, o - 1], dst_ref=first_in.at[e, o - 1],
            send_sem=first_send.at[e, o - 1], recv_sem=first_recv.at[e, o - 1],
            device_id=lines[e][o - 1], device_id_type=MESH,
        )

    def second_copy(e, o):
        return pltpu.make_async_remote_copy(
            src_ref=second_out.at[e, o - 1], dst_ref=second_in.at[e, o - 1],
            send_sem=second_send.at[e, o - 1], recv_sem=second_recv.at[e, o - 1],
            device_id=lines[1 - e][o - 1], device_id_type=MESH,
        )

    def last_copy(e):
        return pltpu.make_async_remote_copy(
            src_ref=last_out.at[e], dst_ref=last_in.at[h],
            send_sem=last_send.at[e], recv_sem=last_recv.at[h], device_id=owner[e], device_id_type=MESH,
        )

    def last_wait(e):
        pltpu.make_async_remote_copy(
            src_ref=last_out.at[e], dst_ref=last_in.at[e],
            send_sem=last_send.at[e], recv_sem=last_recv.at[e], device_id=partner, device_id_type=MESH,
        ).wait_recv()

    def tile(e, kk, store):
        starts = [pl.multiple_of(r * 512 + e * 256 + kk * 128, 128) for r in range(2)]
        right = jnp.concatenate(
            [jnp.concatenate([w_ref[g, pl.ds(at, 128), :] for g in range(3)], axis=1) for at in starts], axis=0
        )
        out = lax.dot_general(lhs_ref[...], right, (((1,), (1,)), ((), ())), preferred_element_type=f32)
        for s in range(NC):
            sx, sfar = SPOT[s]
            for r in range(2):
                sy = 3 * sfar if r == 0 else 1 + sfar
                a, b = (sx, sy) if e == 0 else (sy, sx)
                store(e, a, b, out[s * 128 : (s + 1) * 128, r * 128 : (r + 1) * 128])

    def to_core(e, a, b, value):
        core_out[e, a, b] = value.astype(bf16)

    def to_own(e, a, b, value):
        own[e, a, b] = value

    for e in range(2):
        tile(e, 1 - k, to_core)
        for a in range(4):
            core_copy(e, a).start()
    for e in range(2):
        tile(e, k, to_own)
    order = [2, 1, 3, 0]
    for o in order:
        for e in range(2):
            a = (spots[e] + o) % 4
            core_copy(e, a).wait_recv()
            both = own[e, a] + core_in[e, a].astype(f32)
            if o:
                first_out[e, o - 1] = both.astype(bf16)
                first_copy(e, o).start()
            else:
                own[e, a] = both
    for e in range(2):
        for o in range(1, 4):
            first_copy(e, o).wait_recv()
    for o in order:
        for e in range(2):
            b = (spots[1 - e] + o) % 4
            both = own[e, spots[e], b]
            for i in range(3):
                both = both + first_in[e, i, b].astype(f32)
            if o:
                second_out[e, o - 1] = both
                second_copy(e, o).start()
            else:
                second_own[e] = both
    for e in range(2):
        both = second_own[e]
        for o in range(1, 4):
            second_copy(e, o).wait_recv()
            both = both + second_in[e, o - 1]
        last_out[e] = both

        @pl.when(foreign[e])
        def _():
            last_copy(e).start()

        @pl.when(jnp.logical_not(foreign[e]))
        def _():
            last_in[e] = last_out[e]

    for e in range(2):

        @pl.when(foreign[e])
        def _():
            last_wait(e)

    pair_ref[...] = last_in[...]
    for e in range(2):
        for a in range(4):
            core_copy(e, a).wait_send()
        for o in range(1, 4):
            first_copy(e, o).wait_send()
            second_copy(e, o).wait_send()

        @pl.when(foreign[e])
        def _():
            last_copy(e).wait_send()


def last_kernel(mixed_ref, pair_ref, out_ref, grad_ref):
    out_ref[...] = mixed_ref[...]
    grad_ref[...] = (pair_ref[0] + pair_ref[1]).astype(jnp.bfloat16)


def on_device(token_ids, embed, w_in, taps, rates, residues, cotangent):
    bf16, f32, i32 = jnp.bfloat16, jnp.float32, jnp.int32
    dma = pltpu.SemaphoreType.DMA
    w = w_in.transpose(1, 0, 2)
    taps = taps.transpose(1, 0, 2)
    p, toks, cots = pl.pallas_call(
        table_kernel,
        out_shape=(
            jax.ShapeDtypeStruct((VOCAB, 384), bf16),
            jax.ShapeDtypeStruct((NC, 128), i32),
            jax.ShapeDtypeStruct((NC, 128, 128), bf16),
        ),
        in_specs=[ANY, VMEM, VMEM, VMEM],
        out_specs=(VMEM, VMEM, VMEM),
        scratch_shapes=[
            pltpu.VMEM((8, VOCAB, 128), bf16),
            pltpu.VMEM((2, 4, 64, 384), f32),
            pltpu.VMEM((3, 2, 64, 384), bf16), pltpu.VMEM((3, 2, 64, 384), bf16),
            pltpu.VMEM((2, 64, 384), bf16), pltpu.VMEM((2, 64, 384), bf16),
            pltpu.VMEM((4, 2, 64, 384), bf16),
            pltpu.VMEM((NC, 1, 128), i32),
            pltpu.VMEM((NC, 128, 128), bf16),
            dma, dma((PIECES,)), dma((2, 3, PIECES)), dma((2, 3, PIECES)), dma((4, PIECES)), dma((8, PIECES)),
            dma((3, 2)), dma((3, 2)), dma((2,)), dma((2,)), dma((3, 2)), dma((3, 2)),
            dma((NC - 1,)), dma((NC - 1,)), dma((NC - 1,)), dma((NC - 1,)),
        ],
        compiler_params=pltpu.CompilerParams(collective_id=0, has_side_effects=True, vmem_limit_bytes=LIMIT),
        name="table",
    )(embed, w, token_ids.reshape(1, 128), cotangent)
    wide = pltpu.VMEM((1024, 128), f32)
    mixed, pair = pl.pallas_call(
        mix_kernel,
        out_shape=(
            jax.ShapeDtypeStruct((128, 128), bf16),
            jax.ShapeDtypeStruct((2, 128, 128), f32),
        ),
        in_specs=[VMEM] * 7,
        out_specs=(VMEM, VMEM),
        scratch_shapes=[
            pltpu.VMEM((3, 136 * 8, 128), f32), pltpu.VMEM((3, 1024, 128), f32),
            wide, wide, wide, wide, wide,
            pltpu.VMEM((3, 1024, 128), f32), pltpu.VMEM((1024, 384), bf16),
            pltpu.VMEM((2, 4, 4, 128, 128), f32),
            pltpu.VMEM((2, 4, 4, 128, 128), bf16), pltpu.VMEM((2, 4, 4, 128, 128), bf16),
            pltpu.VMEM((2, 3, 4, 128, 128), bf16), pltpu.VMEM((2, 3, 4, 128, 128), bf16),
            pltpu.VMEM((2, 128, 128), f32),
            pltpu.VMEM((2, 3, 128, 128), f32), pltpu.VMEM((2, 3, 128, 128), f32),
            pltpu.VMEM((2, 128, 128), f32), pltpu.VMEM((2, 128, 128), f32),
            dma((2, 4)), dma((2, 4)), dma((2, 3)), dma((2, 3)), dma((2, 3)), dma((2, 3)), dma((2,)), dma((2,)),
        ],
        compiler_params=pltpu.CompilerParams(collective_id=1, has_side_effects=True, vmem_limit_bytes=LIMIT),
        name="mix",
    )(p, toks, cots, taps, rates, residues, w)
    return pl.pallas_call(
        last_kernel,
        out_shape=(jax.ShapeDtypeStruct((128, 128), bf16), jax.ShapeDtypeStruct((128, 128), bf16)),
        in_specs=[VMEM, VMEM],
        out_specs=(VMEM, VMEM),
        name="last",
    )(mixed, pair)


def solution(mesh):
    in_specs = (
        P("ctx"),
        P(None, "fsdp"),
        P("ctx", None, "fsdp"),
        P(None, None, "fsdp"),
        P(None, "fsdp"),
        P(None, "fsdp"),
        P("ctx", "fsdp"),
    )
    out_specs = (P("ctx", "fsdp"), P("ctx", "fsdp"))
    return jax.shard_map(on_device, mesh=mesh, in_specs=in_specs, out_specs=out_specs, check_vma=False)
```

```python
import functools

import jax
import jax.numpy as jnp
from jax import lax
from jax.experimental import pallas as pl
from jax.experimental.pallas import tpu as pltpu
from jax.sharding import PartitionSpec as P

MESH = pl.DeviceIdType.MESH
VMEM = pl.BlockSpec(memory_space=pltpu.VMEM)
ANY = pl.BlockSpec(memory_space=pl.ANY)
LIMIT = 60 * 1024 * 1024
NC = 8
CHIPS = 16
PIECE = 32
VOCAB = 512
MODES = 16
TAPS = 7


def place():
    f = lax.axis_index("fsdp")
    c = lax.axis_index("ctx")
    return f // 16, (f // 4) % 4, (f // 2) % 2, f % 2, c


def flat(x, y, h, k):
    return (x % 4) * 16 + (y % 4) * 4 + h * 2 + k


def hail(devices):
    barrier = pltpu.get_barrier_semaphore()
    for device, wanted in devices:
        if wanted is None:
            pl.semaphore_signal(barrier, inc=1, device_id=device, device_id_type=MESH)
        else:

            @pl.when(wanted)
            def _():
                pl.semaphore_signal(barrier, inc=1, device_id=device, device_id_type=MESH)


def greet(devices, count):
    hail(devices)
    pl.semaphore_wait(pltpu.get_barrier_semaphore(), count)


def table_kernel(
    embed_ref, w_ref, tok_ref, cot_ref,
    p_ref, tokall_ref, cotall_ref,
    emb, stage, acc, part_out, part_in, pair_out, pair_in, table, toks, cots,
    local_sem, half_send, half_recv, scat_send, scat_recv, all_send, all_recv, core_send, core_recv,
    part_send, part_recv, pair_send, pair_recv, done_send, done_recv,
    cot_send, cot_recv, tok_send, tok_recv,
):
    f32, bf16 = jnp.float32, jnp.bfloat16
    x, y, h, k, c = place()
    me = flat(x, y, h, k)
    spot = x * 4 + y
    mine = 2 * x + y // 2
    yb = y % 2
    edge = jnp.where(mine < NC // 2, NC - 1, 0)
    source = mine == c
    gives = c == edge
    partner = flat(x, y, h, 1 - k)
    other = flat(x, y, 1 - h, k)
    q = c % 4
    base = c - q
    across = (c + 4) % NC
    group = [(me, base + (q + o) % 4) for o in range(1, 4)]

    def chip(i):
        return flat(i // 4, i % 4, h, k)

    greet(
        [((chip((spot + o) % CHIPS), c), None) for o in range(1, CHIPS)]
        + [((partner, c), None)]
        + [(d, None) for d in group + [(me, across)]]
        + [((other, edge), source)],
        CHIPS + 4 + gives.astype(jnp.int32),
    )

    def half_copy(m):
        rows = pl.ds(m * 128, 128)
        return pltpu.make_async_remote_copy(
            src_ref=embed_ref.at[rows], dst_ref=stage.at[rows], send_sem=half_send.at[m], recv_sem=half_recv.at[m],
            device_id=(other, mine), device_id_type=MESH,
        )

    def side(b):
        return h if b == 0 else 1 - h

    def scat_copy(b, i, row):
        rows = pl.ds(pl.multiple_of(i * PIECE, PIECE), PIECE)
        return pltpu.make_async_remote_copy(
            src_ref=(embed_ref if b == 0 else stage).at[rows], dst_ref=emb.at[i, side(b), k, row],
            send_sem=scat_send.at[b, i], recv_sem=scat_recv.at[b, row], device_id=(chip(i), c), device_id_type=MESH,
        )

    def own_copy(b):
        rows = pl.ds(pl.multiple_of(spot * PIECE, PIECE), PIECE)
        return pltpu.make_async_copy(
            (embed_ref if b == 0 else stage).at[rows], emb.at[spot, side(b), k, yb], local_sem.at[b]
        )

    def all_copy(b, o):
        return pltpu.make_async_remote_copy(
            src_ref=emb.at[spot, side(b), k], dst_ref=emb.at[spot, side(b), k], send_sem=all_send.at[b, o],
            recv_sem=all_recv.at[b, o], device_id=(chip((spot + o) % CHIPS), c), device_id_type=MESH,
        )

    def core_copy(b, o):
        i = (spot + CHIPS - o) % CHIPS
        return pltpu.make_async_remote_copy(
            src_ref=emb.at[i, side(b), k], dst_ref=emb.at[i, side(b), k], send_sem=core_send.at[b, o],
            recv_sem=core_recv.at[b, o], device_id=(partner, c), device_id_type=MESH,
        )

    def each(first, last, body):
        def step(i, _):
            body(i)
            return 0

        lax.fori_loop(first, last, step, 0)

    @pl.when(gives)
    def _():
        for m in range(4):
            half_copy(m).start()

    def scatter(b, o):
        i = (spot + o) % CHIPS
        scat_copy(b, i, yb).start()

    @pl.when(source)
    def _():
        each(1, CHIPS, lambda o: scatter(0, o))
        own_copy(0).start()
        own_copy(0).wait()

    extra = []

    def spread(index, target, sem):
        for src, dst, ss, rs in ((cot_ref, cots, cot_send, cot_recv), (tok_ref, toks, tok_send, tok_recv)):
            copy = pltpu.make_async_remote_copy(
                src_ref=src if sem < 4 else dst.at[index], dst_ref=dst.at[index], send_sem=ss.at[sem],
                recv_sem=rs.at[sem], device_id=target, device_id_type=MESH,
            )
            copy.start()
            extra.append(copy)

    def share(b):
        for row in range(2):

            @pl.when(jnp.logical_not(jnp.logical_and(source, yb == row)))
            def _():
                scat_copy(b, spot, row).wait_recv()

        each(1, CHIPS, lambda o: all_copy(b, o).start())
        core_copy(b, 0).start()

    def gathered(b, o):
        all_copy(b, o).wait_recv()
        core_copy(b, o).start()

    share(0)

    @pl.when(source)
    def _():
        for m in range(4):
            half_copy(m).wait_recv()
            for i in range(m * 4, m * 4 + 4):

                @pl.when(i != spot)
                def _():
                    scat_copy(1, i, yb).start()

        own_copy(1).start()
        own_copy(1).wait()

    for o in range(1, 4):
        spread(c, group[o - 1], o - 1)
    spread(c, (me, across), 3)
    share(1)
    each(1, CHIPS, lambda o: gathered(0, o))
    for copy in extra[6:8]:
        copy.wait_recv()
    for o in range(1, 4):
        spread(across, group[o - 1], 3 + o)

    def product(s, b):
        total = None
        hb = side(b)
        for e in range(2):
            left = jnp.concatenate(
                [
                    jnp.concatenate([emb[s * 8 + i, hb, kk, e] for kk in range(2)], axis=1)
                    for i in range(8)
                ],
                axis=0,
            )
            at = pl.ds(pl.multiple_of(e * 512 + hb * 256, 256), 256)
            right = jnp.concatenate([w_ref[g, at, :] for g in range(3)], axis=1)
            part = jnp.dot(left, right, preferred_element_type=f32)
            total = part if total is None else total + part
        return total.reshape(4, 64, 384)

    each(0, CHIPS, lambda o: core_copy(0, o).wait_recv())
    for s in range(2):
        acc[s] = product(s, 0)
    each(1, CHIPS, lambda o: gathered(1, o))
    each(0, CHIPS, lambda o: core_copy(1, o).wait_recv())

    def part_copy(o, s):
        return pltpu.make_async_remote_copy(
            src_ref=part_out.at[o - 1, s], dst_ref=part_in.at[o - 1, s], send_sem=part_send.at[o - 1, s],
            recv_sem=part_recv.at[o - 1, s], device_id=(me, base + (q + o) % 4), device_id_type=MESH,
        )

    def pair_copy(s):
        return pltpu.make_async_remote_copy(
            src_ref=pair_out.at[s], dst_ref=pair_in.at[s], send_sem=pair_send.at[s], recv_sem=pair_recv.at[s],
            device_id=(me, (c + 4) % NC), device_id_type=MESH,
        )

    def done_copy(o, s):
        return pltpu.make_async_remote_copy(
            src_ref=table.at[q, s], dst_ref=table.at[q, s], send_sem=done_send.at[o - 1, s],
            recv_sem=done_recv.at[o - 1, s], device_id=(me, base + (q + o) % 4), device_id_type=MESH,
        )

    for s in range(2):
        acc[s] = acc[s] + product(s, 1)
        for o in (3, 1, 2):
            part_out[o - 1, s] = acc[s, (q + o) % 4].astype(bf16)
            part_copy(o, s).start()
    for s in range(2):
        total = acc[s, q]
        for o in range(1, 4):
            part_copy(o, s).wait_recv()
            total = total + part_in[o - 1, s].astype(f32)
        acc[s, q] = total
        pair_out[s] = total.astype(bf16)
        pair_copy(s).start()
    for s in range(2):
        pair_copy(s).wait_recv()
        table[q, s] = (acc[s, q] + pair_in[s].astype(f32)).astype(bf16)
        for o in (3, 1, 2):
            done_copy(o, s).start()

    cots[c] = cot_ref[...]
    toks[c] = tok_ref[...]
    for i, copy in enumerate(extra):
        if 6 <= i < 8:
            copy.wait_send()
        else:
            copy.wait()
    for i in range(NC):
        cotall_ref[i] = cots[i]
        tokall_ref[pl.ds(i, 1), :] = toks[i]
    for b in range(2):
        each(1, CHIPS, lambda o: all_copy(b, o).wait_send())
        each(0, CHIPS, lambda o: core_copy(b, o).wait_send())

    @pl.when(source)
    def _():
        for b in range(2):
            each(1, CHIPS, lambda o: scat_copy(b, (spot + o) % CHIPS, yb).wait_send())

    @pl.when(gives)
    def _():
        for m in range(4):
            half_copy(m).wait_send()

    for s in range(2):
        pair_copy(s).wait_send()
        for o in range(1, 4):
            part_copy(o, s).wait_send()
            done_copy(o, s).wait()
    for i in range(4):
        for s in range(2):
            p_ref[pl.ds(s * 256 + i * 64, 64), :] = table[i, s]


def shifted_up(value, by, row):
    return jnp.where(row >= by, pltpu.roll(value, by, 0), 0.0)


def shifted_down(value, by, row):
    return jnp.where(row < 8 - by, pltpu.roll(value, 8 - by, 0), 0.0)


def scan_modes(drive_at, out_ref, rates_ref, res_ref, backward):
    row = lax.broadcasted_iota(jnp.int32, (8, 128), 0)
    shifted = shifted_down if backward else shifted_up
    length = 128

    def spread(ref, m):
        return jnp.broadcast_to(ref[m : m + 1, :], (8, 128))

    def at(j):
        j = length - 1 - j if backward else j
        return pl.ds(pl.multiple_of(j * 8, 8), 8)

    decay = [jnp.exp(-spread(rates_ref, m)) for m in range(MODES)]

    def ends(j, state):
        drive = drive_at(at(j))
        return tuple(decay[m] * state[m] + drive for m in range(MODES))

    zero = jnp.zeros((8, 128), jnp.float32)
    state = lax.fori_loop(0, length, ends, (zero,) * MODES, unroll=4)
    entering = []
    for m in range(MODES):
        rate = spread(rates_ref, m)
        whole = state[m]
        for by in (1, 2, 4):
            whole = whole + jnp.exp(-rate * float(length * by)) * shifted(whole, by, row)
        entering.append(shifted(whole, 1, row))
    weight = [spread(res_ref, m) for m in range(MODES)]

    def outs(j, state):
        where = at(j)
        drive = drive_at(where)
        state = tuple(decay[m] * state[m] + drive for m in range(MODES))
        terms = [weight[m] * state[m] for m in range(MODES)]
        while len(terms) > 1:
            terms = [a + b for a, b in zip(terms[::2], terms[1::2])]
        out_ref[where, :] = terms[0]
        return state

    lax.fori_loop(0, length, outs, tuple(entering), unroll=4)


def mix(
    p_ref, tok_ref, cot_ref, taps_ref, rates_ref, res_ref,
    mixed_ref, lhs_ref,
    z, filt, cot, drive, glong, lo, gd, gz,
):
    c = lax.axis_index("ctx")
    halo = 8
    row = lax.broadcasted_iota(jnp.int32, (8, 128), 0)
    lane = lax.broadcasted_iota(jnp.int32, (8, VOCAB), 1)

    for s in range(NC):
        cot[pl.ds(s, 128, stride=8), :] = cot_ref[s].astype(jnp.float32)

    def pick(i, toks):
        rows = []
        for j in range(0, 16, 2):
            two = [jnp.where(toks[:, j + e : j + e + 1] == lane, 1.0, 0.0) for e in range(2)]
            rows.append(jnp.concatenate(two, axis=0).astype(jnp.bfloat16))
        hot = jnp.concatenate(rows, axis=0)
        found = jnp.dot(hot, p_ref[...], preferred_element_type=jnp.float32)
        start = pl.ds(pl.multiple_of((halo + i * 16) * 8, 128 // 2), 128)
        for g in range(3):
            z[g, start, :] = found[:, g * 128 : (g + 1) * 128]
        return pltpu.roll(toks, 112, 1)

    lax.fori_loop(0, 8, pick, tok_ref[...])
    for g in range(3):
        for d in range(1, TAPS):
            z[g, pl.ds((halo - d) * 8, 8), :] = shifted_up(z[g, pl.ds((halo + 128 - d) * 8, 8), :], 1, row)

    def filter_rows(i, _):
        base = i * 64
        for g in range(3):
            value = None
            for d in range(TAPS):
                term = taps_ref[g, d : d + 1, :] * z[g, pl.ds(pl.multiple_of(base + (halo - d) * 8, 8), 64), :]
                value = term if value is None else value + term
            filt[g, pl.ds(pl.multiple_of(base, 64), 64), :] = value
        here = pl.ds(pl.multiple_of(base, 64), 64)
        drive[here, :] = filt[1, here, :] * filt[2, here, :]
        glong[here, :] = cot[here, :] * filt[0, here, :]
        return 0

    lax.fori_loop(0, 16, filter_rows, 0)
    scan_modes(lambda at: drive[at, :], lo, rates_ref, res_ref, False)
    scan_modes(lambda at: glong[at, :], gd, rates_ref, res_ref, True)

    def grads(i, _):
        here = pl.ds(pl.multiple_of(i * 64, 64), 64)
        long_out, grad_drive = lo[here, :], gd[here, :]
        z[0, here, :] = cot[here, :] * long_out
        z[1, here, :] = grad_drive * filt[2, here, :]
        z[2, here, :] = grad_drive * filt[1, here, :]
        lo[here, :] = filt[0, here, :] * long_out
        return 0

    lax.fori_loop(0, 16, grads, 0)
    mixed_ref[...] = lo[pl.ds(c, 128, stride=8), :].astype(jnp.bfloat16)
    for g in range(3):
        for d in range(TAPS - 1):
            z[g, pl.ds((128 + d) * 8, 8), :] = shifted_down(z[g, pl.ds(d * 8, 8), :], 1, row)

    def adjoint_rows(i, _):
        base = i * 64
        for g in range(3):
            value = None
            for d in range(TAPS):
                term = taps_ref[g, d : d + 1, :] * z[g, pl.ds(pl.multiple_of(base + d * 8, 8), 64), :]
                value = term if value is None else value + term
            gz[g, pl.ds(pl.multiple_of(base, 64), 64), :] = value
        return 0

    lax.fori_loop(0, 16, adjoint_rows, 0)
    for s in range(NC):
        start = (c + s) % NC
        for g in range(3):
            lhs_ref[pl.ds(s * 128, 128), pl.ds(g * 128, 128)] = gz[g, pl.ds(start, 128, stride=8), :].astype(jnp.bfloat16)


SPOT = {0: (0, 0), 1: (1, 0), 2: (0, 1), 3: (1, 1), 4: (2, 1), 5: (3, 1), 6: (2, 0), 7: (3, 0)}


def mix_kernel(
    p_ref, tok_ref, cot_ref, taps_ref, rates_ref, res_ref, w_ref,
    mixed_ref, pair_ref,
    z, filt, cot, drive, glong, lo, gd, gz, lhs_ref,
    own, core_out, core_in, rest_out, rest_in, last_out, last_in,
    core_send, core_recv, rest_send, rest_recv, last_send, last_recv,
):
    f32, bf16 = jnp.float32, jnp.bfloat16
    x, y, h, k, c = place()
    x0, y0 = c // 2, (c % 2) * 2
    dx, dy = (x - x0 + 4) % 4, (y - y0 + 4) % 4
    partner = (flat(x, y, h, 1 - k), c)
    spot = x * 4 + y

    def chip(o):
        i = (spot + o) % CHIPS
        return i // 4, i % 4

    yb = jnp.where(jnp.logical_or(dy == 1, dy == 2), 1, 0)
    far = jnp.where(dy >= 2, 1, 0)
    step = jnp.where(dx < 2, dx + 2 * far, dx + 4 - 2 * far)
    owner = [(flat(x0, y0 + yb, e, k), (c + step) % NC) for e in range(2)]
    from_c = 2 * x + y // 2
    back = (c - from_c + NC) % NC
    back_x = jnp.where(back < 4, back % 2, 2 + back % 2)
    back_far = jnp.where(back < 4, back // 2, 3 - back // 2)
    back_y = jnp.where(y % 2 == 0, 3 * back_far, 1 + back_far)
    givers = [(flat(x + back_x, (y // 2) * 2 + back_y, e, k), from_c) for e in range(2)]
    loop = jnp.logical_and(dx == 0, dy < 2)
    foreign = [jnp.logical_not(jnp.logical_and(loop, h == e)) for e in range(2)]
    plane = [(flat(*chip(o), h, k), c) for o in range(1, CHIPS)]
    hail([(d, None) for d in [partner] + plane] + [(givers[e], foreign[e]) for e in range(2)])
    mix(
        p_ref, tok_ref, cot_ref, taps_ref, rates_ref, res_ref, mixed_ref, lhs_ref,
        z, filt, cot, drive, glong, lo, gd, gz,
    )
    pl.semaphore_wait(pltpu.get_barrier_semaphore(), CHIPS + 2 - loop.astype(jnp.int32))

    def core_copy(e, a):
        return pltpu.make_async_remote_copy(
            src_ref=core_out.at[e, pl.ds(a * 4, 4)], dst_ref=core_in.at[e, pl.ds(a * 4, 4)],
            send_sem=core_send.at[e, a], recv_sem=core_recv.at[e, a], device_id=partner, device_id_type=MESH,
        )

    def slot(o):
        cx, cy = chip(o)
        return ((cx - x0 + 4) % 4) * 4 + (cy - y0 + 4) % 4

    def rest_copy(e, o):
        return pltpu.make_async_remote_copy(
            src_ref=rest_out.at[e, o], dst_ref=rest_in.at[e, o],
            send_sem=rest_send.at[e, o], recv_sem=rest_recv.at[e, o],
            device_id=(flat(*chip(o), h, k), c), device_id_type=MESH,
        )

    def last_copy(e):
        return pltpu.make_async_remote_copy(
            src_ref=last_out.at[e], dst_ref=last_in.at[h],
            send_sem=last_send.at[e], recv_sem=last_recv.at[h], device_id=owner[e], device_id_type=MESH,
        )

    def last_wait(e):
        pltpu.make_async_remote_copy(
            src_ref=last_out.at[e], dst_ref=last_in.at[e],
            send_sem=last_send.at[e], recv_sem=last_recv.at[e], device_id=partner, device_id_type=MESH,
        ).wait_recv()

    def tile(e, kk, store):
        starts = [pl.multiple_of(r * 512 + e * 256 + kk * 128, 128) for r in range(2)]
        right = jnp.concatenate(
            [jnp.concatenate([w_ref[g, pl.ds(at, 128), :] for g in range(3)], axis=1) for at in starts], axis=0
        )
        out = lax.dot_general(lhs_ref[...], right, (((1,), (1,)), ((), ())), preferred_element_type=f32)
        for s in range(NC):
            sx, sfar = SPOT[s]
            for r in range(2):
                sy = 3 * sfar if r == 0 else 1 + sfar
                store(e, sx * 4 + sy, out[s * 128 : (s + 1) * 128, r * 128 : (r + 1) * 128])

    def to_core(e, a, value):
        core_out[e, a] = value.astype(bf16)

    def to_own(e, a, value):
        own[e, a] = value

    for e in range(2):
        tile(e, 1 - k, to_core)
        for a in range(4):
            core_copy(e, a).start()
    for e in range(2):
        tile(e, k, to_own)
        for a in range(4):
            core_copy(e, a).wait_recv()

        def give(o, _):
            a = slot(o)
            rest_out[e, o] = (own[e, a] + core_in[e, a].astype(f32)).astype(bf16)
            rest_copy(e, o).start()
            return 0

        lax.fori_loop(1, CHIPS, give, 0)
    for e in range(2):

        def take(o, both):
            rest_copy(e, o).wait_recv()
            return both + rest_in[e, o].astype(f32)

        home = dx * 4 + dy
        both = lax.fori_loop(1, CHIPS, take, own[e, home] + core_in[e, home].astype(f32))
        last_out[e] = both

        @pl.when(foreign[e])
        def _():
            last_copy(e).start()

        @pl.when(jnp.logical_not(foreign[e]))
        def _():
            last_in[e] = last_out[e]

    for e in range(2):

        @pl.when(foreign[e])
        def _():
            last_wait(e)

    pair_ref[...] = last_in[...]
    for e in range(2):
        for a in range(4):
            core_copy(e, a).wait_send()

        def sent(o, _):
            rest_copy(e, o).wait_send()
            return 0

        lax.fori_loop(1, CHIPS, sent, 0)

        @pl.when(foreign[e])
        def _():
            last_copy(e).wait_send()


def last_kernel(mixed_ref, pair_ref, out_ref, grad_ref):
    out_ref[...] = mixed_ref[...]
    grad_ref[...] = (pair_ref[0] + pair_ref[1]).astype(jnp.bfloat16)


def on_device(token_ids, embed, w_in, taps, rates, residues, cotangent):
    bf16, f32, i32 = jnp.bfloat16, jnp.float32, jnp.int32
    dma = pltpu.SemaphoreType.DMA
    w = w_in.transpose(1, 0, 2)
    taps = taps.transpose(1, 0, 2)
    p, toks, cots = pl.pallas_call(
        table_kernel,
        out_shape=(
            jax.ShapeDtypeStruct((VOCAB, 384), bf16),
            jax.ShapeDtypeStruct((NC, 128), i32),
            jax.ShapeDtypeStruct((NC, 128, 128), bf16),
        ),
        in_specs=[ANY, VMEM, VMEM, VMEM],
        out_specs=(VMEM, VMEM, VMEM),
        scratch_shapes=[
            pltpu.VMEM((CHIPS, 2, 2, 2, PIECE, 128), bf16),
            pltpu.VMEM((VOCAB, 128), bf16),
            pltpu.VMEM((2, 4, 64, 384), f32),
            pltpu.VMEM((3, 2, 64, 384), bf16), pltpu.VMEM((3, 2, 64, 384), bf16),
            pltpu.VMEM((2, 64, 384), bf16), pltpu.VMEM((2, 64, 384), bf16),
            pltpu.VMEM((4, 2, 64, 384), bf16),
            pltpu.VMEM((NC, 1, 128), i32),
            pltpu.VMEM((NC, 128, 128), bf16),
            dma((2,)), dma((4,)), dma((4,)), dma((2, CHIPS)), dma((2, 2)),
            dma((2, CHIPS)), dma((2, CHIPS)), dma((2, CHIPS)), dma((2, CHIPS)),
            dma((3, 2)), dma((3, 2)), dma((2,)), dma((2,)), dma((3, 2)), dma((3, 2)),
            dma((NC - 1,)), dma((NC - 1,)), dma((NC - 1,)), dma((NC - 1,)),
        ],
        compiler_params=pltpu.CompilerParams(collective_id=0, has_side_effects=True, vmem_limit_bytes=LIMIT),
        name="table",
    )(embed, w, token_ids.reshape(1, 128), cotangent)
    wide = pltpu.VMEM((1024, 128), f32)
    mixed, pair = pl.pallas_call(
        mix_kernel,
        out_shape=(
            jax.ShapeDtypeStruct((128, 128), bf16),
            jax.ShapeDtypeStruct((2, 128, 128), f32),
        ),
        in_specs=[VMEM] * 7,
        out_specs=(VMEM, VMEM),
        scratch_shapes=[
            pltpu.VMEM((3, 136 * 8, 128), f32), pltpu.VMEM((3, 1024, 128), f32),
            wide, wide, wide, wide, wide,
            pltpu.VMEM((3, 1024, 128), f32), pltpu.VMEM((1024, 384), bf16),
            pltpu.VMEM((2, CHIPS, 128, 128), f32),
            pltpu.VMEM((2, CHIPS, 128, 128), bf16), pltpu.VMEM((2, CHIPS, 128, 128), bf16),
            pltpu.VMEM((2, CHIPS, 128, 128), bf16), pltpu.VMEM((2, CHIPS, 128, 128), bf16),
            pltpu.VMEM((2, 128, 128), f32), pltpu.VMEM((2, 128, 128), f32),
            dma((2, 4)), dma((2, 4)), dma((2, CHIPS)), dma((2, CHIPS)), dma((2,)), dma((2,)),
        ],
        compiler_params=pltpu.CompilerParams(collective_id=1, has_side_effects=True, vmem_limit_bytes=LIMIT),
        name="mix",
    )(p, toks, cots, taps, rates, residues, w)
    return pl.pallas_call(
        last_kernel,
        out_shape=(jax.ShapeDtypeStruct((128, 128), bf16), jax.ShapeDtypeStruct((128, 128), bf16)),
        in_specs=[VMEM, VMEM],
        out_specs=(VMEM, VMEM),
        name="last",
    )(mixed, pair)


def solution(mesh):
    in_specs = (
        P("ctx"),
        P(None, "fsdp"),
        P("ctx", None, "fsdp"),
        P(None, None, "fsdp"),
        P(None, "fsdp"),
        P(None, "fsdp"),
        P("ctx", "fsdp"),
    )
    out_specs = (P("ctx", "fsdp"), P("ctx", "fsdp"))
    return jax.shard_map(on_device, mesh=mesh, in_specs=in_specs, out_specs=out_specs, check_vma=False)
```

```python
import functools

import jax
import jax.numpy as jnp
from jax import lax
from jax.experimental import pallas as pl
from jax.experimental.pallas import tpu as pltpu
from jax.sharding import PartitionSpec as P

MESH = pl.DeviceIdType.MESH
VMEM = pl.BlockSpec(memory_space=pltpu.VMEM)
ANY = pl.BlockSpec(memory_space=pl.ANY)
LIMIT = 60 * 1024 * 1024
NC = 8
CHIPS = 16
PIECE = 32
VOCAB = 512
MODES = 16
TAPS = 7


def place():
    f = lax.axis_index("fsdp")
    c = lax.axis_index("ctx")
    return f // 16, (f // 4) % 4, (f // 2) % 2, f % 2, c


def flat(x, y, h, k):
    return (x % 4) * 16 + (y % 4) * 4 + h * 2 + k


def hail(devices):
    barrier = pltpu.get_barrier_semaphore()
    for device, wanted in devices:
        if wanted is None:
            pl.semaphore_signal(barrier, inc=1, device_id=device, device_id_type=MESH)
        else:

            @pl.when(wanted)
            def _():
                pl.semaphore_signal(barrier, inc=1, device_id=device, device_id_type=MESH)


def greet(devices, count):
    hail(devices)
    pl.semaphore_wait(pltpu.get_barrier_semaphore(), count)


def build_table(
    friends, count, embed_ref, w_ref, w_copy, tok_ref, cot_ref,
    emb, stage, acc, part_out, part_in, pair_out, pair_in, table, toks, cots,
    local_sem, half_send, half_recv, scat_send, scat_recv, all_send, all_recv, core_send, core_recv,
    part_send, part_recv, pair_send, pair_recv, done_send, done_recv,
    cot_send, cot_recv, tok_send, tok_recv,
):
    f32, bf16 = jnp.float32, jnp.bfloat16
    x, y, h, k, c = place()
    me = flat(x, y, h, k)
    spot = x * 4 + y
    mine = 2 * x + y // 2
    yb = y % 2
    edge = jnp.where(mine < NC // 2, NC - 1, 0)
    source = mine == c
    gives = c == edge
    partner = flat(x, y, h, 1 - k)
    other = flat(x, y, 1 - h, k)
    q = c % 4
    base = c - q
    across = (c + 4) % NC
    group = [(me, base + (q + o) % 4) for o in range(1, 4)]

    def chip(i):
        return flat(i // 4, i % 4, h, k)

    greet(
        [((chip((spot + o) % CHIPS), c), None) for o in range(1, CHIPS)]
        + [((partner, c), None)]
        + [(d, None) for d in group + [(me, across)]]
        + [((other, edge), source)]
        + friends,
        CHIPS + 4 + gives.astype(jnp.int32) + count,
    )

    def half_copy(m):
        rows = pl.ds(m * 128, 128)
        return pltpu.make_async_remote_copy(
            src_ref=embed_ref.at[rows], dst_ref=stage.at[rows], send_sem=half_send.at[m], recv_sem=half_recv.at[m],
            device_id=(other, mine), device_id_type=MESH,
        )

    def side(b):
        return h if b == 0 else 1 - h

    def scat_copy(b, i, row):
        rows = pl.ds(pl.multiple_of(i * PIECE, PIECE), PIECE)
        return pltpu.make_async_remote_copy(
            src_ref=(embed_ref if b == 0 else stage).at[rows], dst_ref=emb.at[i, side(b), k, row],
            send_sem=scat_send.at[b, i], recv_sem=scat_recv.at[b, row], device_id=(chip(i), c), device_id_type=MESH,
        )

    def own_copy(b):
        rows = pl.ds(pl.multiple_of(spot * PIECE, PIECE), PIECE)
        return pltpu.make_async_copy(
            (embed_ref if b == 0 else stage).at[rows], emb.at[spot, side(b), k, yb], local_sem.at[b]
        )

    def all_copy(b, o):
        return pltpu.make_async_remote_copy(
            src_ref=emb.at[spot, side(b), k], dst_ref=emb.at[spot, side(b), k], send_sem=all_send.at[b, o],
            recv_sem=all_recv.at[b, o], device_id=(chip((spot + o) % CHIPS), c), device_id_type=MESH,
        )

    def core_copy(b, o):
        i = (spot + CHIPS - o) % CHIPS
        return pltpu.make_async_remote_copy(
            src_ref=emb.at[i, side(b), k], dst_ref=emb.at[i, side(b), k], send_sem=core_send.at[b, o],
            recv_sem=core_recv.at[b, o], device_id=(partner, c), device_id_type=MESH,
        )

    def each(first, last, body):
        def step(i, _):
            body(i)
            return 0

        lax.fori_loop(first, last, step, 0)

    @pl.when(gives)
    def _():
        for m in range(4):
            half_copy(m).start()

    def scatter(b, o):
        i = (spot + o) % CHIPS
        scat_copy(b, i, yb).start()

    @pl.when(source)
    def _():
        each(1, CHIPS, lambda o: scatter(0, o))
        own_copy(0).start()
        own_copy(0).wait()

    extra = []

    def spread(index, target, sem):
        for src, dst, ss, rs in ((cot_ref, cots, cot_send, cot_recv), (tok_ref, toks, tok_send, tok_recv)):
            copy = pltpu.make_async_remote_copy(
                src_ref=src if sem < 4 else dst.at[index], dst_ref=dst.at[index], send_sem=ss.at[sem],
                recv_sem=rs.at[sem], device_id=target, device_id_type=MESH,
            )
            copy.start()
            extra.append(copy)

    def share(b):
        for row in range(2):

            @pl.when(jnp.logical_not(jnp.logical_and(source, yb == row)))
            def _():
                scat_copy(b, spot, row).wait_recv()

        each(1, CHIPS, lambda o: all_copy(b, o).start())
        core_copy(b, 0).start()

    def gathered(b, o):
        all_copy(b, o).wait_recv()
        core_copy(b, o).start()

    share(0)

    @pl.when(source)
    def _():
        for m in range(4):
            half_copy(m).wait_recv()
            for i in range(m * 4, m * 4 + 4):

                @pl.when(i != spot)
                def _():
                    scat_copy(1, i, yb).start()

        own_copy(1).start()
        own_copy(1).wait()

    for o in range(1, 4):
        spread(c, group[o - 1], o - 1)
    spread(c, (me, across), 3)
    share(1)
    each(1, CHIPS, lambda o: gathered(0, o))
    for copy in extra[6:8]:
        copy.wait_recv()
    for o in range(1, 4):
        spread(across, group[o - 1], 3 + o)

    def product(s, b):
        total = None
        hb = side(b)
        for e in range(2):
            left = jnp.concatenate(
                [
                    jnp.concatenate([emb[s * 8 + i, hb, kk, e] for kk in range(2)], axis=1)
                    for i in range(8)
                ],
                axis=0,
            )
            at = pl.ds(pl.multiple_of(e * 512 + hb * 256, 256), 256)
            right = jnp.concatenate([w_ref[g, at, :] for g in range(3)], axis=1)
            part = jnp.dot(left, right, preferred_element_type=f32)
            total = part if total is None else total + part
        return total.reshape(4, 64, 384)

    each(0, CHIPS, lambda o: core_copy(0, o).wait_recv())
    w_copy.wait()
    for s in range(2):
        acc[s] = product(s, 0)
    each(1, CHIPS, lambda o: gathered(1, o))
    each(0, CHIPS, lambda o: core_copy(1, o).wait_recv())

    def part_copy(o, s):
        return pltpu.make_async_remote_copy(
            src_ref=part_out.at[o - 1, s], dst_ref=part_in.at[o - 1, s], send_sem=part_send.at[o - 1, s],
            recv_sem=part_recv.at[o - 1, s], device_id=(me, base + (q + o) % 4), device_id_type=MESH,
        )

    def pair_copy(s):
        return pltpu.make_async_remote_copy(
            src_ref=pair_out.at[s], dst_ref=pair_in.at[s], send_sem=pair_send.at[s], recv_sem=pair_recv.at[s],
            device_id=(me, (c + 4) % NC), device_id_type=MESH,
        )

    def done_copy(o, s):
        return pltpu.make_async_remote_copy(
            src_ref=table.at[s, q], dst_ref=table.at[s, q], send_sem=done_send.at[o - 1, s],
            recv_sem=done_recv.at[o - 1, s], device_id=(me, base + (q + o) % 4), device_id_type=MESH,
        )

    for s in range(2):
        acc[s] = acc[s] + product(s, 1)
        for o in (3, 1, 2):
            part_out[o - 1, s] = acc[s, (q + o) % 4].astype(bf16)
            part_copy(o, s).start()
    for s in range(2):
        total = acc[s, q]
        for o in range(1, 4):
            part_copy(o, s).wait_recv()
            total = total + part_in[o - 1, s].astype(f32)
        acc[s, q] = total
        pair_out[s] = total.astype(bf16)
        pair_copy(s).start()
    for s in range(2):
        pair_copy(s).wait_recv()
        table[s, q] = (acc[s, q] + pair_in[s].astype(f32)).astype(bf16)
        for o in (3, 1, 2):
            done_copy(o, s).start()

    cots[c] = cot_ref[...]
    toks[c] = tok_ref[...]
    for i, copy in enumerate(extra):
        if not 6 <= i < 8:
            copy.wait_recv()
    for s in range(2):
        for o in range(1, 4):
            done_copy(o, s).wait_recv()

    def finish():
        for copy in extra:
            copy.wait_send()
        for b in range(2):
            each(1, CHIPS, lambda o: all_copy(b, o).wait_send())
            each(0, CHIPS, lambda o: core_copy(b, o).wait_send())

        @pl.when(source)
        def _():
            for b in range(2):
                each(1, CHIPS, lambda o: scat_copy(b, (spot + o) % CHIPS, yb).wait_send())

        @pl.when(gives)
        def _():
            for m in range(4):
                half_copy(m).wait_send()

        for s in range(2):
            pair_copy(s).wait_send()
            for o in range(1, 4):
                part_copy(o, s).wait_send()
                done_copy(o, s).wait_send()

    return finish


def shifted_up(value, by, row):
    return jnp.where(row >= by, pltpu.roll(value, by, 0), 0.0)


def shifted_down(value, by, row):
    return jnp.where(row < 8 - by, pltpu.roll(value, 8 - by, 0), 0.0)


def scan_modes(drive_at, out_ref, rates_ref, res_ref, backward):
    row = lax.broadcasted_iota(jnp.int32, (8, 128), 0)
    shifted = shifted_down if backward else shifted_up
    length = 128

    def spread(ref, m):
        return jnp.broadcast_to(ref[m : m + 1, :], (8, 128))

    def at(j):
        j = length - 1 - j if backward else j
        return pl.ds(pl.multiple_of(j * 8, 8), 8)

    decay = [jnp.exp(-spread(rates_ref, m)) for m in range(MODES)]

    def ends(j, state):
        drive = drive_at(at(j))
        return tuple(decay[m] * state[m] + drive for m in range(MODES))

    zero = jnp.zeros((8, 128), jnp.float32)
    state = lax.fori_loop(0, length, ends, (zero,) * MODES, unroll=4)
    entering = []
    for m in range(MODES):
        rate = spread(rates_ref, m)
        whole = state[m]
        for by in (1, 2, 4):
            whole = whole + jnp.exp(-rate * float(length * by)) * shifted(whole, by, row)
        entering.append(shifted(whole, 1, row))
    weight = [spread(res_ref, m) for m in range(MODES)]

    def outs(j, state):
        where = at(j)
        drive = drive_at(where)
        state = tuple(decay[m] * state[m] + drive for m in range(MODES))
        terms = [weight[m] * state[m] for m in range(MODES)]
        while len(terms) > 1:
            terms = [a + b for a, b in zip(terms[::2], terms[1::2])]
        out_ref[where, :] = terms[0]
        return state

    lax.fori_loop(0, length, outs, tuple(entering), unroll=4)


def mix(
    table, toks, cots, taps_ref, rates_ref, res_ref,
    mixed_ref, lhs_ref,
    z, filt, cot, drive, glong, lo, gd, gz,
):
    c = lax.axis_index("ctx")
    halo = 8
    row = lax.broadcasted_iota(jnp.int32, (8, 128), 0)
    lane = lax.broadcasted_iota(jnp.int32, (8, VOCAB), 1)

    for s in range(NC):
        cot[pl.ds(s, 128, stride=8), :] = cots[s].astype(jnp.float32)

    ids = jnp.concatenate([toks[i] for i in range(NC)], axis=0)
    whole = table[...].reshape(VOCAB, 384)

    def pick(i, ids):
        rows = []
        for j in range(0, 16, 2):
            two = [jnp.where(ids[:, j + e : j + e + 1] == lane, 1.0, 0.0) for e in range(2)]
            rows.append(jnp.concatenate(two, axis=0).astype(jnp.bfloat16))
        hot = jnp.concatenate(rows, axis=0)
        found = jnp.dot(hot, whole, preferred_element_type=jnp.float32)
        start = pl.ds(pl.multiple_of((halo + i * 16) * 8, 128 // 2), 128)
        for g in range(3):
            z[g, start, :] = found[:, g * 128 : (g + 1) * 128]
        return pltpu.roll(ids, 112, 1)

    lax.fori_loop(0, 8, pick, ids)
    for g in range(3):
        for d in range(1, TAPS):
            z[g, pl.ds((halo - d) * 8, 8), :] = shifted_up(z[g, pl.ds((halo + 128 - d) * 8, 8), :], 1, row)

    def filter_rows(i, _):
        base = i * 64
        for g in range(3):
            value = None
            for d in range(TAPS):
                term = taps_ref[g, d : d + 1, :] * z[g, pl.ds(pl.multiple_of(base + (halo - d) * 8, 8), 64), :]
                value = term if value is None else value + term
            filt[g, pl.ds(pl.multiple_of(base, 64), 64), :] = value
        here = pl.ds(pl.multiple_of(base, 64), 64)
        drive[here, :] = filt[1, here, :] * filt[2, here, :]
        glong[here, :] = cot[here, :] * filt[0, here, :]
        return 0

    lax.fori_loop(0, 16, filter_rows, 0)
    scan_modes(lambda at: drive[at, :], lo, rates_ref, res_ref, False)
    scan_modes(lambda at: glong[at, :], gd, rates_ref, res_ref, True)

    def grads(i, _):
        here = pl.ds(pl.multiple_of(i * 64, 64), 64)
        long_out, grad_drive = lo[here, :], gd[here, :]
        z[0, here, :] = cot[here, :] * long_out
        z[1, here, :] = grad_drive * filt[2, here, :]
        z[2, here, :] = grad_drive * filt[1, here, :]
        lo[here, :] = filt[0, here, :] * long_out
        return 0

    lax.fori_loop(0, 16, grads, 0)
    mixed_ref[...] = lo[pl.ds(c, 128, stride=8), :].astype(jnp.bfloat16)
    for g in range(3):
        for d in range(TAPS - 1):
            z[g, pl.ds((128 + d) * 8, 8), :] = shifted_down(z[g, pl.ds(d * 8, 8), :], 1, row)

    def adjoint_rows(i, _):
        base = i * 64
        for g in range(3):
            value = None
            for d in range(TAPS):
                term = taps_ref[g, d : d + 1, :] * z[g, pl.ds(pl.multiple_of(base + d * 8, 8), 64), :]
                value = term if value is None else value + term
            gz[g, pl.ds(pl.multiple_of(base, 64), 64), :] = value
        return 0

    lax.fori_loop(0, 16, adjoint_rows, 0)
    for s in range(NC):
        start = (c + s) % NC
        for g in range(3):
            lhs_ref[pl.ds(s * 128, 128), pl.ds(g * 128, 128)] = gz[g, pl.ds(start, 128, stride=8), :].astype(jnp.bfloat16)


SPOT = {0: (0, 0), 1: (1, 0), 2: (0, 1), 3: (1, 1), 4: (2, 1), 5: (3, 1), 6: (2, 0), 7: (3, 0)}


def whole_kernel(
    embed_ref, w_hbm, tok_ref, cot_ref, taps_ref, rates_ref, res_ref,
    mixed_ref, pair_ref,
    w_ref, w_sem,
    emb, stage, acc, part_out, part_in, pair_out, pair_in, table, toks, cots,
    local_sem, half_send, half_recv, scat_send, scat_recv, all_send, all_recv, swap_send, swap_recv,
    part_send, part_recv, pair_send, pair_recv, done_send, done_recv,
    cot_send, cot_recv, tok_send, tok_recv,
    z, filt, cot, drive, glong, lo, gd, gz, lhs_ref,
    own, core_out, core_in, rest_out, rest_in, last_out, last_in,
    core_send, core_recv, rest_send, rest_recv, last_send, last_recv,
):
    w_copy = pltpu.make_async_copy(w_hbm, w_ref, w_sem)
    w_copy.start()
    f32, bf16 = jnp.float32, jnp.bfloat16
    x, y, h, k, c = place()
    x0, y0 = c // 2, (c % 2) * 2
    dx, dy = (x - x0 + 4) % 4, (y - y0 + 4) % 4
    partner = (flat(x, y, h, 1 - k), c)
    spot = x * 4 + y

    def chip(o):
        i = (spot + o) % CHIPS
        return i // 4, i % 4

    yb = jnp.where(jnp.logical_or(dy == 1, dy == 2), 1, 0)
    far = jnp.where(dy >= 2, 1, 0)
    step = jnp.where(dx < 2, dx + 2 * far, dx + 4 - 2 * far)
    owner = [(flat(x0, y0 + yb, e, k), (c + step) % NC) for e in range(2)]
    from_c = 2 * x + y // 2
    back = (c - from_c + NC) % NC
    back_x = jnp.where(back < 4, back % 2, 2 + back % 2)
    back_far = jnp.where(back < 4, back // 2, 3 - back // 2)
    back_y = jnp.where(y % 2 == 0, 3 * back_far, 1 + back_far)
    givers = [(flat(x + back_x, (y // 2) * 2 + back_y, e, k), from_c) for e in range(2)]
    loop = jnp.logical_and(dx == 0, dy < 2)
    foreign = [jnp.logical_not(jnp.logical_and(loop, h == e)) for e in range(2)]
    finish = build_table(
        [(givers[e], foreign[e]) for e in range(2)], 2 - loop.astype(jnp.int32),
        embed_ref, w_ref, w_copy, tok_ref, cot_ref,
        emb, stage, acc, part_out, part_in, pair_out, pair_in, table, toks, cots,
        local_sem, half_send, half_recv, scat_send, scat_recv, all_send, all_recv, swap_send, swap_recv,
        part_send, part_recv, pair_send, pair_recv, done_send, done_recv,
        cot_send, cot_recv, tok_send, tok_recv,
    )
    mix(
        table, toks, cots, taps_ref, rates_ref, res_ref, mixed_ref, lhs_ref,
        z, filt, cot, drive, glong, lo, gd, gz,
    )

    def core_copy(e, a):
        return pltpu.make_async_remote_copy(
            src_ref=core_out.at[e, pl.ds(a * 4, 4)], dst_ref=core_in.at[e, pl.ds(a * 4, 4)],
            send_sem=core_send.at[e, a], recv_sem=core_recv.at[e, a], device_id=partner, device_id_type=MESH,
        )

    def slot(o):
        cx, cy = chip(o)
        return ((cx - x0 + 4) % 4) * 4 + (cy - y0 + 4) % 4

    def rest_copy(e, o):
        return pltpu.make_async_remote_copy(
            src_ref=rest_out.at[e, o], dst_ref=rest_in.at[e, o],
            send_sem=rest_send.at[e, o], recv_sem=rest_recv.at[e, o],
            device_id=(flat(*chip(o), h, k), c), device_id_type=MESH,
        )

    def last_copy(e):
        return pltpu.make_async_remote_copy(
            src_ref=last_out.at[e], dst_ref=last_in.at[h],
            send_sem=last_send.at[e], recv_sem=last_recv.at[h], device_id=owner[e], device_id_type=MESH,
        )

    def last_wait(e):
        pltpu.make_async_remote_copy(
            src_ref=last_out.at[e], dst_ref=last_in.at[e],
            send_sem=last_send.at[e], recv_sem=last_recv.at[e], device_id=partner, device_id_type=MESH,
        ).wait_recv()

    def tile(e, kk, store):
        starts = [pl.multiple_of(r * 512 + e * 256 + kk * 128, 128) for r in range(2)]
        right = jnp.concatenate(
            [jnp.concatenate([w_ref[g, pl.ds(at, 128), :] for g in range(3)], axis=1) for at in starts], axis=0
        )
        out = lax.dot_general(lhs_ref[...], right, (((1,), (1,)), ((), ())), preferred_element_type=f32)
        for s in range(NC):
            sx, sfar = SPOT[s]
            for r in range(2):
                sy = 3 * sfar if r == 0 else 1 + sfar
                store(e, sx * 4 + sy, out[s * 128 : (s + 1) * 128, r * 128 : (r + 1) * 128])

    def to_core(e, a, value):
        core_out[e, a] = value.astype(bf16)

    def to_own(e, a, value):
        own[e, a] = value

    for e in range(2):
        tile(e, 1 - k, to_core)
        for a in range(4):
            core_copy(e, a).start()
    for e in range(2):
        tile(e, k, to_own)
        for a in range(4):
            core_copy(e, a).wait_recv()

        def give(o, _):
            a = slot(o)
            rest_out[e, o] = (own[e, a] + core_in[e, a].astype(f32)).astype(bf16)
            rest_copy(e, o).start()
            return 0

        lax.fori_loop(1, CHIPS, give, 0)
    for e in range(2):

        def take(o, both):
            rest_copy(e, o).wait_recv()
            return both + rest_in[e, o].astype(f32)

        home = dx * 4 + dy
        both = lax.fori_loop(1, CHIPS, take, own[e, home] + core_in[e, home].astype(f32))
        last_out[e] = both.astype(bf16)

        @pl.when(foreign[e])
        def _():
            last_copy(e).start()

        @pl.when(jnp.logical_not(foreign[e]))
        def _():
            last_in[e] = last_out[e]

    for e in range(2):

        @pl.when(foreign[e])
        def _():
            last_wait(e)

    pair_ref[...] = last_in[...]
    finish()
    for e in range(2):
        for a in range(4):
            core_copy(e, a).wait_send()

        def sent(o, _):
            rest_copy(e, o).wait_send()
            return 0

        lax.fori_loop(1, CHIPS, sent, 0)

        @pl.when(foreign[e])
        def _():
            last_copy(e).wait_send()


def last_kernel(mixed_ref, pair_ref, out_ref, grad_ref):
    out_ref[...] = mixed_ref[...]
    grad_ref[...] = (pair_ref[0].astype(jnp.float32) + pair_ref[1].astype(jnp.float32)).astype(jnp.bfloat16)


def on_device(token_ids, embed, w_in, taps, rates, residues, cotangent):
    bf16, f32, i32 = jnp.bfloat16, jnp.float32, jnp.int32
    dma = pltpu.SemaphoreType.DMA
    w = w_in.transpose(1, 0, 2)
    taps = taps.transpose(1, 0, 2)
    wide = pltpu.VMEM((1024, 128), f32)
    mixed, pair = pl.pallas_call(
        whole_kernel,
        out_shape=(
            jax.ShapeDtypeStruct((128, 128), bf16),
            jax.ShapeDtypeStruct((2, 128, 128), bf16),
        ),
        in_specs=[ANY, ANY] + [VMEM] * 5,
        out_specs=(VMEM, VMEM),
        scratch_shapes=[
            pltpu.VMEM((3, 1024, 128), bf16), dma,
            pltpu.VMEM((CHIPS, 2, 2, 2, PIECE, 128), bf16),
            pltpu.VMEM((VOCAB, 128), bf16),
            pltpu.VMEM((2, 4, 64, 384), f32),
            pltpu.VMEM((3, 2, 64, 384), bf16), pltpu.VMEM((3, 2, 64, 384), bf16),
            pltpu.VMEM((2, 64, 384), bf16), pltpu.VMEM((2, 64, 384), bf16),
            pltpu.VMEM((2, 4, 64, 384), bf16),
            pltpu.VMEM((NC, 1, 128), i32),
            pltpu.VMEM((NC, 128, 128), bf16),
            dma((2,)), dma((4,)), dma((4,)), dma((2, CHIPS)), dma((2, 2)),
            dma((2, CHIPS)), dma((2, CHIPS)), dma((2, CHIPS)), dma((2, CHIPS)),
            dma((3, 2)), dma((3, 2)), dma((2,)), dma((2,)), dma((3, 2)), dma((3, 2)),
            dma((NC - 1,)), dma((NC - 1,)), dma((NC - 1,)), dma((NC - 1,)),
            pltpu.VMEM((3, 136 * 8, 128), f32), pltpu.VMEM((3, 1024, 128), f32),
            wide, wide, wide, wide, wide,
            pltpu.VMEM((3, 1024, 128), f32), pltpu.VMEM((1024, 384), bf16),
            pltpu.VMEM((2, CHIPS, 128, 128), f32),
            pltpu.VMEM((2, CHIPS, 128, 128), bf16), pltpu.VMEM((2, CHIPS, 128, 128), bf16),
            pltpu.VMEM((2, CHIPS, 128, 128), bf16), pltpu.VMEM((2, CHIPS, 128, 128), bf16),
            pltpu.VMEM((2, 128, 128), bf16), pltpu.VMEM((2, 128, 128), bf16),
            dma((2, 4)), dma((2, 4)), dma((2, CHIPS)), dma((2, CHIPS)), dma((2,)), dma((2,)),
        ],
        compiler_params=pltpu.CompilerParams(collective_id=0, has_side_effects=True, vmem_limit_bytes=LIMIT),
        name="whole",
    )(embed, w, token_ids.reshape(1, 128), cotangent, taps, rates, residues)
    return pl.pallas_call(
        last_kernel,
        out_shape=(jax.ShapeDtypeStruct((128, 128), bf16), jax.ShapeDtypeStruct((128, 128), bf16)),
        in_specs=[VMEM, VMEM],
        out_specs=(VMEM, VMEM),
        name="last",
    )(mixed, pair)


def solution(mesh):
    in_specs = (
        P("ctx"),
        P(None, "fsdp"),
        P("ctx", None, "fsdp"),
        P(None, None, "fsdp"),
        P(None, "fsdp"),
        P(None, "fsdp"),
        P("ctx", "fsdp"),
    )
    out_specs = (P("ctx", "fsdp"), P("ctx", "fsdp"))
    return jax.shard_map(on_device, mesh=mesh, in_specs=in_specs, out_specs=out_specs, check_vma=False)
```

```python
import functools

import jax
import jax.numpy as jnp
from jax import lax
from jax.experimental import pallas as pl
from jax.experimental.pallas import tpu as pltpu
from jax.sharding import PartitionSpec as P

MESH = pl.DeviceIdType.MESH
VMEM = pl.BlockSpec(memory_space=pltpu.VMEM)
ANY = pl.BlockSpec(memory_space=pl.ANY)
LIMIT = 60 * 1024 * 1024
NC = 8
CHIPS = 16
PIECE = 32
FAR_FIRST = (10, 6, 14, 9, 11, 2, 8, 5, 7, 13, 15, 1, 3, 4, 12)
VOCAB = 512
MODES = 16
TAPS = 7


def place():
    f = lax.axis_index("fsdp")
    c = lax.axis_index("ctx")
    return lax.div(f, 16), lax.rem(lax.div(f, 4), 4), lax.rem(lax.div(f, 2), 2), lax.rem(f, 2), c


def flat(x, y, h, k):
    return x * 16 + y * 4 + h * 2 + k


def hail(devices):
    barrier = pltpu.get_barrier_semaphore()
    for device, wanted in devices:
        if wanted is None:
            pl.semaphore_signal(barrier, inc=1, device_id=device, device_id_type=MESH)
        else:

            @pl.when(wanted)
            def _():
                pl.semaphore_signal(barrier, inc=1, device_id=device, device_id_type=MESH)


def greet(devices, count):
    hail(devices)
    pl.semaphore_wait(pltpu.get_barrier_semaphore(), count)


def build_table(
    friends, count, embed_ref, w_ref, w_copy, tok_ref, cot_ref,
    emb, acc, part_out, part_in, pair_out, pair_in, table, toks, cots,
    local_sem, scat_send, scat_recv, all_send, all_recv, core_send, core_recv,
    part_send, part_recv, pair_send, pair_recv, done_send, done_recv,
    cot_send, cot_recv, tok_send, tok_recv,
):
    f32, bf16 = jnp.float32, jnp.bfloat16
    x, y, h, k, c = place()
    me = flat(x, y, h, k)
    spot = x * 4 + y
    lane = h * 2 + k
    mine = 2 * x + lax.div(y, 2)
    yb = lax.rem(y, 2)
    edge = jnp.where(mine < NC // 2, NC - 1, 0)
    source = mine == c
    gives = c == edge
    partner = flat(x, y, h, 1 - k)
    q = lax.rem(c, 4)
    base = c - q
    across = lax.rem(c + 4, NC)
    group = [(me, base + lax.rem(q + o, 4)) for o in range(1, 4)]
    first = flat(lax.div(c, 2), 2 * lax.rem(c, 2), 1 - h, k)
    givers = [(first + 4 * row, jnp.where(c < NC // 2, NC - 1, 0)) for row in range(2)]

    def chip(i):
        return i * 4 + lane

    def beside(o):
        return lax.rem(spot + o, CHIPS)

    greet(
        friends
        + [(d, None) for d in givers + [(me, across)] + group[::-1]]
        + [((chip(beside(o)), c), None) for o in FAR_FIRST]
        + [((partner, c), None)],
        CHIPS + 4 + CHIPS * gives.astype(jnp.int32) + count,
    )

    def side(b):
        return h if b == 0 else 1 - h

    def scat_copy(b, i, row):
        rows = pl.ds(pl.multiple_of(i * PIECE, PIECE), PIECE)
        return pltpu.make_async_remote_copy(
            src_ref=embed_ref.at[rows], dst_ref=emb.at[i, side(b), k, row],
            send_sem=scat_send.at[b, i], recv_sem=scat_recv.at[b, row], device_id=(chip(i), c), device_id_type=MESH,
        )

    def give_copy(i):
        rows = pl.ds(i * PIECE, PIECE)
        return pltpu.make_async_remote_copy(
            src_ref=embed_ref.at[rows], dst_ref=emb.at[i, h, k, yb], send_sem=scat_send.at[1, i],
            recv_sem=scat_recv.at[1, yb], device_id=(i * 4 + (1 - h) * 2 + k, mine), device_id_type=MESH,
        )

    own_rows = pl.ds(pl.multiple_of(spot * PIECE, PIECE), PIECE)
    own_copy = pltpu.make_async_copy(embed_ref.at[own_rows], emb.at[spot, h, k, yb], local_sem)

    def all_copy(b, o):
        return pltpu.make_async_remote_copy(
            src_ref=emb.at[spot, side(b), k], dst_ref=emb.at[spot, side(b), k], send_sem=all_send.at[b, o],
            recv_sem=all_recv.at[b, o], device_id=(chip(beside(o)), c), device_id_type=MESH,
        )

    def core_copy(b, o):
        i = lax.rem(spot + CHIPS - o, CHIPS)
        return pltpu.make_async_remote_copy(
            src_ref=emb.at[i, side(b), k], dst_ref=emb.at[i, side(b), k], send_sem=core_send.at[b, o],
            recv_sem=core_recv.at[b, o], device_id=(partner, c), device_id_type=MESH,
        )

    def each(first, last, body, unroll=1):
        def step(i, _):
            body(i)
            return 0

        lax.fori_loop(first, last, step, 0, unroll=unroll)

    @pl.when(gives)
    def _():
        for i in range(CHIPS):
            give_copy(i).start()

    @pl.when(source)
    def _():
        own_copy.start()
        each(1, CHIPS, lambda o: scat_copy(0, beside(o), yb).start(), 5)
        own_copy.wait()

    extra = []

    def spread(index, target, sem):
        for src, dst, ss, rs in ((cot_ref, cots, cot_send, cot_recv), (tok_ref, toks, tok_send, tok_recv)):
            copy = pltpu.make_async_remote_copy(
                src_ref=src if sem < 4 else dst.at[index], dst_ref=dst.at[index], send_sem=ss.at[sem],
                recv_sem=rs.at[sem], device_id=target, device_id_type=MESH,
            )
            copy.start()
            extra.append(copy)

    def share(b):
        for row in range(2):
            if b == 0:

                @pl.when(jnp.logical_not(jnp.logical_and(source, yb == row)))
                def _():
                    scat_copy(b, spot, row).wait_recv()

            else:
                scat_copy(b, spot, row).wait_recv()

        each(1, CHIPS, lambda o: all_copy(b, o).start(), 5)
        core_copy(b, 0).start()

    def gathered(b, o):
        all_copy(b, o).wait_recv()
        core_copy(b, o).start()

    share(0)

    for o in range(1, 4):
        spread(c, group[o - 1], o - 1)
    spread(c, (me, across), 3)
    share(1)
    each(1, CHIPS, lambda o: gathered(0, o), 5)
    for copy in extra[6:8]:
        copy.wait_recv()
    for o in range(1, 4):
        spread(across, group[o - 1], 3 + o)

    def product(s, b):
        total = None
        hb = side(b)
        for e in range(2):
            left = jnp.concatenate(
                [
                    jnp.concatenate([emb[s * 8 + i, hb, kk, e] for kk in range(2)], axis=1)
                    for i in range(8)
                ],
                axis=0,
            )
            at = pl.ds(pl.multiple_of(e * 512 + hb * 256, 256), 256)
            right = jnp.concatenate([w_ref[g, at, :] for g in range(3)], axis=1)
            part = jnp.dot(left, right, preferred_element_type=f32)
            total = part if total is None else total + part
        return total.reshape(4, 64, 384)

    each(0, CHIPS, lambda o: core_copy(0, o).wait_recv())
    w_copy.wait()
    for s in range(2):
        acc[s] = product(s, 0)
    each(1, CHIPS, lambda o: gathered(1, o), 5)
    each(0, CHIPS, lambda o: core_copy(1, o).wait_recv())

    def part_copy(o, s):
        return pltpu.make_async_remote_copy(
            src_ref=part_out.at[o - 1, s], dst_ref=part_in.at[o - 1, s], send_sem=part_send.at[o - 1, s],
            recv_sem=part_recv.at[o - 1, s], device_id=(me, base + lax.rem(q + o, 4)), device_id_type=MESH,
        )

    def pair_copy(s):
        return pltpu.make_async_remote_copy(
            src_ref=pair_out.at[s], dst_ref=pair_in.at[s], send_sem=pair_send.at[s], recv_sem=pair_recv.at[s],
            device_id=(me, across), device_id_type=MESH,
        )

    def done_copy(o, s):
        return pltpu.make_async_remote_copy(
            src_ref=table.at[s, q], dst_ref=table.at[s, q], send_sem=done_send.at[o - 1, s],
            recv_sem=done_recv.at[o - 1, s], device_id=(me, base + lax.rem(q + o, 4)), device_id_type=MESH,
        )

    for s in range(2):
        acc[s] = acc[s] + product(s, 1)
        for o in (3, 1, 2):
            part_out[o - 1, s] = acc[s, lax.rem(q + o, 4)].astype(bf16)
            part_copy(o, s).start()
    for s in range(2):
        total = acc[s, q]
        for o in range(1, 4):
            part_copy(o, s).wait_recv()
            total = total + part_in[o - 1, s].astype(f32)
        acc[s, q] = total
        pair_out[s] = total.astype(bf16)
        pair_copy(s).start()
    for s in range(2):
        pair_copy(s).wait_recv()
        table[s, q] = (acc[s, q] + pair_in[s].astype(f32)).astype(bf16)
        for o in (3, 1, 2):
            done_copy(o, s).start()

    cots[c] = cot_ref[...]
    toks[c] = tok_ref[...]
    for i, copy in enumerate(extra):
        if not 6 <= i < 8:
            copy.wait_recv()
    for s in range(2):
        for o in range(1, 4):
            done_copy(o, s).wait_recv()

    def finish():
        for copy in extra:
            copy.wait_send()
        for b in range(2):
            each(1, CHIPS, lambda o: all_copy(b, o).wait_send())
            each(0, CHIPS, lambda o: core_copy(b, o).wait_send())

        @pl.when(source)
        def _():
            each(1, CHIPS, lambda o: scat_copy(0, beside(o), yb).wait_send())

        @pl.when(gives)
        def _():
            for i in range(CHIPS):
                give_copy(i).wait_send()

        for s in range(2):
            pair_copy(s).wait_send()
            for o in range(1, 4):
                part_copy(o, s).wait_send()
                done_copy(o, s).wait_send()

    return finish


def shifted_up(value, by, row):
    return jnp.where(row >= by, pltpu.roll(value, by, 0), 0.0)


def shifted_down(value, by, row):
    return jnp.where(row < 8 - by, pltpu.roll(value, 8 - by, 0), 0.0)


def scan_modes(drive_at, out_ref, rates_ref, res_ref, backward):
    row = lax.broadcasted_iota(jnp.int32, (8, 128), 0)
    shifted = shifted_down if backward else shifted_up
    length = 128

    def spread(ref, m):
        return jnp.broadcast_to(ref[m : m + 1, :], (8, 128))

    def at(j):
        j = length - 1 - j if backward else j
        return pl.ds(pl.multiple_of(j * 8, 8), 8)

    decay = [jnp.exp(-spread(rates_ref, m)) for m in range(MODES)]

    def ends(j, state):
        drive = drive_at(at(j))
        return tuple(decay[m] * state[m] + drive for m in range(MODES))

    zero = jnp.zeros((8, 128), jnp.float32)
    state = lax.fori_loop(0, length, ends, (zero,) * MODES, unroll=4)
    entering = []
    for m in range(MODES):
        rate = spread(rates_ref, m)
        whole = state[m]
        for by in (1, 2, 4):
            whole = whole + jnp.exp(-rate * float(length * by)) * shifted(whole, by, row)
        entering.append(shifted(whole, 1, row))
    weight = [spread(res_ref, m) for m in range(MODES)]

    def outs(j, state):
        where = at(j)
        drive = drive_at(where)
        state = tuple(decay[m] * state[m] + drive for m in range(MODES))
        terms = [weight[m] * state[m] for m in range(MODES)]
        while len(terms) > 1:
            terms = [a + b for a, b in zip(terms[::2], terms[1::2])]
        out_ref[where, :] = terms[0]
        return state

    lax.fori_loop(0, length, outs, tuple(entering), unroll=4)


def mix(
    table, toks, cots, taps_ref, rates_ref, res_ref,
    mixed_ref, lhs_ref,
    z, filt, cot, drive, glong, lo, gd, gz,
):
    c = lax.axis_index("ctx")
    halo = 8
    row = lax.broadcasted_iota(jnp.int32, (8, 128), 0)
    lane = lax.broadcasted_iota(jnp.int32, (8, VOCAB), 1)

    for s in range(NC):
        cot[pl.ds(s, 128, stride=8), :] = cots[s].astype(jnp.float32)

    ids = jnp.concatenate([toks[i] for i in range(NC)], axis=0)
    whole = table[...].reshape(VOCAB, 384)

    def pick(i, ids):
        rows = []
        for j in range(0, 16, 2):
            two = [jnp.where(ids[:, j + e : j + e + 1] == lane, 1.0, 0.0) for e in range(2)]
            rows.append(jnp.concatenate(two, axis=0).astype(jnp.bfloat16))
        hot = jnp.concatenate(rows, axis=0)
        found = jnp.dot(hot, whole, preferred_element_type=jnp.float32)
        start = pl.ds(pl.multiple_of((halo + i * 16) * 8, 128 // 2), 128)
        for g in range(3):
            z[g, start, :] = found[:, g * 128 : (g + 1) * 128]
        return pltpu.roll(ids, 112, 1)

    lax.fori_loop(0, 8, pick, ids)
    for g in range(3):
        for d in range(1, TAPS):
            z[g, pl.ds((halo - d) * 8, 8), :] = shifted_up(z[g, pl.ds((halo + 128 - d) * 8, 8), :], 1, row)

    def filter_rows(i, _):
        base = i * 64
        for g in range(3):
            value = None
            for d in range(TAPS):
                term = taps_ref[g, d : d + 1, :] * z[g, pl.ds(pl.multiple_of(base + (halo - d) * 8, 8), 64), :]
                value = term if value is None else value + term
            filt[g, pl.ds(pl.multiple_of(base, 64), 64), :] = value
        here = pl.ds(pl.multiple_of(base, 64), 64)
        drive[here, :] = filt[1, here, :] * filt[2, here, :]
        glong[here, :] = cot[here, :] * filt[0, here, :]
        return 0

    lax.fori_loop(0, 16, filter_rows, 0)
    scan_modes(lambda at: drive[at, :], lo, rates_ref, res_ref, False)
    scan_modes(lambda at: glong[at, :], gd, rates_ref, res_ref, True)

    def grads(i, _):
        here = pl.ds(pl.multiple_of(i * 64, 64), 64)
        long_out, grad_drive = lo[here, :], gd[here, :]
        z[0, here, :] = cot[here, :] * long_out
        z[1, here, :] = grad_drive * filt[2, here, :]
        z[2, here, :] = grad_drive * filt[1, here, :]
        lo[here, :] = filt[0, here, :] * long_out
        return 0

    lax.fori_loop(0, 16, grads, 0)
    mixed_ref[...] = lo[pl.ds(c, 128, stride=8), :].astype(jnp.bfloat16)
    for g in range(3):
        for d in range(TAPS - 1):
            z[g, pl.ds((128 + d) * 8, 8), :] = shifted_down(z[g, pl.ds(d * 8, 8), :], 1, row)

    def adjoint_rows(i, _):
        base = i * 64
        for g in range(3):
            value = None
            for d in range(TAPS):
                term = taps_ref[g, d : d + 1, :] * z[g, pl.ds(pl.multiple_of(base + d * 8, 8), 64), :]
                value = term if value is None else value + term
            gz[g, pl.ds(pl.multiple_of(base, 64), 64), :] = value
        return 0

    lax.fori_loop(0, 16, adjoint_rows, 0)
    for s in range(NC):
        start = lax.rem(c + s, NC)
        for g in range(3):
            lhs_ref[pl.ds(s * 128, 128), pl.ds(g * 128, 128)] = gz[g, pl.ds(start, 128, stride=8), :].astype(jnp.bfloat16)


SPOT = {0: (0, 0), 1: (1, 0), 2: (0, 1), 3: (1, 1), 4: (2, 1), 5: (3, 1), 6: (2, 0), 7: (3, 0)}


def whole_kernel(
    embed_ref, w_hbm, tok_ref, cot_ref, taps_ref, rates_ref, res_ref,
    mixed_ref, pair_ref,
    w_ref, w_sem,
    emb, acc, part_out, part_in, pair_out, pair_in, table, toks, cots,
    local_sem, scat_send, scat_recv, all_send, all_recv, swap_send, swap_recv,
    part_send, part_recv, pair_send, pair_recv, done_send, done_recv,
    cot_send, cot_recv, tok_send, tok_recv,
    z, filt, cot, drive, glong, lo, gd, gz, lhs_ref,
    own, core_out, core_in, rest_out, rest_in, last_out, last_in,
    core_send, core_recv, rest_send, rest_recv, last_send, last_recv,
):
    w_copy = pltpu.make_async_copy(w_hbm, w_ref, w_sem)
    w_copy.start()
    f32, bf16 = jnp.float32, jnp.bfloat16
    x, y, h, k, c = place()
    x0, y0 = lax.div(c, 2), lax.rem(c, 2) * 2
    dx, dy = lax.rem(x - x0 + 4, 4), lax.rem(y - y0 + 4, 4)
    partner = (flat(x, y, h, 1 - k), c)
    spot = x * 4 + y
    lane = h * 2 + k

    def beside(o):
        return lax.rem(spot + o, CHIPS)

    yb = jnp.where(jnp.logical_or(dy == 1, dy == 2), 1, 0)
    far = jnp.where(dy >= 2, 1, 0)
    step = jnp.where(dx < 2, dx + 2 * far, dx + 4 - 2 * far)
    owner = [(flat(x0, y0 + yb, e, k), lax.rem(c + step, NC)) for e in range(2)]
    from_c = 2 * x + lax.div(y, 2)
    back = lax.rem(c - from_c + NC, NC)
    back_x = jnp.where(back < 4, lax.rem(back, 2), 2 + lax.rem(back, 2))
    back_far = jnp.where(back < 4, lax.div(back, 2), 3 - lax.div(back, 2))
    back_y = jnp.where(lax.rem(y, 2) == 0, 3 * back_far, 1 + back_far)
    giver_x, giver_y = lax.rem(x + back_x, 4), lax.rem(lax.div(y, 2) * 2 + back_y, 4)
    givers = [(flat(giver_x, giver_y, e, k), from_c) for e in range(2)]
    loop = jnp.logical_and(dx == 0, dy < 2)
    foreign = [jnp.logical_not(jnp.logical_and(loop, h == e)) for e in range(2)]
    finish = build_table(
        [(givers[e], foreign[e]) for e in range(2)], 2 - loop.astype(jnp.int32),
        embed_ref, w_ref, w_copy, tok_ref, cot_ref,
        emb, acc, part_out, part_in, pair_out, pair_in, table, toks, cots,
        local_sem, scat_send, scat_recv, all_send, all_recv, swap_send, swap_recv,
        part_send, part_recv, pair_send, pair_recv, done_send, done_recv,
        cot_send, cot_recv, tok_send, tok_recv,
    )
    mix(
        table, toks, cots, taps_ref, rates_ref, res_ref, mixed_ref, lhs_ref,
        z, filt, cot, drive, glong, lo, gd, gz,
    )

    def core_copy(e, a):
        return pltpu.make_async_remote_copy(
            src_ref=core_out.at[e, pl.ds(a * 4, 4)], dst_ref=core_in.at[e, pl.ds(a * 4, 4)],
            send_sem=core_send.at[e, a], recv_sem=core_recv.at[e, a], device_id=partner, device_id_type=MESH,
        )

    def slot(o):
        i = beside(o)
        return lax.rem(lax.div(i, 4) + 4 - x0, 4) * 4 + lax.rem(lax.rem(i, 4) + 4 - y0, 4)

    def rest_copy(e, o):
        return pltpu.make_async_remote_copy(
            src_ref=rest_out.at[e, o], dst_ref=rest_in.at[e, o],
            send_sem=rest_send.at[e, o], recv_sem=rest_recv.at[e, o],
            device_id=(beside(o) * 4 + lane, c), device_id_type=MESH,
        )

    def last_copy(e):
        return pltpu.make_async_remote_copy(
            src_ref=last_out.at[e], dst_ref=last_in.at[h],
            send_sem=last_send.at[e], recv_sem=last_recv.at[h], device_id=owner[e], device_id_type=MESH,
        )

    def last_wait(e):
        pltpu.make_async_remote_copy(
            src_ref=last_out.at[e], dst_ref=last_in.at[e],
            send_sem=last_send.at[e], recv_sem=last_recv.at[e], device_id=partner, device_id_type=MESH,
        ).wait_recv()

    def tile(e, kk, store):
        starts = [pl.multiple_of(r * 512 + e * 256 + kk * 128, 128) for r in range(2)]
        right = jnp.concatenate(
            [jnp.concatenate([w_ref[g, pl.ds(at, 128), :] for g in range(3)], axis=1) for at in starts], axis=0
        )
        out = lax.dot_general(lhs_ref[...], right, (((1,), (1,)), ((), ())), preferred_element_type=f32)
        for s in range(NC):
            sx, sfar = SPOT[s]
            for r in range(2):
                sy = 3 * sfar if r == 0 else 1 + sfar
                store(e, sx * 4 + sy, out[s * 128 : (s + 1) * 128, r * 128 : (r + 1) * 128])

    def to_core(e, a, value):
        core_out[e, a] = value.astype(bf16)

    def to_own(e, a, value):
        own[e, a] = value

    for e in range(2):
        tile(e, 1 - k, to_core)
        for a in range(4):
            core_copy(e, a).start()
    for e in range(2):
        tile(e, k, to_own)
        for a in range(4):
            core_copy(e, a).wait_recv()

        def give(o, _):
            a = slot(o)
            rest_out[e, o] = (own[e, a] + core_in[e, a].astype(f32)).astype(bf16)
            rest_copy(e, o).start()
            return 0

        lax.fori_loop(1, CHIPS, give, 0, unroll=3)
    for e in range(2):

        def take(o, both):
            rest_copy(e, o).wait_recv()
            return both + rest_in[e, o].astype(f32)

        home = dx * 4 + dy
        both = lax.fori_loop(1, CHIPS, take, own[e, home] + core_in[e, home].astype(f32), unroll=3)
        last_out[e] = both.astype(bf16)

        @pl.when(foreign[e])
        def _():
            last_copy(e).start()

        @pl.when(jnp.logical_not(foreign[e]))
        def _():
            last_in[e] = last_out[e]

    for e in range(2):

        @pl.when(foreign[e])
        def _():
            last_wait(e)

    pair_ref[...] = last_in[...]
    finish()
    for e in range(2):
        for a in range(4):
            core_copy(e, a).wait_send()

        def sent(o, _):
            rest_copy(e, o).wait_send()
            return 0

        lax.fori_loop(1, CHIPS, sent, 0)

        @pl.when(foreign[e])
        def _():
            last_copy(e).wait_send()


def last_kernel(mixed_ref, pair_ref, out_ref, grad_ref):
    out_ref[...] = mixed_ref[...]
    grad_ref[...] = (pair_ref[0].astype(jnp.float32) + pair_ref[1].astype(jnp.float32)).astype(jnp.bfloat16)


def on_device(token_ids, embed, w_in, taps, rates, residues, cotangent):
    bf16, f32, i32 = jnp.bfloat16, jnp.float32, jnp.int32
    dma = pltpu.SemaphoreType.DMA
    w = w_in.transpose(1, 0, 2)
    taps = taps.transpose(1, 0, 2)
    wide = pltpu.VMEM((1024, 128), f32)
    mixed, pair = pl.pallas_call(
        whole_kernel,
        out_shape=(
            jax.ShapeDtypeStruct((128, 128), bf16),
            jax.ShapeDtypeStruct((2, 128, 128), bf16),
        ),
        in_specs=[ANY, ANY] + [VMEM] * 5,
        out_specs=(VMEM, VMEM),
        scratch_shapes=[
            pltpu.VMEM((3, 1024, 128), bf16), dma,
            pltpu.VMEM((CHIPS, 2, 2, 2, PIECE, 128), bf16),
            pltpu.VMEM((2, 4, 64, 384), f32),
            pltpu.VMEM((3, 2, 64, 384), bf16), pltpu.VMEM((3, 2, 64, 384), bf16),
            pltpu.VMEM((2, 64, 384), bf16), pltpu.VMEM((2, 64, 384), bf16),
            pltpu.VMEM((2, 4, 64, 384), bf16),
            pltpu.VMEM((NC, 1, 128), i32),
            pltpu.VMEM((NC, 128, 128), bf16),
            dma, dma((2, CHIPS)), dma((2, 2)),
            dma((2, CHIPS)), dma((2, CHIPS)), dma((2, CHIPS)), dma((2, CHIPS)),
            dma((3, 2)), dma((3, 2)), dma((2,)), dma((2,)), dma((3, 2)), dma((3, 2)),
            dma((NC - 1,)), dma((NC - 1,)), dma((NC - 1,)), dma((NC - 1,)),
            pltpu.VMEM((3, 136 * 8, 128), f32), pltpu.VMEM((3, 1024, 128), f32),
            wide, wide, wide, wide, wide,
            pltpu.VMEM((3, 1024, 128), f32), pltpu.VMEM((1024, 384), bf16),
            pltpu.VMEM((2, CHIPS, 128, 128), f32),
            pltpu.VMEM((2, CHIPS, 128, 128), bf16), pltpu.VMEM((2, CHIPS, 128, 128), bf16),
            pltpu.VMEM((2, CHIPS, 128, 128), bf16), pltpu.VMEM((2, CHIPS, 128, 128), bf16),
            pltpu.VMEM((2, 128, 128), bf16), pltpu.VMEM((2, 128, 128), bf16),
            dma((2, 4)), dma((2, 4)), dma((2, CHIPS)), dma((2, CHIPS)), dma((2,)), dma((2,)),
        ],
        compiler_params=pltpu.CompilerParams(collective_id=0, has_side_effects=True, vmem_limit_bytes=LIMIT),
        name="whole",
    )(embed, w, token_ids.reshape(1, 128), cotangent, taps, rates, residues)
    return pl.pallas_call(
        last_kernel,
        out_shape=(jax.ShapeDtypeStruct((128, 128), bf16), jax.ShapeDtypeStruct((128, 128), bf16)),
        in_specs=[VMEM, VMEM],
        out_specs=(VMEM, VMEM),
        name="last",
    )(mixed, pair)


def solution(mesh):
    in_specs = (
        P("ctx"),
        P(None, "fsdp"),
        P("ctx", None, "fsdp"),
        P(None, None, "fsdp"),
        P(None, "fsdp"),
        P(None, "fsdp"),
        P("ctx", "fsdp"),
    )
    out_specs = (P("ctx", "fsdp"), P("ctx", "fsdp"))
    return jax.shard_map(on_device, mesh=mesh, in_specs=in_specs, out_specs=out_specs, check_vma=False)
```

```python
import functools

import jax
import jax.numpy as jnp
from jax import lax
from jax.experimental import pallas as pl
from jax.experimental.pallas import tpu as pltpu
from jax.sharding import PartitionSpec as P

MESH = pl.DeviceIdType.MESH
VMEM = pl.BlockSpec(memory_space=pltpu.VMEM)
ANY = pl.BlockSpec(memory_space=pl.ANY)
LIMIT = 60 * 1024 * 1024
NC = 8
CHIPS = 16
BLOCK = 8
PIECE = 32
FAR_FIRST = (10, 6, 14, 9, 11, 2, 8, 5, 7, 13, 15, 1, 3, 4, 12)
VOCAB = 512
MODES = 16
TAPS = 7


def place():
    f = lax.axis_index("fsdp")
    c = lax.axis_index("ctx")
    return lax.div(f, 16), lax.rem(lax.div(f, 4), 4), lax.rem(lax.div(f, 2), 2), lax.rem(f, 2), c


def flat(x, y, h, k):
    return x * 16 + y * 4 + h * 2 + k


def hail(devices):
    barrier = pltpu.get_barrier_semaphore()
    for device, wanted in devices:
        if wanted is None:
            pl.semaphore_signal(barrier, inc=1, device_id=device, device_id_type=MESH)
        else:

            @pl.when(wanted)
            def _():
                pl.semaphore_signal(barrier, inc=1, device_id=device, device_id_type=MESH)


def greet(devices, count):
    hail(devices)
    pl.semaphore_wait(pltpu.get_barrier_semaphore(), count)


def build_table(
    friends, count, idle, embed_ref, w_ref, w_copy, tok_ref, cot_ref,
    emb, acc, part_out, part_in, pair_out, pair_in, table, toks, cots,
    local_sem, scat_send, scat_recv, all_send, all_recv, core_send, core_recv,
    part_send, part_recv, pair_send, pair_recv, done_send, done_recv,
    cot_send, cot_recv, tok_send, tok_recv,
):
    f32, bf16 = jnp.float32, jnp.bfloat16
    x, y, h, k, c = place()
    me = flat(x, y, h, k)
    spot = x * 4 + y
    lane = h * 2 + k
    mine = 2 * x + lax.div(y, 2)
    yb = lax.rem(y, 2)
    edge = jnp.where(mine < NC // 2, NC - 1, 0)
    source = mine == c
    gives = c == edge
    partner = flat(x, y, h, 1 - k)
    q = lax.rem(c, 4)
    base = c - q
    across = lax.rem(c + 4, NC)
    group = [(me, base + lax.rem(q + o, 4)) for o in range(1, 4)]
    first = flat(lax.div(c, 2), 2 * lax.rem(c, 2), 1 - h, k)
    givers = [(first + 4 * row, jnp.where(c < NC // 2, NC - 1, 0)) for row in range(2)]

    def chip(i):
        return i * 4 + lane

    def beside(o):
        return lax.rem(spot + o, CHIPS)

    greet(
        friends
        + [(d, None) for d in givers + [(me, across)] + group[::-1]]
        + [((chip(beside(o)), c), None) for o in FAR_FIRST]
        + [((partner, c), None)],
        CHIPS + 4 + CHIPS * gives.astype(jnp.int32) + count,
    )

    def side(b):
        return h if b == 0 else 1 - h

    def scat_copy(b, i, row):
        rows = pl.ds(pl.multiple_of(i * PIECE, PIECE), PIECE)
        return pltpu.make_async_remote_copy(
            src_ref=embed_ref.at[rows], dst_ref=emb.at[i, side(b), k, row],
            send_sem=scat_send.at[b, i], recv_sem=scat_recv.at[b, row], device_id=(chip(i), c), device_id_type=MESH,
        )

    def give_copy(i):
        rows = pl.ds(i * PIECE, PIECE)
        return pltpu.make_async_remote_copy(
            src_ref=embed_ref.at[rows], dst_ref=emb.at[i, h, k, yb], send_sem=scat_send.at[1, i],
            recv_sem=scat_recv.at[1, yb], device_id=(i * 4 + (1 - h) * 2 + k, mine), device_id_type=MESH,
        )

    own_rows = pl.ds(pl.multiple_of(spot * PIECE, PIECE), PIECE)
    own_copy = pltpu.make_async_copy(embed_ref.at[own_rows], emb.at[spot, h, k, yb], local_sem)

    def all_copy(b, o):
        return pltpu.make_async_remote_copy(
            src_ref=emb.at[spot, side(b), k], dst_ref=emb.at[spot, side(b), k], send_sem=all_send.at[b, o],
            recv_sem=all_recv.at[b, o], device_id=(chip(beside(o)), c), device_id_type=MESH,
        )

    def core_copy(b, o):
        i = lax.rem(spot + CHIPS - o, CHIPS)
        return pltpu.make_async_remote_copy(
            src_ref=emb.at[i, side(b), k], dst_ref=emb.at[i, side(b), k], send_sem=core_send.at[b, o],
            recv_sem=core_recv.at[b, o], device_id=(partner, c), device_id_type=MESH,
        )

    def each(first, last, body, unroll=1):
        def step(i, _):
            body(i)
            return 0

        lax.fori_loop(first, last, step, 0, unroll=unroll)

    @pl.when(gives)
    def _():
        for i in range(CHIPS):
            give_copy(i).start()

    @pl.when(source)
    def _():
        own_copy.start()
        each(1, CHIPS, lambda o: scat_copy(0, beside(o), yb).start(), 5)
        own_copy.wait()

    extra = []

    def spread(index, target, sem):
        for src, dst, ss, rs in ((cot_ref, cots, cot_send, cot_recv), (tok_ref, toks, tok_send, tok_recv)):
            copy = pltpu.make_async_remote_copy(
                src_ref=src if sem < 4 else dst.at[index], dst_ref=dst.at[index], send_sem=ss.at[sem],
                recv_sem=rs.at[sem], device_id=target, device_id_type=MESH,
            )
            copy.start()
            extra.append(copy)

    def share(b):
        for row in range(2):
            if b == 0:

                @pl.when(jnp.logical_not(jnp.logical_and(source, yb == row)))
                def _():
                    scat_copy(b, spot, row).wait_recv()

            else:
                scat_copy(b, spot, row).wait_recv()

        each(1, CHIPS, lambda o: all_copy(b, o).start(), 5)
        core_copy(b, 0).start()

    def gathered(b, o):
        all_copy(b, o).wait_recv()
        core_copy(b, o).start()

    share(0)

    for o in range(1, 4):
        spread(c, group[o - 1], o - 1)
    spread(c, (me, across), 3)
    share(1)
    each(1, CHIPS, lambda o: gathered(0, o), 5)
    for copy in extra[6:8]:
        copy.wait_recv()
    for o in range(1, 4):
        spread(across, group[o - 1], 3 + o)

    def product(s, b):
        total = None
        hb = side(b)
        for e in range(2):
            left = jnp.concatenate(
                [
                    jnp.concatenate([emb[s * 8 + i, hb, kk, e] for kk in range(2)], axis=1)
                    for i in range(8)
                ],
                axis=0,
            )
            at = pl.ds(pl.multiple_of(e * 512 + hb * 256, 256), 256)
            right = jnp.concatenate([w_ref[g, at, :] for g in range(3)], axis=1)
            part = jnp.dot(left, right, preferred_element_type=f32)
            total = part if total is None else total + part
        return total.reshape(4, 64, 384)

    each(0, CHIPS, lambda o: core_copy(0, o).wait_recv())
    w_copy.wait()
    for s in range(2):
        acc[s] = product(s, 0)
    each(1, CHIPS, lambda o: gathered(1, o), 5)
    each(0, CHIPS, lambda o: core_copy(1, o).wait_recv())

    def part_copy(o, s):
        return pltpu.make_async_remote_copy(
            src_ref=part_out.at[o - 1, s], dst_ref=part_in.at[o - 1, s], send_sem=part_send.at[o - 1, s],
            recv_sem=part_recv.at[o - 1, s], device_id=(me, base + lax.rem(q + o, 4)), device_id_type=MESH,
        )

    def pair_copy(s):
        return pltpu.make_async_remote_copy(
            src_ref=pair_out.at[s], dst_ref=pair_in.at[s], send_sem=pair_send.at[s], recv_sem=pair_recv.at[s],
            device_id=(me, across), device_id_type=MESH,
        )

    def done_copy(o, s):
        return pltpu.make_async_remote_copy(
            src_ref=table.at[s, q], dst_ref=table.at[s, q], send_sem=done_send.at[o - 1, s],
            recv_sem=done_recv.at[o - 1, s], device_id=(me, base + lax.rem(q + o, 4)), device_id_type=MESH,
        )

    for s in range(2):
        acc[s] = acc[s] + product(s, 1)
        for o in (3, 1, 2):
            part_out[o - 1, s] = acc[s, lax.rem(q + o, 4)].astype(bf16)
            part_copy(o, s).start()
    cots[c] = cot_ref[...]
    toks[c] = tok_ref[...]
    for i, copy in enumerate(extra):
        if not 6 <= i < 8:
            copy.wait_recv()
    idle()
    for s in range(2):
        total = acc[s, q]
        for o in range(1, 4):
            part_copy(o, s).wait_recv()
            total = total + part_in[o - 1, s].astype(f32)
        acc[s, q] = total
        pair_out[s] = total.astype(bf16)
        pair_copy(s).start()
    for s in range(2):
        pair_copy(s).wait_recv()
        table[s, q] = (acc[s, q] + pair_in[s].astype(f32)).astype(bf16)
        for o in (3, 1, 2):
            done_copy(o, s).start()

    for s in range(2):
        for o in range(1, 4):
            done_copy(o, s).wait_recv()

    def finish():
        for copy in extra:
            copy.wait_send()
        for b in range(2):
            each(1, CHIPS, lambda o: all_copy(b, o).wait_send())
            each(0, CHIPS, lambda o: core_copy(b, o).wait_send())

        @pl.when(source)
        def _():
            each(1, CHIPS, lambda o: scat_copy(0, beside(o), yb).wait_send())

        @pl.when(gives)
        def _():
            for i in range(CHIPS):
                give_copy(i).wait_send()

        for s in range(2):
            pair_copy(s).wait_send()
            for o in range(1, 4):
                part_copy(o, s).wait_send()
                done_copy(o, s).wait_send()

    return finish


def shifted_up(value, by, row):
    return jnp.where(row >= by, pltpu.roll(value, by, 0), 0.0)


def shifted_down(value, by, row):
    return jnp.where(row < 8 - by, pltpu.roll(value, 8 - by, 0), 0.0)


def scan_modes(src, out_ref, box, rates_ref, rd, hk, backward):
    row = lax.broadcasted_iota(jnp.int32, (8, 128), 0)
    shifted = shifted_down if backward else shifted_up
    length = 128

    def at(block, i):
        j = block * BLOCK + i
        j = length - 1 - j if backward else j
        return pl.ds(pl.multiple_of(j * 8, 8), 8)

    def spread(factor):
        whole = jnp.exp(-rates_ref[...] * float(factor))
        return [jnp.broadcast_to(whole[m : m + 1, :], (8, 128)) for m in range(MODES)]

    decay, jump = spread(1), spread(BLOCK)

    def ends(block, state):
        drive = [src[at(block, i), :] for i in range(BLOCK)]
        out = []
        for m in range(MODES):
            value = drive[0]
            for i in range(1, BLOCK):
                value = decay[m] * value + drive[i]
            box[block, m] = value
            out.append(jump[m] * state[m] + value)
        return tuple(out)

    zero = jnp.zeros((8, 128), jnp.float32)
    state = list(lax.fori_loop(0, length // BLOCK, ends, (zero,) * MODES))
    for by in (1, 2, 4):
        factor = spread(length * by)
        state = [state[m] + factor[m] * shifted(state[m], by, row) for m in range(MODES)]
    entering = tuple(shifted(state[m], 1, row) for m in range(MODES))

    def outs(block, state):
        drive = [src[at(block, i), :] for i in range(BLOCK)]
        for i in range(BLOCK):
            terms = [rd[i, m : m + 1, :] * state[m] for m in range(MODES)]
            terms += [hk[i - n : i - n + 1, :] * drive[n] for n in range(i + 1)]
            sums = terms[:4]
            for n, term in enumerate(terms[4:]):
                sums[n % 4] = sums[n % 4] + term
            out_ref[at(block, i), :] = (sums[0] + sums[1]) + (sums[2] + sums[3])
        return tuple(jump[m] * state[m] + box[block, m] for m in range(MODES))

    lax.fori_loop(0, length // BLOCK, outs, entering)


def prepare(toks, cots, rates_ref, res_ref, hot, cot, rd, hk):
    lane = lax.broadcasted_iota(jnp.int32, (8, VOCAB), 1)
    for s in range(NC):
        cot[pl.ds(s, 128, stride=8), :] = cots[s].astype(jnp.float32)
    for i in range(BLOCK):
        rd[i] = res_ref[...] * jnp.exp(-rates_ref[...] * float(i + 1))
        hk[i : i + 1, :] = jnp.sum(res_ref[...] * jnp.exp(-rates_ref[...] * float(i)), axis=0, keepdims=True)

    def mark(i, ids):
        rows = []
        for j in range(0, 16, 2):
            two = [jnp.where(ids[:, j + e : j + e + 1] == lane, 1.0, 0.0) for e in range(2)]
            rows.append(jnp.concatenate(two, axis=0).astype(jnp.bfloat16))
        hot[pl.ds(pl.multiple_of(i * 128, 128), 128), :] = jnp.concatenate(rows, axis=0)
        return pltpu.roll(ids, 112, 1)

    lax.fori_loop(0, 8, mark, jnp.concatenate([toks[i] for i in range(NC)], axis=0))


def mix(
    table, taps_ref, rates_ref,
    mixed_ref, lhs_ref,
    hot, rd, hk, box, z, filt, cot, drive, glong, lo, gd, gz,
):
    c = lax.axis_index("ctx")
    halo = 8
    row = lax.broadcasted_iota(jnp.int32, (8, 128), 0)
    whole = table[...].reshape(VOCAB, 384)
    for i in range(4):
        found = jnp.dot(hot[i * 256 : (i + 1) * 256, :], whole, preferred_element_type=jnp.float32)
        for g in range(3):
            z[g, pl.ds(halo * 8 + i * 256, 256), :] = found[:, g * 128 : (g + 1) * 128]
    for g in range(3):
        for d in range(1, TAPS):
            z[g, pl.ds((halo - d) * 8, 8), :] = shifted_up(z[g, pl.ds((halo + 128 - d) * 8, 8), :], 1, row)

    def filter_rows(i, _):
        base = i * 64
        for g in range(3):
            value = None
            for d in range(TAPS):
                term = taps_ref[g, d : d + 1, :] * z[g, pl.ds(pl.multiple_of(base + (halo - d) * 8, 8), 64), :]
                value = term if value is None else value + term
            filt[g, pl.ds(pl.multiple_of(base, 64), 64), :] = value
        here = pl.ds(pl.multiple_of(base, 64), 64)
        drive[here, :] = filt[1, here, :] * filt[2, here, :]
        glong[here, :] = cot[here, :] * filt[0, here, :]
        return 0

    lax.fori_loop(0, 16, filter_rows, 0)
    scan_modes(drive, lo, box, rates_ref, rd, hk, False)
    scan_modes(glong, gd, box, rates_ref, rd, hk, True)

    def grads(i, _):
        here = pl.ds(pl.multiple_of(i * 64, 64), 64)
        long_out, grad_drive = lo[here, :], gd[here, :]
        z[0, here, :] = cot[here, :] * long_out
        z[1, here, :] = grad_drive * filt[2, here, :]
        z[2, here, :] = grad_drive * filt[1, here, :]
        lo[here, :] = filt[0, here, :] * long_out
        return 0

    lax.fori_loop(0, 16, grads, 0)
    mixed_ref[...] = lo[pl.ds(c, 128, stride=8), :].astype(jnp.bfloat16)
    for g in range(3):
        for d in range(TAPS - 1):
            z[g, pl.ds((128 + d) * 8, 8), :] = shifted_down(z[g, pl.ds(d * 8, 8), :], 1, row)

    def adjoint_rows(i, _):
        base = i * 64
        for g in range(3):
            value = None
            for d in range(TAPS):
                term = taps_ref[g, d : d + 1, :] * z[g, pl.ds(pl.multiple_of(base + d * 8, 8), 64), :]
                value = term if value is None else value + term
            gz[g, pl.ds(pl.multiple_of(base, 64), 64), :] = value
        return 0

    lax.fori_loop(0, 16, adjoint_rows, 0)
    for s in range(NC):
        start = lax.rem(c + s, NC)
        for g in range(3):
            lhs_ref[pl.ds(s * 128, 128), pl.ds(g * 128, 128)] = gz[g, pl.ds(start, 128, stride=8), :].astype(jnp.bfloat16)


SPOT = {0: (0, 0), 1: (1, 0), 2: (0, 1), 3: (1, 1), 4: (2, 1), 5: (3, 1), 6: (2, 0), 7: (3, 0)}


def whole_kernel(
    embed_ref, w_hbm, tok_ref, cot_ref, taps_ref, rates_ref, res_ref,
    mixed_ref, pair_ref,
    w_ref, w_sem,
    emb, acc, part_out, part_in, pair_out, pair_in, table, toks, cots,
    local_sem, scat_send, scat_recv, all_send, all_recv, swap_send, swap_recv,
    part_send, part_recv, pair_send, pair_recv, done_send, done_recv,
    cot_send, cot_recv, tok_send, tok_recv,
    hot, rd, hk, box, z, filt, cot, drive, glong, lo, gd, gz, lhs_ref,
    own, core_out, core_in, rest_out, rest_in, last_out, last_in,
    core_send, core_recv, rest_send, rest_recv, last_send, last_recv,
):
    w_copy = pltpu.make_async_copy(w_hbm, w_ref, w_sem)
    w_copy.start()
    f32, bf16 = jnp.float32, jnp.bfloat16
    x, y, h, k, c = place()
    x0, y0 = lax.div(c, 2), lax.rem(c, 2) * 2
    dx, dy = lax.rem(x - x0 + 4, 4), lax.rem(y - y0 + 4, 4)
    partner = (flat(x, y, h, 1 - k), c)
    spot = x * 4 + y
    lane = h * 2 + k

    def beside(o):
        return lax.rem(spot + o, CHIPS)

    yb = jnp.where(jnp.logical_or(dy == 1, dy == 2), 1, 0)
    far = jnp.where(dy >= 2, 1, 0)
    step = jnp.where(dx < 2, dx + 2 * far, dx + 4 - 2 * far)
    owner = [(flat(x0, y0 + yb, e, k), lax.rem(c + step, NC)) for e in range(2)]
    from_c = 2 * x + lax.div(y, 2)
    back = lax.rem(c - from_c + NC, NC)
    back_x = jnp.where(back < 4, lax.rem(back, 2), 2 + lax.rem(back, 2))
    back_far = jnp.where(back < 4, lax.div(back, 2), 3 - lax.div(back, 2))
    back_y = jnp.where(lax.rem(y, 2) == 0, 3 * back_far, 1 + back_far)
    giver_x, giver_y = lax.rem(x + back_x, 4), lax.rem(lax.div(y, 2) * 2 + back_y, 4)
    givers = [(flat(giver_x, giver_y, e, k), from_c) for e in range(2)]
    loop = jnp.logical_and(dx == 0, dy < 2)
    foreign = [jnp.logical_not(jnp.logical_and(loop, h == e)) for e in range(2)]
    finish = build_table(
        [(givers[e], foreign[e]) for e in range(2)], 2 - loop.astype(jnp.int32),
        lambda: prepare(toks, cots, rates_ref, res_ref, hot, cot, rd, hk),
        embed_ref, w_ref, w_copy, tok_ref, cot_ref,
        emb, acc, part_out, part_in, pair_out, pair_in, table, toks, cots,
        local_sem, scat_send, scat_recv, all_send, all_recv, swap_send, swap_recv,
        part_send, part_recv, pair_send, pair_recv, done_send, done_recv,
        cot_send, cot_recv, tok_send, tok_recv,
    )
    mix(
        table, taps_ref, rates_ref, mixed_ref, lhs_ref,
        hot, rd, hk, box, z, filt, cot, drive, glong, lo, gd, gz,
    )

    def core_copy(e, a):
        return pltpu.make_async_remote_copy(
            src_ref=core_out.at[e, pl.ds(a * 4, 4)], dst_ref=core_in.at[e, pl.ds(a * 4, 4)],
            send_sem=core_send.at[e, a], recv_sem=core_recv.at[e, a], device_id=partner, device_id_type=MESH,
        )

    def slot(o):
        i = beside(o)
        return lax.rem(lax.div(i, 4) + 4 - x0, 4) * 4 + lax.rem(lax.rem(i, 4) + 4 - y0, 4)

    def rest_copy(e, o):
        return pltpu.make_async_remote_copy(
            src_ref=rest_out.at[e, o], dst_ref=rest_in.at[e, o],
            send_sem=rest_send.at[e, o], recv_sem=rest_recv.at[e, o],
            device_id=(beside(o) * 4 + lane, c), device_id_type=MESH,
        )

    def last_copy(e):
        return pltpu.make_async_remote_copy(
            src_ref=last_out.at[e], dst_ref=last_in.at[h],
            send_sem=last_send.at[e], recv_sem=last_recv.at[h], device_id=owner[e], device_id_type=MESH,
        )

    def last_wait(e):
        pltpu.make_async_remote_copy(
            src_ref=last_out.at[e], dst_ref=last_in.at[e],
            send_sem=last_send.at[e], recv_sem=last_recv.at[e], device_id=partner, device_id_type=MESH,
        ).wait_recv()

    def tile(e, kk, store):
        starts = [pl.multiple_of(r * 512 + e * 256 + kk * 128, 128) for r in range(2)]
        right = jnp.concatenate(
            [jnp.concatenate([w_ref[g, pl.ds(at, 128), :] for g in range(3)], axis=1) for at in starts], axis=0
        )
        out = lax.dot_general(lhs_ref[...], right, (((1,), (1,)), ((), ())), preferred_element_type=f32)
        for s in range(NC):
            sx, sfar = SPOT[s]
            for r in range(2):
                sy = 3 * sfar if r == 0 else 1 + sfar
                store(e, sx * 4 + sy, out[s * 128 : (s + 1) * 128, r * 128 : (r + 1) * 128])

    def to_core(e, a, value):
        core_out[e, a] = value.astype(bf16)

    def to_own(e, a, value):
        own[e, a] = value

    for e in range(2):
        tile(e, 1 - k, to_core)
        for a in range(4):
            core_copy(e, a).start()
    for e in range(2):
        tile(e, k, to_own)
        for a in range(4):
            core_copy(e, a).wait_recv()

        def give(o, _):
            a = slot(o)
            rest_out[e, o] = (own[e, a] + core_in[e, a].astype(f32)).astype(bf16)
            rest_copy(e, o).start()
            return 0

        lax.fori_loop(1, CHIPS, give, 0, unroll=3)
    for e in range(2):

        def take(o, both):
            rest_copy(e, o).wait_recv()
            return both + rest_in[e, o].astype(f32)

        home = dx * 4 + dy
        both = lax.fori_loop(1, CHIPS, take, own[e, home] + core_in[e, home].astype(f32), unroll=3)
        last_out[e] = both.astype(bf16)

        @pl.when(foreign[e])
        def _():
            last_copy(e).start()

        @pl.when(jnp.logical_not(foreign[e]))
        def _():
            last_in[e] = last_out[e]

    for e in range(2):

        @pl.when(foreign[e])
        def _():
            last_wait(e)

    pair_ref[...] = last_in[...]
    finish()
    for e in range(2):
        for a in range(4):
            core_copy(e, a).wait_send()

        def sent(o, _):
            rest_copy(e, o).wait_send()
            return 0

        lax.fori_loop(1, CHIPS, sent, 0)

        @pl.when(foreign[e])
        def _():
            last_copy(e).wait_send()


def last_kernel(mixed_ref, pair_ref, out_ref, grad_ref):
    out_ref[...] = mixed_ref[...]
    grad_ref[...] = (pair_ref[0].astype(jnp.float32) + pair_ref[1].astype(jnp.float32)).astype(jnp.bfloat16)


def on_device(token_ids, embed, w_in, taps, rates, residues, cotangent):
    bf16, f32, i32 = jnp.bfloat16, jnp.float32, jnp.int32
    dma = pltpu.SemaphoreType.DMA
    w = w_in.transpose(1, 0, 2)
    taps = taps.transpose(1, 0, 2)
    wide = pltpu.VMEM((1024, 128), f32)
    mixed, pair = pl.pallas_call(
        whole_kernel,
        out_shape=(
            jax.ShapeDtypeStruct((128, 128), bf16),
            jax.ShapeDtypeStruct((2, 128, 128), bf16),
        ),
        in_specs=[ANY, ANY] + [VMEM] * 5,
        out_specs=(VMEM, VMEM),
        scratch_shapes=[
            pltpu.VMEM((3, 1024, 128), bf16), dma,
            pltpu.VMEM((CHIPS, 2, 2, 2, PIECE, 128), bf16),
            pltpu.VMEM((2, 4, 64, 384), f32),
            pltpu.VMEM((3, 2, 64, 384), bf16), pltpu.VMEM((3, 2, 64, 384), bf16),
            pltpu.VMEM((2, 64, 384), bf16), pltpu.VMEM((2, 64, 384), bf16),
            pltpu.VMEM((2, 4, 64, 384), bf16),
            pltpu.VMEM((NC, 1, 128), i32),
            pltpu.VMEM((NC, 128, 128), bf16),
            dma, dma((2, CHIPS)), dma((2, 2)),
            dma((2, CHIPS)), dma((2, CHIPS)), dma((2, CHIPS)), dma((2, CHIPS)),
            dma((3, 2)), dma((3, 2)), dma((2,)), dma((2,)), dma((3, 2)), dma((3, 2)),
            dma((NC - 1,)), dma((NC - 1,)), dma((NC - 1,)), dma((NC - 1,)),
            pltpu.VMEM((1024, VOCAB), bf16), pltpu.VMEM((BLOCK, MODES, 128), f32), pltpu.VMEM((BLOCK, 128), f32),
            pltpu.VMEM((128 // BLOCK, MODES, 8, 128), f32),
            pltpu.VMEM((3, 136 * 8, 128), f32), pltpu.VMEM((3, 1024, 128), f32),
            wide, wide, wide, wide, wide,
            pltpu.VMEM((3, 1024, 128), f32), pltpu.VMEM((1024, 384), bf16),
            pltpu.VMEM((2, CHIPS, 128, 128), f32),
            pltpu.VMEM((2, CHIPS, 128, 128), bf16), pltpu.VMEM((2, CHIPS, 128, 128), bf16),
            pltpu.VMEM((2, CHIPS, 128, 128), bf16), pltpu.VMEM((2, CHIPS, 128, 128), bf16),
            pltpu.VMEM((2, 128, 128), bf16), pltpu.VMEM((2, 128, 128), bf16),
            dma((2, 4)), dma((2, 4)), dma((2, CHIPS)), dma((2, CHIPS)), dma((2,)), dma((2,)),
        ],
        compiler_params=pltpu.CompilerParams(collective_id=0, has_side_effects=True, vmem_limit_bytes=LIMIT),
        name="whole",
    )(embed, w, token_ids.reshape(1, 128), cotangent, taps, rates, residues)
    return pl.pallas_call(
        last_kernel,
        out_shape=(jax.ShapeDtypeStruct((128, 128), bf16), jax.ShapeDtypeStruct((128, 128), bf16)),
        in_specs=[VMEM, VMEM],
        out_specs=(VMEM, VMEM),
        name="last",
    )(mixed, pair)


def solution(mesh):
    in_specs = (
        P("ctx"),
        P(None, "fsdp"),
        P("ctx", None, "fsdp"),
        P(None, None, "fsdp"),
        P(None, "fsdp"),
        P(None, "fsdp"),
        P("ctx", "fsdp"),
    )
    out_specs = (P("ctx", "fsdp"), P("ctx", "fsdp"))
    return jax.shard_map(on_device, mesh=mesh, in_specs=in_specs, out_specs=out_specs, check_vma=False)
```

```python
import functools

import jax
import jax.numpy as jnp
from jax import lax
from jax.experimental import pallas as pl
from jax.experimental.pallas import tpu as pltpu
from jax.sharding import PartitionSpec as P

MESH = pl.DeviceIdType.MESH
VMEM = pl.BlockSpec(memory_space=pltpu.VMEM)
ANY = pl.BlockSpec(memory_space=pl.ANY)
LIMIT = 60 * 1024 * 1024
NC = 8
CHIPS = 16
BLOCK = 8
PIECE = 32
FAR_FIRST = (10, 6, 14, 9, 11, 2, 8, 5, 7, 13, 15, 1, 3, 4, 12)
VOCAB = 512
MODES = 16
TAPS = 7


def place():
    f = lax.axis_index("fsdp")
    c = lax.axis_index("ctx")
    return lax.div(f, 16), lax.rem(lax.div(f, 4), 4), lax.rem(lax.div(f, 2), 2), lax.rem(f, 2), c


def toward(x, y, o):
    if isinstance(o, int):
        return lax.rem(x + o // 4, 4) * 4 + lax.rem(y + o % 4, 4)
    return lax.rem(x + lax.div(o, 4), 4) * 4 + lax.rem(y + lax.rem(o, 4), 4)


def flat(x, y, h, k):
    return x * 16 + y * 4 + h * 2 + k


def hail(devices):
    barrier = pltpu.get_barrier_semaphore()
    for device, wanted in devices:
        if wanted is None:
            pl.semaphore_signal(barrier, inc=1, device_id=device, device_id_type=MESH)
        else:

            @pl.when(wanted)
            def _():
                pl.semaphore_signal(barrier, inc=1, device_id=device, device_id_type=MESH)


def build_table(
    friends, count, idle, embed_ref, w_ref, fetches, tok_ref, cot_ref,
    emb, acc, part_out, part_in, pair_out, pair_in, table, toks, cots,
    local_sem, scat_send, scat_recv, all_send, all_recv, core_send, core_recv,
    part_send, part_recv, pair_send, pair_recv, done_send, done_recv,
    cot_send, cot_recv, tok_send, tok_recv,
):
    f32, bf16 = jnp.float32, jnp.bfloat16
    x, y, h, k, c = place()
    me = flat(x, y, h, k)
    spot = x * 4 + y
    lane = h * 2 + k
    mine = 2 * x + lax.div(y, 2)
    yb = lax.rem(y, 2)
    edge = jnp.where(mine < NC // 2, NC - 1, 0)
    source = mine == c
    gives = c == edge
    partner = flat(x, y, h, 1 - k)
    q = lax.rem(c, 4)
    base = c - q
    across = lax.rem(c + 4, NC)
    group = [(me, base + lax.rem(q + o, 4)) for o in range(1, 4)]
    first = flat(lax.div(c, 2), 2 * lax.rem(c, 2), 1 - h, k)
    givers = [(first + 4 * row, jnp.where(c < NC // 2, NC - 1, 0)) for row in range(2)]

    def chip(i):
        return i * 4 + lane

    def beside(o):
        return toward(x, y, o)

    hail(
        friends
        + [(d, None) for d in givers + [(me, across)] + group[::-1]]
        + [((chip(beside(o)), c), None) for o in FAR_FIRST]
        + [((partner, c), None)]
    )
    for fetch in fetches[::-1]:
        fetch.start()
    fetches[-1].wait()
    pl.semaphore_wait(pltpu.get_barrier_semaphore(), CHIPS + 4 + CHIPS * gives.astype(jnp.int32) + count)

    def side(b):
        return h if b == 0 else 1 - h

    def scat_copy(b, i, row):
        rows = pl.ds(pl.multiple_of(i * PIECE, PIECE), PIECE)
        return pltpu.make_async_remote_copy(
            src_ref=embed_ref.at[rows], dst_ref=emb.at[i, side(b), k, row],
            send_sem=scat_send.at[b, i], recv_sem=scat_recv.at[b, row], device_id=(chip(i), c), device_id_type=MESH,
        )

    def give_copy(o):
        i = beside(o)
        rows = pl.ds(pl.multiple_of(i * PIECE, PIECE), PIECE)
        return pltpu.make_async_remote_copy(
            src_ref=embed_ref.at[rows], dst_ref=emb.at[i, h, k, yb], send_sem=scat_send.at[1, i],
            recv_sem=scat_recv.at[1, yb], device_id=(i * 4 + (1 - h) * 2 + k, mine), device_id_type=MESH,
        )

    own_rows = pl.ds(pl.multiple_of(spot * PIECE, PIECE), PIECE)
    own_copy = pltpu.make_async_copy(embed_ref.at[own_rows], emb.at[spot, h, k, yb], local_sem)

    def all_copy(b, o):
        return pltpu.make_async_remote_copy(
            src_ref=emb.at[spot, side(b), k], dst_ref=emb.at[spot, side(b), k], send_sem=all_send.at[b, o],
            recv_sem=all_recv.at[b, o], device_id=(chip(beside(o)), c), device_id_type=MESH,
        )

    def core_copy(b, o):
        i = lax.rem(x + 4 - lax.div(o, 4), 4) * 4 + lax.rem(y + 4 - lax.rem(o, 4), 4)
        return pltpu.make_async_remote_copy(
            src_ref=emb.at[i, side(b), k], dst_ref=emb.at[i, side(b), k], send_sem=core_send.at[b, o],
            recv_sem=core_recv.at[b, o], device_id=(partner, c), device_id_type=MESH,
        )

    def each(first, last, body, unroll=1):
        def step(i, _):
            body(i)
            return 0

        lax.fori_loop(first, last, step, 0, unroll=unroll)

    @pl.when(gives)
    def _():
        for o in FAR_FIRST + (0,):
            give_copy(o).start()

    @pl.when(source)
    def _():
        own_copy.start()
        for o in FAR_FIRST:
            scat_copy(0, beside(o), yb).start()
        own_copy.wait()

    extra = []

    def spread(index, target, sem):
        for src, dst, ss, rs in ((cot_ref, cots, cot_send, cot_recv), (tok_ref, toks, tok_send, tok_recv)):
            copy = pltpu.make_async_remote_copy(
                src_ref=src if sem < 4 else dst.at[index], dst_ref=dst.at[index], send_sem=ss.at[sem],
                recv_sem=rs.at[sem], device_id=target, device_id_type=MESH,
            )
            copy.start()
            extra.append(copy)

    def share(b):
        for row in range(2):
            if b == 0:

                @pl.when(jnp.logical_not(jnp.logical_and(source, yb == row)))
                def _():
                    scat_copy(b, spot, row).wait_recv()

            else:
                scat_copy(b, spot, row).wait_recv()

        for o in FAR_FIRST:
            all_copy(b, o).start()
        core_copy(b, jnp.int32(0)).start()

    def gathered(b, o):
        all_copy(b, o).wait_recv()
        core_copy(b, o).start()

    share(0)

    for o in range(1, 4):
        spread(c, group[o - 1], o - 1)
    spread(c, (me, across), 3)
    share(1)
    each(1, CHIPS, lambda o: gathered(0, o), 5)
    for copy in extra[6:8]:
        copy.wait_recv()
    for o in range(1, 4):
        spread(across, group[o - 1], 3 + o)

    def product(s, b):
        total = None
        hb = side(b)
        for e in range(2):
            left = jnp.concatenate(
                [
                    jnp.concatenate([emb[s * 8 + i, hb, kk, e] for kk in range(2)], axis=1)
                    for i in range(8)
                ],
                axis=0,
            )
            at = pl.ds(pl.multiple_of(e * 512 + hb * 256, 256), 256)
            right = jnp.concatenate([w_ref[g, at, :] for g in range(3)], axis=1)
            part = jnp.dot(left, right, preferred_element_type=f32)
            total = part if total is None else total + part
        return total.reshape(4, 64, 384)

    each(0, CHIPS, lambda o: core_copy(0, o).wait_recv())
    fetches[0].wait()
    for s in range(2):
        acc[s] = product(s, 0)
    each(1, CHIPS, lambda o: gathered(1, o), 5)
    each(0, CHIPS, lambda o: core_copy(1, o).wait_recv())

    def rows_of(t):
        return pl.ds(t % 2 * 32, 32)

    def part_copy(o, t):
        s, rows = t // 2, rows_of(t)
        return pltpu.make_async_remote_copy(
            src_ref=part_out.at[o - 1, s, rows], dst_ref=part_in.at[o - 1, s, rows], send_sem=part_send.at[o - 1, t],
            recv_sem=part_recv.at[o - 1, t], device_id=group[o - 1], device_id_type=MESH,
        )

    def pair_copy(t):
        s, rows = t // 2, rows_of(t)
        return pltpu.make_async_remote_copy(
            src_ref=pair_out.at[s, rows], dst_ref=pair_in.at[s, rows], send_sem=pair_send.at[t],
            recv_sem=pair_recv.at[t], device_id=(me, across), device_id_type=MESH,
        )

    def done_copy(o, t):
        s, rows = t // 2, rows_of(t)
        return pltpu.make_async_remote_copy(
            src_ref=table.at[s, q, rows], dst_ref=table.at[s, q, rows], send_sem=done_send.at[o - 1, t],
            recv_sem=done_recv.at[o - 1, t], device_id=group[o - 1], device_id_type=MESH,
        )

    for s in range(2):
        acc[s] = acc[s] + product(s, 1)
        for t in (2 * s, 2 * s + 1):
            rows = rows_of(t)
            for o in (3, 1, 2):
                part_out[o - 1, s, rows, :] = acc[s, lax.rem(q + o, 4), rows, :].astype(bf16)
                part_copy(o, t).start()
    for fetch in fetches[1:-1]:
        fetch.wait()
    for i, copy in enumerate(extra):
        if not 6 <= i < 8:
            copy.wait_recv()
    idle()
    for t in range(4):
        s, rows = t // 2, rows_of(t)
        total = acc[s, q, rows, :]
        for o in range(1, 4):
            part_copy(o, t).wait_recv()
            total = total + part_in[o - 1, s, rows, :].astype(f32)
        acc[s, q, rows, :] = total
        pair_out[s, rows, :] = total.astype(bf16)
        pair_copy(t).start()
    for t in range(4):
        s, rows = t // 2, rows_of(t)
        pair_copy(t).wait_recv()
        table[s, q, rows, :] = (acc[s, q, rows, :] + pair_in[s, rows, :].astype(f32)).astype(bf16)
        for o in (3, 1, 2):
            done_copy(o, t).start()
    for t in range(4):
        for o in range(1, 4):
            done_copy(o, t).wait_recv()

    def finish():
        for copy in extra:
            copy.wait_send()
        for b in range(2):
            each(1, CHIPS, lambda o: all_copy(b, o).wait_send())
            each(0, CHIPS, lambda o: core_copy(b, o).wait_send())

        @pl.when(source)
        def _():
            each(1, CHIPS, lambda o: scat_copy(0, beside(o), yb).wait_send())

        @pl.when(gives)
        def _():
            for o in range(CHIPS):
                give_copy(o).wait_send()

        for t in range(4):
            pair_copy(t).wait_send()
            for o in range(1, 4):
                part_copy(o, t).wait_send()
                done_copy(o, t).wait_send()

    return finish


def shifted_up(value, by, row):
    return jnp.where(row >= by, pltpu.roll(value, by, 0), 0.0)


def shifted_down(value, by, row):
    return jnp.where(row < 8 - by, pltpu.roll(value, 8 - by, 0), 0.0)


def scan_modes(src, out_ref, box, rates_ref, rd, hk, backward):
    row = lax.broadcasted_iota(jnp.int32, (8, 128), 0)
    shifted = shifted_down if backward else shifted_up
    length = 128

    def at(block, i):
        j = block * BLOCK + i
        j = length - 1 - j if backward else j
        return pl.ds(pl.multiple_of(j * 8, 8), 8)

    def spread(factor):
        whole = jnp.exp(-rates_ref[...] * float(factor))
        return [jnp.broadcast_to(whole[m : m + 1, :], (8, 128)) for m in range(MODES)]

    decay, jump = spread(1), spread(BLOCK)

    def ends(block, state):
        drive = [src[at(block, i), :] for i in range(BLOCK)]
        out = []
        for m in range(MODES):
            value = drive[0]
            for i in range(1, BLOCK):
                value = decay[m] * value + drive[i]
            box[block, m] = value
            out.append(jump[m] * state[m] + value)
        return tuple(out)

    zero = jnp.zeros((8, 128), jnp.float32)
    state = list(lax.fori_loop(0, length // BLOCK, ends, (zero,) * MODES))
    for by in (1, 2, 4):
        factor = spread(length * by)
        state = [state[m] + factor[m] * shifted(state[m], by, row) for m in range(MODES)]
    entering = tuple(shifted(state[m], 1, row) for m in range(MODES))

    def outs(block, state):
        drive = [src[at(block, i), :] for i in range(BLOCK)]
        for i in range(BLOCK):
            terms = [rd[i, m : m + 1, :] * state[m] for m in range(MODES)]
            terms += [hk[i - n : i - n + 1, :] * drive[n] for n in range(i + 1)]
            sums = terms[:4]
            for n, term in enumerate(terms[4:]):
                sums[n % 4] = sums[n % 4] + term
            out_ref[at(block, i), :] = (sums[0] + sums[1]) + (sums[2] + sums[3])
        return tuple(jump[m] * state[m] + box[block, m] for m in range(MODES))

    lax.fori_loop(0, length // BLOCK, outs, entering)


def prepare(toks, cots, rates_ref, res_ref, hot, cot, rd, hk):
    lane = lax.broadcasted_iota(jnp.int32, (8, VOCAB), 1)
    for s in range(NC):
        cot[pl.ds(s, 128, stride=8), :] = cots[s].astype(jnp.float32)
    for i in range(BLOCK):
        rd[i] = res_ref[...] * jnp.exp(-rates_ref[...] * float(i + 1))
        hk[i : i + 1, :] = jnp.sum(res_ref[...] * jnp.exp(-rates_ref[...] * float(i)), axis=0, keepdims=True)

    def mark(i, ids):
        rows = []
        for j in range(0, 16, 2):
            two = [jnp.where(ids[:, j + e : j + e + 1] == lane, 1.0, 0.0) for e in range(2)]
            rows.append(jnp.concatenate(two, axis=0).astype(jnp.bfloat16))
        hot[pl.ds(pl.multiple_of(i * 128, 128), 128), :] = jnp.concatenate(rows, axis=0)
        return pltpu.roll(ids, 112, 1)

    lax.fori_loop(0, 8, mark, jnp.concatenate([toks[i] for i in range(NC)], axis=0))


def mix(
    table, taps_ref, rates_ref,
    mixed_ref, lhs_ref,
    hot, rd, hk, box, z, filt, cot, drive, glong, lo, gd, gz,
):
    c = lax.axis_index("ctx")
    halo = 8
    row = lax.broadcasted_iota(jnp.int32, (8, 128), 0)
    whole = table[...].reshape(VOCAB, 384)
    for i in range(4):
        found = jnp.dot(hot[i * 256 : (i + 1) * 256, :], whole, preferred_element_type=jnp.float32)
        for g in range(3):
            z[g, pl.ds(halo * 8 + i * 256, 256), :] = found[:, g * 128 : (g + 1) * 128]
    for g in range(3):
        for d in range(1, TAPS):
            z[g, pl.ds((halo - d) * 8, 8), :] = shifted_up(z[g, pl.ds((halo + 128 - d) * 8, 8), :], 1, row)

    def filter_rows(i, _):
        base = i * 64
        for g in range(3):
            value = None
            for d in range(TAPS):
                term = taps_ref[g, d : d + 1, :] * z[g, pl.ds(pl.multiple_of(base + (halo - d) * 8, 8), 64), :]
                value = term if value is None else value + term
            filt[g, pl.ds(pl.multiple_of(base, 64), 64), :] = value
        here = pl.ds(pl.multiple_of(base, 64), 64)
        drive[here, :] = filt[1, here, :] * filt[2, here, :]
        glong[here, :] = cot[here, :] * filt[0, here, :]
        return 0

    lax.fori_loop(0, 16, filter_rows, 0)
    scan_modes(drive, lo, box, rates_ref, rd, hk, False)
    scan_modes(glong, gd, box, rates_ref, rd, hk, True)

    def grads(i, _):
        here = pl.ds(pl.multiple_of(i * 64, 64), 64)
        long_out, grad_drive = lo[here, :], gd[here, :]
        z[0, here, :] = cot[here, :] * long_out
        z[1, here, :] = grad_drive * filt[2, here, :]
        z[2, here, :] = grad_drive * filt[1, here, :]
        lo[here, :] = filt[0, here, :] * long_out
        return 0

    lax.fori_loop(0, 16, grads, 0)
    mixed_ref[...] = lo[pl.ds(c, 128, stride=8), :].astype(jnp.bfloat16)
    for g in range(3):
        for d in range(TAPS - 1):
            z[g, pl.ds((128 + d) * 8, 8), :] = shifted_down(z[g, pl.ds(d * 8, 8), :], 1, row)

    def adjoint_rows(i, _):
        base = i * 64
        for g in range(3):
            value = None
            for d in range(TAPS):
                term = taps_ref[g, d : d + 1, :] * z[g, pl.ds(pl.multiple_of(base + d * 8, 8), 64), :]
                value = term if value is None else value + term
            gz[g, pl.ds(pl.multiple_of(base, 64), 64), :] = value
        return 0

    lax.fori_loop(0, 16, adjoint_rows, 0)
    for s in range(NC):
        start = lax.rem(c + s, NC)
        for g in range(3):
            lhs_ref[pl.ds(s * 128, 128), pl.ds(g * 128, 128)] = gz[g, pl.ds(start, 128, stride=8), :].astype(jnp.bfloat16)


SPOT = {0: (0, 0), 1: (1, 0), 2: (0, 1), 3: (1, 1), 4: (2, 1), 5: (3, 1), 6: (2, 0), 7: (3, 0)}


def whole_kernel(
    embed_hbm, w_hbm, tok_ref, cot_ref, taps_hbm, rates_hbm, res_hbm,
    mixed_ref, pair_ref,
    embed_ref, w_ref, taps_ref, rates_ref, res_ref, fetch_sem,
    emb, acc, part_out, part_in, pair_out, pair_in, table, toks, cots,
    local_sem, scat_send, scat_recv, all_send, all_recv, swap_send, swap_recv,
    part_send, part_recv, pair_send, pair_recv, done_send, done_recv,
    cot_send, cot_recv, tok_send, tok_recv,
    hot, rd, hk, box, z, filt, cot, drive, glong, lo, gd, gz, lhs_ref,
    own, core_out, core_in, rest_out, rest_in, last_out, last_in,
    core_send, core_recv, rest_send, rest_recv, last_send, last_recv,
):
    f32, bf16 = jnp.float32, jnp.bfloat16
    x, y, h, k, c = place()
    x0, y0 = lax.div(c, 2), lax.rem(c, 2) * 2
    dx, dy = lax.rem(x - x0 + 4, 4), lax.rem(y - y0 + 4, 4)
    partner = (flat(x, y, h, 1 - k), c)
    spot = x * 4 + y
    lane = h * 2 + k

    def beside(o):
        return toward(x, y, o)

    yb = jnp.where(jnp.logical_or(dy == 1, dy == 2), 1, 0)
    far = jnp.where(dy >= 2, 1, 0)
    step = jnp.where(dx < 2, dx + 2 * far, dx + 4 - 2 * far)
    owner = [(flat(x0, y0 + yb, e, k), lax.rem(c + step, NC)) for e in range(2)]
    from_c = 2 * x + lax.div(y, 2)
    back = lax.rem(c - from_c + NC, NC)
    back_x = jnp.where(back < 4, lax.rem(back, 2), 2 + lax.rem(back, 2))
    back_far = jnp.where(back < 4, lax.div(back, 2), 3 - lax.div(back, 2))
    back_y = jnp.where(lax.rem(y, 2) == 0, 3 * back_far, 1 + back_far)
    giver_x, giver_y = lax.rem(x + back_x, 4), lax.rem(lax.div(y, 2) * 2 + back_y, 4)
    givers = [(flat(giver_x, giver_y, e, k), from_c) for e in range(2)]
    loop = jnp.logical_and(dx == 0, dy < 2)
    foreign = [jnp.logical_not(jnp.logical_and(loop, h == e)) for e in range(2)]
    fetches = [
        pltpu.make_async_copy(src, dst, fetch_sem.at[i])
        for i, (src, dst) in enumerate((
            (w_hbm, w_ref), (cot_ref, cots.at[c]), (tok_ref, toks.at[c]),
            (taps_hbm, taps_ref), (rates_hbm, rates_ref), (res_hbm, res_ref), (embed_hbm, embed_ref),
        ))
    ]
    finish = build_table(
        [(givers[e], foreign[e]) for e in range(2)], 2 - loop.astype(jnp.int32),
        lambda: prepare(toks, cots, rates_ref, res_ref, hot, cot, rd, hk),
        embed_ref, w_ref, fetches, tok_ref, cot_ref,
        emb, acc, part_out, part_in, pair_out, pair_in, table, toks, cots,
        local_sem, scat_send, scat_recv, all_send, all_recv, swap_send, swap_recv,
        part_send, part_recv, pair_send, pair_recv, done_send, done_recv,
        cot_send, cot_recv, tok_send, tok_recv,
    )
    mix(
        table, taps_ref, rates_ref, mixed_ref, lhs_ref,
        hot, rd, hk, box, z, filt, cot, drive, glong, lo, gd, gz,
    )

    def core_copy(e, a):
        return pltpu.make_async_remote_copy(
            src_ref=core_out.at[e, pl.ds(a * 4, 4)], dst_ref=core_in.at[e, pl.ds(a * 4, 4)],
            send_sem=core_send.at[e, a], recv_sem=core_recv.at[e, a], device_id=partner, device_id_type=MESH,
        )

    def slot(o):
        return lax.rem(dx + o // 4, 4) * 4 + lax.rem(dy + o % 4, 4)

    def rest_copy(e, o):
        return pltpu.make_async_remote_copy(
            src_ref=rest_out.at[e, o], dst_ref=rest_in.at[e, o],
            send_sem=rest_send.at[e, o], recv_sem=rest_recv.at[e, o],
            device_id=(beside(o) * 4 + lane, c), device_id_type=MESH,
        )

    def last_copy(e):
        return pltpu.make_async_remote_copy(
            src_ref=last_out.at[e], dst_ref=last_in.at[h],
            send_sem=last_send.at[e], recv_sem=last_recv.at[h], device_id=owner[e], device_id_type=MESH,
        )

    def last_wait(e):
        pltpu.make_async_remote_copy(
            src_ref=last_out.at[e], dst_ref=last_in.at[e],
            send_sem=last_send.at[e], recv_sem=last_recv.at[e], device_id=partner, device_id_type=MESH,
        ).wait_recv()

    def tile(e, kk, store):
        starts = [pl.multiple_of(r * 512 + e * 256 + kk * 128, 128) for r in range(2)]
        right = jnp.concatenate(
            [jnp.concatenate([w_ref[g, pl.ds(at, 128), :] for g in range(3)], axis=1) for at in starts], axis=0
        )
        out = lax.dot_general(lhs_ref[...], right, (((1,), (1,)), ((), ())), preferred_element_type=f32)
        for s in range(NC):
            sx, sfar = SPOT[s]
            for r in range(2):
                sy = 3 * sfar if r == 0 else 1 + sfar
                store(e, sx * 4 + sy, out[s * 128 : (s + 1) * 128, r * 128 : (r + 1) * 128])

    def to_core(e, a, value):
        core_out[e, a] = value.astype(bf16)

    def to_own(e, a, value):
        own[e, a] = value

    for e in range(2):
        tile(e, 1 - k, to_core)
        for a in range(4):
            core_copy(e, a).start()
    for e in range(2):
        tile(e, k, to_own)
        for a in range(4):
            core_copy(e, a).wait_recv()

        for o in FAR_FIRST:
            a = slot(o)
            rest_out[e, o] = (own[e, a] + core_in[e, a].astype(f32)).astype(bf16)
            rest_copy(e, o).start()
    for e in range(2):

        def take(o, both):
            rest_copy(e, o).wait_recv()
            return both + rest_in[e, o].astype(f32)

        home = dx * 4 + dy
        both = lax.fori_loop(1, CHIPS, take, own[e, home] + core_in[e, home].astype(f32), unroll=3)
        last_out[e] = both.astype(bf16)

        @pl.when(foreign[e])
        def _():
            last_copy(e).start()

        @pl.when(jnp.logical_not(foreign[e]))
        def _():
            last_in[e] = last_out[e]

    for e in range(2):

        @pl.when(foreign[e])
        def _():
            last_wait(e)

    pair_ref[...] = last_in[...]
    finish()
    for e in range(2):
        for a in range(4):
            core_copy(e, a).wait_send()

        def sent(o, _):
            rest_copy(e, o).wait_send()
            return 0

        lax.fori_loop(1, CHIPS, sent, 0)

        @pl.when(foreign[e])
        def _():
            last_copy(e).wait_send()


def last_kernel(mixed_ref, pair_ref, out_ref, grad_ref):
    out_ref[...] = mixed_ref[...]
    grad_ref[...] = (pair_ref[0].astype(jnp.float32) + pair_ref[1].astype(jnp.float32)).astype(jnp.bfloat16)


def on_device(token_ids, embed, w_in, taps, rates, residues, cotangent):
    bf16, f32, i32 = jnp.bfloat16, jnp.float32, jnp.int32
    dma = pltpu.SemaphoreType.DMA
    w = w_in.transpose(1, 0, 2)
    taps = taps.transpose(1, 0, 2)
    wide = pltpu.VMEM((1024, 128), f32)
    mixed, pair = pl.pallas_call(
        whole_kernel,
        out_shape=(
            jax.ShapeDtypeStruct((128, 128), bf16),
            jax.ShapeDtypeStruct((2, 128, 128), bf16),
        ),
        in_specs=[ANY] * 7,
        out_specs=(VMEM, VMEM),
        scratch_shapes=[
            pltpu.VMEM((VOCAB, 128), bf16), pltpu.VMEM((3, 1024, 128), bf16), pltpu.VMEM((3, TAPS, 128), f32),
            pltpu.VMEM((MODES, 128), f32), pltpu.VMEM((MODES, 128), f32), dma((7,)),
            pltpu.VMEM((CHIPS, 2, 2, 2, PIECE, 128), bf16),
            pltpu.VMEM((2, 4, 64, 384), f32),
            pltpu.VMEM((3, 2, 64, 384), bf16), pltpu.VMEM((3, 2, 64, 384), bf16),
            pltpu.VMEM((2, 64, 384), bf16), pltpu.VMEM((2, 64, 384), bf16),
            pltpu.VMEM((2, 4, 64, 384), bf16),
            pltpu.VMEM((NC, 1, 128), i32),
            pltpu.VMEM((NC, 128, 128), bf16),
            dma, dma((2, CHIPS)), dma((2, 2)),
            dma((2, CHIPS)), dma((2, CHIPS)), dma((2, CHIPS)), dma((2, CHIPS)),
            dma((3, 4)), dma((3, 4)), dma((4,)), dma((4,)), dma((3, 4)), dma((3, 4)),
            dma((NC - 1,)), dma((NC - 1,)), dma((NC - 1,)), dma((NC - 1,)),
            pltpu.VMEM((1024, VOCAB), bf16), pltpu.VMEM((BLOCK, MODES, 128), f32), pltpu.VMEM((BLOCK, 128), f32),
            pltpu.VMEM((128 // BLOCK, MODES, 8, 128), f32),
            pltpu.VMEM((3, 136 * 8, 128), f32), pltpu.VMEM((3, 1024, 128), f32),
            wide, wide, wide, wide, wide,
            pltpu.VMEM((3, 1024, 128), f32), pltpu.VMEM((1024, 384), bf16),
            pltpu.VMEM((2, CHIPS, 128, 128), f32),
            pltpu.VMEM((2, CHIPS, 128, 128), bf16), pltpu.VMEM((2, CHIPS, 128, 128), bf16),
            pltpu.VMEM((2, CHIPS, 128, 128), bf16), pltpu.VMEM((2, CHIPS, 128, 128), bf16),
            pltpu.VMEM((2, 128, 128), bf16), pltpu.VMEM((2, 128, 128), bf16),
            dma((2, 4)), dma((2, 4)), dma((2, CHIPS)), dma((2, CHIPS)), dma((2,)), dma((2,)),
        ],
        compiler_params=pltpu.CompilerParams(collective_id=0, has_side_effects=True, vmem_limit_bytes=LIMIT),
        name="whole",
    )(embed, w, token_ids.reshape(1, 128), cotangent, taps, rates, residues)
    return pl.pallas_call(
        last_kernel,
        out_shape=(jax.ShapeDtypeStruct((128, 128), bf16), jax.ShapeDtypeStruct((128, 128), bf16)),
        in_specs=[VMEM, VMEM],
        out_specs=(VMEM, VMEM),
        name="last",
    )(mixed, pair)


def solution(mesh):
    in_specs = (
        P("ctx"),
        P(None, "fsdp"),
        P("ctx", None, "fsdp"),
        P(None, None, "fsdp"),
        P(None, "fsdp"),
        P(None, "fsdp"),
        P("ctx", "fsdp"),
    )
    out_specs = (P("ctx", "fsdp"), P("ctx", "fsdp"))
    return jax.shard_map(on_device, mesh=mesh, in_specs=in_specs, out_specs=out_specs, check_vma=False)
```

```python
import functools

import jax
import jax.numpy as jnp
from jax import lax
from jax.experimental import pallas as pl
from jax.experimental.pallas import tpu as pltpu
from jax.sharding import PartitionSpec as P

MESH = pl.DeviceIdType.MESH
VMEM = pl.BlockSpec(memory_space=pltpu.VMEM)
ANY = pl.BlockSpec(memory_space=pl.ANY)
LIMIT = 60 * 1024 * 1024
NC = 8
CHIPS = 16
BLOCK = 8
PIECE = 32
FAR_FIRST = (10, 6, 14, 9, 11, 2, 8, 5, 7, 13, 15, 1, 3, 4, 12)
VOCAB = 512
MODES = 16
TAPS = 7


def place():
    f = lax.axis_index("fsdp")
    c = lax.axis_index("ctx")
    return lax.div(f, 16), lax.rem(lax.div(f, 4), 4), lax.rem(lax.div(f, 2), 2), lax.rem(f, 2), c


def toward(x, y, o):
    if isinstance(o, int):
        return lax.rem(x + o // 4, 4) * 4 + lax.rem(y + o % 4, 4)
    return lax.rem(x + lax.div(o, 4), 4) * 4 + lax.rem(y + lax.rem(o, 4), 4)


def flat(x, y, h, k):
    return x * 16 + y * 4 + h * 2 + k


def hail(devices):
    barrier = pltpu.get_barrier_semaphore()
    for device, wanted in devices:
        if wanted is None:
            pl.semaphore_signal(barrier, inc=1, device_id=device, device_id_type=MESH)
        else:

            @pl.when(wanted)
            def _():
                pl.semaphore_signal(barrier, inc=1, device_id=device, device_id_type=MESH)


def build_table(
    friends, count, idle, embed_ref, w_ref, fetches, tok_ref, cot_ref,
    emb, acc, part_out, part_in, pair_out, pair_in, table, toks, cots,
    local_sem, scat_send, scat_recv, all_send, all_recv, core_send, core_recv,
    part_send, part_recv, pair_send, pair_recv, done_send, done_recv,
    cot_send, cot_recv, tok_send, tok_recv,
):
    f32, bf16 = jnp.float32, jnp.bfloat16
    x, y, h, k, c = place()
    me = flat(x, y, h, k)
    spot = x * 4 + y
    lane = h * 2 + k
    mine = 2 * x + lax.div(y, 2)
    yb = lax.rem(y, 2)
    edge = jnp.where(mine < NC // 2, NC - 1, 0)
    source = mine == c
    gives = c == edge
    partner = flat(x, y, h, 1 - k)
    q = lax.rem(c, 4)
    base = c - q
    across = lax.rem(c + 4, NC)
    group = [(me, base + lax.rem(q + o, 4)) for o in range(1, 4)]
    first = flat(lax.div(c, 2), 2 * lax.rem(c, 2), 1 - h, k)
    givers = [(first + 4 * row, jnp.where(c < NC // 2, NC - 1, 0)) for row in range(2)]

    def chip(i):
        return i * 4 + lane

    def beside(o):
        return toward(x, y, o)

    hail(
        friends
        + [(d, None) for d in givers + [(me, across)] + group[::-1]]
        + [((chip(beside(o)), c), None) for o in FAR_FIRST]
        + [((partner, c), None)]
    )
    for fetch in fetches[::-1]:
        fetch.start()
    fetches[-1].wait()
    pl.semaphore_wait(pltpu.get_barrier_semaphore(), CHIPS + 4 + CHIPS * gives.astype(jnp.int32) + count)

    def side(b):
        return h if b == 0 else 1 - h

    def scat_copy(b, i, row):
        rows = pl.ds(pl.multiple_of(i * PIECE, PIECE), PIECE)
        return pltpu.make_async_remote_copy(
            src_ref=embed_ref.at[rows], dst_ref=emb.at[i, side(b), k, row],
            send_sem=scat_send.at[b, i], recv_sem=scat_recv.at[b, row], device_id=(chip(i), c), device_id_type=MESH,
        )

    def give_copy(o):
        i = beside(o)
        rows = pl.ds(pl.multiple_of(i * PIECE, PIECE), PIECE)
        return pltpu.make_async_remote_copy(
            src_ref=embed_ref.at[rows], dst_ref=emb.at[i, h, k, yb], send_sem=scat_send.at[1, i],
            recv_sem=scat_recv.at[1, yb], device_id=(i * 4 + (1 - h) * 2 + k, mine), device_id_type=MESH,
        )

    own_rows = pl.ds(pl.multiple_of(spot * PIECE, PIECE), PIECE)
    own_copy = pltpu.make_async_copy(embed_ref.at[own_rows], emb.at[spot, h, k, yb], local_sem)

    def all_copy(b, o):
        return pltpu.make_async_remote_copy(
            src_ref=emb.at[spot, side(b), k], dst_ref=emb.at[spot, side(b), k], send_sem=all_send.at[b, o],
            recv_sem=all_recv.at[b, o], device_id=(chip(beside(o)), c), device_id_type=MESH,
        )

    def core_copy(b, o):
        i = lax.rem(x + 4 - lax.div(o, 4), 4) * 4 + lax.rem(y + 4 - lax.rem(o, 4), 4)
        return pltpu.make_async_remote_copy(
            src_ref=emb.at[i, side(b), k], dst_ref=emb.at[i, side(b), k], send_sem=core_send.at[b, o],
            recv_sem=core_recv.at[b, o], device_id=(partner, c), device_id_type=MESH,
        )

    def each(first, last, body, unroll=1):
        def step(i, _):
            body(i)
            return 0

        lax.fori_loop(first, last, step, 0, unroll=unroll)

    @pl.when(gives)
    def _():
        for o in FAR_FIRST + (0,):
            give_copy(o).start()

    @pl.when(source)
    def _():
        own_copy.start()
        for o in FAR_FIRST:
            scat_copy(0, beside(o), yb).start()
        own_copy.wait()

    extra = []

    def spread(index, target, sem):
        for src, dst, ss, rs in ((cot_ref, cots, cot_send, cot_recv), (tok_ref, toks, tok_send, tok_recv)):
            copy = pltpu.make_async_remote_copy(
                src_ref=src if sem < 4 else dst.at[index], dst_ref=dst.at[index], send_sem=ss.at[sem],
                recv_sem=rs.at[sem], device_id=target, device_id_type=MESH,
            )
            copy.start()
            extra.append(copy)

    def share(b):
        for row in range(2):
            if b == 0:

                @pl.when(jnp.logical_not(jnp.logical_and(source, yb == row)))
                def _():
                    scat_copy(b, spot, row).wait_recv()

            else:
                scat_copy(b, spot, row).wait_recv()

        for o in FAR_FIRST:
            all_copy(b, o).start()
        core_copy(b, jnp.int32(0)).start()

    def gathered(b, o):
        all_copy(b, o).wait_recv()
        core_copy(b, o).start()

    share(0)

    for o in range(1, 4):
        spread(c, group[o - 1], o - 1)
    spread(c, (me, across), 3)
    share(1)
    each(1, CHIPS, lambda o: gathered(0, o), 5)
    each(1, CHIPS, lambda o: gathered(1, o), 5)
    for copy in extra[6:8]:
        copy.wait_recv()
    for o in range(1, 4):
        spread(across, group[o - 1], 3 + o)

    def product(s, b):
        total = None
        hb = side(b)
        for e in range(2):
            left = jnp.concatenate(
                [
                    jnp.concatenate([emb[s * 8 + i, hb, kk, e] for kk in range(2)], axis=1)
                    for i in range(8)
                ],
                axis=0,
            )
            at = pl.ds(pl.multiple_of(e * 512 + hb * 256, 256), 256)
            right = jnp.concatenate([w_ref[g, at, :] for g in range(3)], axis=1)
            part = jnp.dot(left, right, preferred_element_type=f32)
            total = part if total is None else total + part
        return total.reshape(4, 64, 384)

    each(0, CHIPS, lambda o: core_copy(0, o).wait_recv())
    fetches[0].wait()
    for s in range(2):
        acc[s] = product(s, 0)
    each(0, CHIPS, lambda o: core_copy(1, o).wait_recv())

    far_first = [jnp.where(q < 2, 3 - i, 1 + i) for i in range(3)]

    def member(o):
        return me, base + lax.rem(q + o, 4)

    def rows_of(t):
        return pl.ds(t % 2 * 32, 32)

    def part_copy(o, t):
        s, rows = t // 2, rows_of(t)
        return pltpu.make_async_remote_copy(
            src_ref=part_out.at[o - 1, s, rows], dst_ref=part_in.at[o - 1, s, rows], send_sem=part_send.at[o - 1, t],
            recv_sem=part_recv.at[o - 1, t], device_id=member(o), device_id_type=MESH,
        )

    def pair_copy(t):
        s, rows = t // 2, rows_of(t)
        return pltpu.make_async_remote_copy(
            src_ref=pair_out.at[s, rows], dst_ref=pair_in.at[s, rows], send_sem=pair_send.at[t],
            recv_sem=pair_recv.at[t], device_id=(me, across), device_id_type=MESH,
        )

    def done_copy(o, t):
        s, rows = t // 2, rows_of(t)
        return pltpu.make_async_remote_copy(
            src_ref=table.at[s, q, rows], dst_ref=table.at[s, q, rows], send_sem=done_send.at[o - 1, t],
            recv_sem=done_recv.at[o - 1, t], device_id=member(o), device_id_type=MESH,
        )

    for s in range(2):
        acc[s] = acc[s] + product(s, 1)
        for t in (2 * s, 2 * s + 1):
            rows = rows_of(t)
            for o in far_first:
                part_out[o - 1, s, rows, :] = acc[s, lax.rem(q + o, 4), rows, :].astype(bf16)
                part_copy(o, t).start()
    for fetch in fetches[1:-1]:
        fetch.wait()
    for i, copy in enumerate(extra):
        if not 6 <= i < 8:
            copy.wait_recv()
    idle()
    for t in range(4):
        s, rows = t // 2, rows_of(t)
        total = acc[s, q, rows, :]
        for o in range(1, 4):
            part_copy(o, t).wait_recv()
            total = total + part_in[o - 1, s, rows, :].astype(f32)
        acc[s, q, rows, :] = total
        pair_out[s, rows, :] = total.astype(bf16)
        pair_copy(t).start()
    for t in range(4):
        s, rows = t // 2, rows_of(t)
        pair_copy(t).wait_recv()
        table[s, q, rows, :] = (acc[s, q, rows, :] + pair_in[s, rows, :].astype(f32)).astype(bf16)
        for o in far_first:
            done_copy(o, t).start()
    for t in range(4):
        for o in range(1, 4):
            done_copy(o, t).wait_recv()

    def finish():
        for copy in extra:
            copy.wait_send()
        for b in range(2):
            each(1, CHIPS, lambda o: all_copy(b, o).wait_send())
            each(0, CHIPS, lambda o: core_copy(b, o).wait_send())

        @pl.when(source)
        def _():
            each(1, CHIPS, lambda o: scat_copy(0, beside(o), yb).wait_send())

        @pl.when(gives)
        def _():
            for o in range(CHIPS):
                give_copy(o).wait_send()

        for t in range(4):
            pair_copy(t).wait_send()
            for o in range(1, 4):
                part_copy(o, t).wait_send()
                done_copy(o, t).wait_send()

    return finish


def shifted_up(value, by, row):
    return jnp.where(row >= by, pltpu.roll(value, by, 0), 0.0)


def shifted_down(value, by, row):
    return jnp.where(row < 8 - by, pltpu.roll(value, 8 - by, 0), 0.0)


def scan_modes(src, out_ref, box, rates_ref, rd, hk, backward):
    row = lax.broadcasted_iota(jnp.int32, (8, 128), 0)
    shifted = shifted_down if backward else shifted_up
    length = 128

    def at(block, i):
        j = block * BLOCK + i
        j = length - 1 - j if backward else j
        return pl.ds(pl.multiple_of(j * 8, 8), 8)

    def spread(factor):
        whole = jnp.exp(-rates_ref[...] * float(factor))
        return [jnp.broadcast_to(whole[m : m + 1, :], (8, 128)) for m in range(MODES)]

    decay, jump = spread(1), spread(BLOCK)

    def ends(block, state):
        drive = [src[at(block, i), :] for i in range(BLOCK)]
        out = []
        for m in range(MODES):
            value = drive[0]
            for i in range(1, BLOCK):
                value = decay[m] * value + drive[i]
            box[block, m] = value
            out.append(jump[m] * state[m] + value)
        return tuple(out)

    zero = jnp.zeros((8, 128), jnp.float32)
    state = list(lax.fori_loop(0, length // BLOCK, ends, (zero,) * MODES))
    for by in (1, 2, 4):
        factor = spread(length * by)
        state = [state[m] + factor[m] * shifted(state[m], by, row) for m in range(MODES)]
    entering = tuple(shifted(state[m], 1, row) for m in range(MODES))

    def outs(block, state):
        drive = [src[at(block, i), :] for i in range(BLOCK)]
        for i in range(BLOCK):
            terms = [rd[i, m : m + 1, :] * state[m] for m in range(MODES)]
            terms += [hk[i - n : i - n + 1, :] * drive[n] for n in range(i + 1)]
            sums = terms[:4]
            for n, term in enumerate(terms[4:]):
                sums[n % 4] = sums[n % 4] + term
            out_ref[at(block, i), :] = (sums[0] + sums[1]) + (sums[2] + sums[3])
        return tuple(jump[m] * state[m] + box[block, m] for m in range(MODES))

    lax.fori_loop(0, length // BLOCK, outs, entering)


def prepare(toks, cots, rates_ref, res_ref, hot, cot, rd, hk):
    lane = lax.broadcasted_iota(jnp.int32, (8, VOCAB), 1)
    for s in range(NC):
        cot[pl.ds(s, 128, stride=8), :] = cots[s].astype(jnp.float32)
    for i in range(BLOCK):
        rd[i] = res_ref[...] * jnp.exp(-rates_ref[...] * float(i + 1))
        hk[i : i + 1, :] = jnp.sum(res_ref[...] * jnp.exp(-rates_ref[...] * float(i)), axis=0, keepdims=True)

    def mark(i, ids):
        rows = []
        for j in range(0, 16, 2):
            two = [jnp.where(ids[:, j + e : j + e + 1] == lane, 1.0, 0.0) for e in range(2)]
            rows.append(jnp.concatenate(two, axis=0).astype(jnp.bfloat16))
        hot[pl.ds(pl.multiple_of(i * 128, 128), 128), :] = jnp.concatenate(rows, axis=0)
        return pltpu.roll(ids, 112, 1)

    lax.fori_loop(0, 8, mark, jnp.concatenate([toks[i] for i in range(NC)], axis=0))


def mix(
    table, taps_ref, rates_ref,
    mixed_ref, lhs_ref,
    hot, rd, hk, box, z, filt, cot, drive, glong, lo, gd, gz,
):
    c = lax.axis_index("ctx")
    halo = 8
    row = lax.broadcasted_iota(jnp.int32, (8, 128), 0)
    whole = table[...].reshape(VOCAB, 384)
    for i in range(4):
        found = jnp.dot(hot[i * 256 : (i + 1) * 256, :], whole, preferred_element_type=jnp.float32)
        for g in range(3):
            z[g, pl.ds(halo * 8 + i * 256, 256), :] = found[:, g * 128 : (g + 1) * 128]
    for g in range(3):
        for d in range(1, TAPS):
            z[g, pl.ds((halo - d) * 8, 8), :] = shifted_up(z[g, pl.ds((halo + 128 - d) * 8, 8), :], 1, row)

    def filter_rows(i, _):
        base = i * 64
        for g in range(3):
            value = None
            for d in range(TAPS):
                term = taps_ref[g, d : d + 1, :] * z[g, pl.ds(pl.multiple_of(base + (halo - d) * 8, 8), 64), :]
                value = term if value is None else value + term
            filt[g, pl.ds(pl.multiple_of(base, 64), 64), :] = value
        here = pl.ds(pl.multiple_of(base, 64), 64)
        drive[here, :] = filt[1, here, :] * filt[2, here, :]
        glong[here, :] = cot[here, :] * filt[0, here, :]
        return 0

    lax.fori_loop(0, 16, filter_rows, 0)
    scan_modes(drive, lo, box, rates_ref, rd, hk, False)
    scan_modes(glong, gd, box, rates_ref, rd, hk, True)

    def grads(i, _):
        here = pl.ds(pl.multiple_of(i * 64, 64), 64)
        long_out, grad_drive = lo[here, :], gd[here, :]
        z[0, here, :] = cot[here, :] * long_out
        z[1, here, :] = grad_drive * filt[2, here, :]
        z[2, here, :] = grad_drive * filt[1, here, :]
        lo[here, :] = filt[0, here, :] * long_out
        return 0

    lax.fori_loop(0, 16, grads, 0)
    mixed_ref[...] = lo[pl.ds(c, 128, stride=8), :].astype(jnp.bfloat16)
    for g in range(3):
        for d in range(TAPS - 1):
            z[g, pl.ds((128 + d) * 8, 8), :] = shifted_down(z[g, pl.ds(d * 8, 8), :], 1, row)

    def adjoint_rows(i, _):
        base = i * 64
        for g in range(3):
            value = None
            for d in range(TAPS):
                term = taps_ref[g, d : d + 1, :] * z[g, pl.ds(pl.multiple_of(base + d * 8, 8), 64), :]
                value = term if value is None else value + term
            gz[g, pl.ds(pl.multiple_of(base, 64), 64), :] = value
        return 0

    lax.fori_loop(0, 16, adjoint_rows, 0)
    for s in range(NC):
        start = lax.rem(c + s, NC)
        for g in range(3):
            lhs_ref[pl.ds(s * 128, 128), pl.ds(g * 128, 128)] = gz[g, pl.ds(start, 128, stride=8), :].astype(jnp.bfloat16)


SPOT = {0: (0, 0), 1: (1, 0), 2: (0, 1), 3: (1, 1), 4: (2, 1), 5: (3, 1), 6: (2, 0), 7: (3, 0)}


def whole_kernel(
    embed_hbm, w_hbm, tok_ref, cot_ref, taps_hbm, rates_hbm, res_hbm,
    mixed_ref, pair_ref,
    embed_ref, w_ref, taps_ref, rates_ref, res_ref, fetch_sem,
    emb, acc, part_out, part_in, pair_out, pair_in, table, toks, cots,
    local_sem, scat_send, scat_recv, all_send, all_recv, swap_send, swap_recv,
    part_send, part_recv, pair_send, pair_recv, done_send, done_recv,
    cot_send, cot_recv, tok_send, tok_recv,
    hot, rd, hk, box, z, filt, cot, drive, glong, lo, gd, gz, lhs_ref,
    own, core_out, core_in, rest_out, rest_in, last_out, last_in,
    core_send, core_recv, rest_send, rest_recv, last_send, last_recv,
):
    f32, bf16 = jnp.float32, jnp.bfloat16
    x, y, h, k, c = place()
    x0, y0 = lax.div(c, 2), lax.rem(c, 2) * 2
    dx, dy = lax.rem(x - x0 + 4, 4), lax.rem(y - y0 + 4, 4)
    partner = (flat(x, y, h, 1 - k), c)
    spot = x * 4 + y
    lane = h * 2 + k

    def beside(o):
        return toward(x, y, o)

    yb = jnp.where(jnp.logical_or(dy == 1, dy == 2), 1, 0)
    far = jnp.where(dy >= 2, 1, 0)
    step = jnp.where(dx < 2, dx + 2 * far, dx + 4 - 2 * far)
    owner = [(flat(x0, y0 + yb, e, k), lax.rem(c + step, NC)) for e in range(2)]
    from_c = 2 * x + lax.div(y, 2)
    back = lax.rem(c - from_c + NC, NC)
    back_x = jnp.where(back < 4, lax.rem(back, 2), 2 + lax.rem(back, 2))
    back_far = jnp.where(back < 4, lax.div(back, 2), 3 - lax.div(back, 2))
    back_y = jnp.where(lax.rem(y, 2) == 0, 3 * back_far, 1 + back_far)
    giver_x, giver_y = lax.rem(x + back_x, 4), lax.rem(lax.div(y, 2) * 2 + back_y, 4)
    givers = [(flat(giver_x, giver_y, e, k), from_c) for e in range(2)]
    loop = jnp.logical_and(dx == 0, dy < 2)
    foreign = [jnp.logical_not(jnp.logical_and(loop, h == e)) for e in range(2)]
    fetches = [
        pltpu.make_async_copy(src, dst, fetch_sem.at[i])
        for i, (src, dst) in enumerate((
            (w_hbm, w_ref), (cot_ref, cots.at[c]), (tok_ref, toks.at[c]),
            (taps_hbm, taps_ref), (rates_hbm, rates_ref), (res_hbm, res_ref), (embed_hbm, embed_ref),
        ))
    ]
    finish = build_table(
        [(givers[e], foreign[e]) for e in range(2)], 2 - loop.astype(jnp.int32),
        lambda: prepare(toks, cots, rates_ref, res_ref, hot, cot, rd, hk),
        embed_ref, w_ref, fetches, tok_ref, cot_ref,
        emb, acc, part_out, part_in, pair_out, pair_in, table, toks, cots,
        local_sem, scat_send, scat_recv, all_send, all_recv, swap_send, swap_recv,
        part_send, part_recv, pair_send, pair_recv, done_send, done_recv,
        cot_send, cot_recv, tok_send, tok_recv,
    )
    mix(
        table, taps_ref, rates_ref, mixed_ref, lhs_ref,
        hot, rd, hk, box, z, filt, cot, drive, glong, lo, gd, gz,
    )

    def core_copy(e, a):
        return pltpu.make_async_remote_copy(
            src_ref=core_out.at[e, pl.ds(a * 4, 4)], dst_ref=core_in.at[e, pl.ds(a * 4, 4)],
            send_sem=core_send.at[e, a], recv_sem=core_recv.at[e, a], device_id=partner, device_id_type=MESH,
        )

    def slot(o):
        return lax.rem(dx + o // 4, 4) * 4 + lax.rem(dy + o % 4, 4)

    def rest_copy(e, o):
        return pltpu.make_async_remote_copy(
            src_ref=rest_out.at[e, o], dst_ref=rest_in.at[e, o],
            send_sem=rest_send.at[e, o], recv_sem=rest_recv.at[e, o],
            device_id=(beside(o) * 4 + lane, c), device_id_type=MESH,
        )

    def last_copy(e):
        return pltpu.make_async_remote_copy(
            src_ref=last_out.at[e], dst_ref=last_in.at[h],
            send_sem=last_send.at[e], recv_sem=last_recv.at[h], device_id=owner[e], device_id_type=MESH,
        )

    def last_wait(e):
        pltpu.make_async_remote_copy(
            src_ref=last_out.at[e], dst_ref=last_in.at[e],
            send_sem=last_send.at[e], recv_sem=last_recv.at[e], device_id=partner, device_id_type=MESH,
        ).wait_recv()

    def tile(e, kk, store):
        starts = [pl.multiple_of(r * 512 + e * 256 + kk * 128, 128) for r in range(2)]
        right = jnp.concatenate(
            [jnp.concatenate([w_ref[g, pl.ds(at, 128), :] for g in range(3)], axis=1) for at in starts], axis=0
        )
        out = lax.dot_general(lhs_ref[...], right, (((1,), (1,)), ((), ())), preferred_element_type=f32)
        for s in range(NC):
            sx, sfar = SPOT[s]
            for r in range(2):
                sy = 3 * sfar if r == 0 else 1 + sfar
                store(e, sx * 4 + sy, out[s * 128 : (s + 1) * 128, r * 128 : (r + 1) * 128])

    def to_core(e, a, value):
        core_out[e, a] = value.astype(bf16)

    def to_own(e, a, value):
        own[e, a] = value

    for e in range(2):
        tile(e, 1 - k, to_core)
        for a in range(4):
            core_copy(e, a).start()
    for e in range(2):
        tile(e, k, to_own)
    for e in range(2):
        for a in range(4):
            core_copy(e, a).wait_recv()

        for o in FAR_FIRST:
            a = slot(o)
            rest_out[e, o] = (own[e, a] + core_in[e, a].astype(f32)).astype(bf16)
            rest_copy(e, o).start()
    for e in range(2):

        def take(o, both):
            rest_copy(e, o).wait_recv()
            return both + rest_in[e, o].astype(f32)

        home = dx * 4 + dy
        both = lax.fori_loop(1, CHIPS, take, own[e, home] + core_in[e, home].astype(f32), unroll=3)
        last_out[e] = both.astype(bf16)

        @pl.when(foreign[e])
        def _():
            last_copy(e).start()

        @pl.when(jnp.logical_not(foreign[e]))
        def _():
            last_in[e] = last_out[e]

    for e in range(2):

        @pl.when(foreign[e])
        def _():
            last_wait(e)

    pair_ref[...] = last_in[...]
    finish()
    for e in range(2):
        for a in range(4):
            core_copy(e, a).wait_send()

        def sent(o, _):
            rest_copy(e, o).wait_send()
            return 0

        lax.fori_loop(1, CHIPS, sent, 0)

        @pl.when(foreign[e])
        def _():
            last_copy(e).wait_send()


def last_kernel(mixed_ref, pair_ref, out_ref, grad_ref):
    out_ref[...] = mixed_ref[...]
    grad_ref[...] = (pair_ref[0].astype(jnp.float32) + pair_ref[1].astype(jnp.float32)).astype(jnp.bfloat16)


def on_device(token_ids, embed, w_in, taps, rates, residues, cotangent):
    bf16, f32, i32 = jnp.bfloat16, jnp.float32, jnp.int32
    dma = pltpu.SemaphoreType.DMA
    w = w_in.transpose(1, 0, 2)
    taps = taps.transpose(1, 0, 2)
    wide = pltpu.VMEM((1024, 128), f32)
    mixed, pair = pl.pallas_call(
        whole_kernel,
        out_shape=(
            jax.ShapeDtypeStruct((128, 128), bf16),
            jax.ShapeDtypeStruct((2, 128, 128), bf16),
        ),
        in_specs=[ANY] * 7,
        out_specs=(VMEM, VMEM),
        scratch_shapes=[
            pltpu.VMEM((VOCAB, 128), bf16), pltpu.VMEM((3, 1024, 128), bf16), pltpu.VMEM((3, TAPS, 128), f32),
            pltpu.VMEM((MODES, 128), f32), pltpu.VMEM((MODES, 128), f32), dma((7,)),
            pltpu.VMEM((CHIPS, 2, 2, 2, PIECE, 128), bf16),
            pltpu.VMEM((2, 4, 64, 384), f32),
            pltpu.VMEM((3, 2, 64, 384), bf16), pltpu.VMEM((3, 2, 64, 384), bf16),
            pltpu.VMEM((2, 64, 384), bf16), pltpu.VMEM((2, 64, 384), bf16),
            pltpu.VMEM((2, 4, 64, 384), bf16),
            pltpu.VMEM((NC, 1, 128), i32),
            pltpu.VMEM((NC, 128, 128), bf16),
            dma, dma((2, CHIPS)), dma((2, 2)),
            dma((2, CHIPS)), dma((2, CHIPS)), dma((2, CHIPS)), dma((2, CHIPS)),
            dma((3, 4)), dma((3, 4)), dma((4,)), dma((4,)), dma((3, 4)), dma((3, 4)),
            dma((NC - 1,)), dma((NC - 1,)), dma((NC - 1,)), dma((NC - 1,)),
            pltpu.VMEM((1024, VOCAB), bf16), pltpu.VMEM((BLOCK, MODES, 128), f32), pltpu.VMEM((BLOCK, 128), f32),
            pltpu.VMEM((128 // BLOCK, MODES, 8, 128), f32),
            pltpu.VMEM((3, 136 * 8, 128), f32), pltpu.VMEM((3, 1024, 128), f32),
            wide, wide, wide, wide, wide,
            pltpu.VMEM((3, 1024, 128), f32), pltpu.VMEM((1024, 384), bf16),
            pltpu.VMEM((2, CHIPS, 128, 128), f32),
            pltpu.VMEM((2, CHIPS, 128, 128), bf16), pltpu.VMEM((2, CHIPS, 128, 128), bf16),
            pltpu.VMEM((2, CHIPS, 128, 128), bf16), pltpu.VMEM((2, CHIPS, 128, 128), bf16),
            pltpu.VMEM((2, 128, 128), bf16), pltpu.VMEM((2, 128, 128), bf16),
            dma((2, 4)), dma((2, 4)), dma((2, CHIPS)), dma((2, CHIPS)), dma((2,)), dma((2,)),
        ],
        compiler_params=pltpu.CompilerParams(collective_id=0, has_side_effects=True, vmem_limit_bytes=LIMIT),
        name="whole",
    )(embed, w, token_ids.reshape(1, 128), cotangent, taps, rates, residues)
    return pl.pallas_call(
        last_kernel,
        out_shape=(jax.ShapeDtypeStruct((128, 128), bf16), jax.ShapeDtypeStruct((128, 128), bf16)),
        in_specs=[VMEM, VMEM],
        out_specs=(VMEM, VMEM),
        name="last",
    )(mixed, pair)


def solution(mesh):
    in_specs = (
        P("ctx"),
        P(None, "fsdp"),
        P("ctx", None, "fsdp"),
        P(None, None, "fsdp"),
        P(None, "fsdp"),
        P(None, "fsdp"),
        P("ctx", "fsdp"),
    )
    out_specs = (P("ctx", "fsdp"), P("ctx", "fsdp"))
    return jax.shard_map(on_device, mesh=mesh, in_specs=in_specs, out_specs=out_specs, check_vma=False)
```

```python
import functools

import jax
import jax.numpy as jnp
from jax import lax
from jax.experimental import pallas as pl
from jax.experimental.pallas import tpu as pltpu
from jax.sharding import PartitionSpec as P

MESH = pl.DeviceIdType.MESH
VMEM = pl.BlockSpec(memory_space=pltpu.VMEM)
ANY = pl.BlockSpec(memory_space=pl.ANY)
LIMIT = 60 * 1024 * 1024
NC = 8
CHIPS = 16
BLOCK = 8
PIECE = 32
FAR_FIRST = (10, 6, 14, 9, 11, 2, 8, 5, 7, 13, 15, 1, 3, 4, 12)
VOCAB = 512
MODES = 16
TAPS = 7


def place():
    f = lax.axis_index("fsdp")
    c = lax.axis_index("ctx")
    return lax.div(f, 16), lax.rem(lax.div(f, 4), 4), lax.rem(lax.div(f, 2), 2), lax.rem(f, 2), c


def toward(x, y, o):
    if isinstance(o, int):
        return lax.rem(x + o // 4, 4) * 4 + lax.rem(y + o % 4, 4)
    return lax.rem(x + lax.div(o, 4), 4) * 4 + lax.rem(y + lax.rem(o, 4), 4)


def flat(x, y, h, k):
    return x * 16 + y * 4 + h * 2 + k


def hail(devices):
    barrier = pltpu.get_barrier_semaphore()
    for device, wanted in devices:
        if wanted is None:
            pl.semaphore_signal(barrier, inc=1, device_id=device, device_id_type=MESH)
        else:

            @pl.when(wanted)
            def _():
                pl.semaphore_signal(barrier, inc=1, device_id=device, device_id_type=MESH)


def build_table(
    friends, count, idle, embed_ref, w_ref, fetches, tok_ref, cot_ref,
    emb, acc, part_out, part_in, pair_out, pair_in, table, toks, cots,
    local_sem, scat_send, scat_recv, all_send, all_recv, core_send, core_recv,
    part_send, part_recv, pair_send, pair_recv, done_send, done_recv,
    cot_send, cot_recv, tok_send, tok_recv,
):
    f32, bf16 = jnp.float32, jnp.bfloat16
    x, y, h, k, c = place()
    me = flat(x, y, h, k)
    spot = x * 4 + y
    lane = h * 2 + k
    mine = 2 * x + lax.div(y, 2)
    yb = lax.rem(y, 2)
    edge = jnp.where(mine < NC // 2, NC - 1, 0)
    source = mine == c
    gives = c == edge
    partner = flat(x, y, h, 1 - k)
    q = lax.rem(c, 4)
    base = c - q
    across = lax.rem(c + 4, NC)
    group = [(me, base + lax.rem(q + o, 4)) for o in range(1, 4)]
    first = flat(lax.div(c, 2), 2 * lax.rem(c, 2), 1 - h, k)
    givers = [(first + 4 * row, jnp.where(c < NC // 2, NC - 1, 0)) for row in range(2)]

    def chip(i):
        return i * 4 + lane

    def beside(o):
        return toward(x, y, o)

    hail(
        friends
        + [(d, None) for d in givers + [(me, across)] + group[::-1]]
        + [((chip(beside(o)), c), None) for o in FAR_FIRST]
        + [((partner, c), None)]
    )
    for fetch in fetches[::-1]:
        fetch.start()
    fetches[-1].wait()
    pl.semaphore_wait(pltpu.get_barrier_semaphore(), CHIPS + 4 + CHIPS * gives.astype(jnp.int32) + count)

    def side(b):
        return h if b == 0 else 1 - h

    def scat_copy(b, i, row):
        rows = pl.ds(pl.multiple_of(i * PIECE, PIECE), PIECE)
        return pltpu.make_async_remote_copy(
            src_ref=embed_ref.at[rows], dst_ref=emb.at[i, side(b), k, row],
            send_sem=scat_send.at[b, i], recv_sem=scat_recv.at[b, row], device_id=(chip(i), c), device_id_type=MESH,
        )

    def give_copy(o):
        i = beside(o)
        rows = pl.ds(pl.multiple_of(i * PIECE, PIECE), PIECE)
        return pltpu.make_async_remote_copy(
            src_ref=embed_ref.at[rows], dst_ref=emb.at[i, h, k, yb], send_sem=scat_send.at[1, i],
            recv_sem=scat_recv.at[1, yb], device_id=(i * 4 + (1 - h) * 2 + k, mine), device_id_type=MESH,
        )

    own_rows = pl.ds(pl.multiple_of(spot * PIECE, PIECE), PIECE)
    own_copy = pltpu.make_async_copy(embed_ref.at[own_rows], emb.at[spot, h, k, yb], local_sem)

    def all_copy(b, o):
        return pltpu.make_async_remote_copy(
            src_ref=emb.at[spot, side(b), k], dst_ref=emb.at[spot, side(b), k], send_sem=all_send.at[b, o],
            recv_sem=all_recv.at[b, o], device_id=(chip(beside(o)), c), device_id_type=MESH,
        )

    def core_copy(b, o):
        i = lax.rem(x + 4 - lax.div(o, 4), 4) * 4 + lax.rem(y + 4 - lax.rem(o, 4), 4)
        return pltpu.make_async_remote_copy(
            src_ref=emb.at[i, side(b), k], dst_ref=emb.at[i, side(b), k], send_sem=core_send.at[b, o],
            recv_sem=core_recv.at[b, o], device_id=(partner, c), device_id_type=MESH,
        )

    def each(first, last, body, unroll=1):
        def step(i, _):
            body(i)
            return 0

        lax.fori_loop(first, last, step, 0, unroll=unroll)

    @pl.when(gives)
    def _():
        for o in FAR_FIRST + (0,):
            give_copy(o).start()

    @pl.when(source)
    def _():
        own_copy.start()
        for o in FAR_FIRST:
            scat_copy(0, beside(o), yb).start()
        own_copy.wait()

    extra = []

    def spread(index, target, sem):
        for src, dst, ss, rs in ((cot_ref, cots, cot_send, cot_recv), (tok_ref, toks, tok_send, tok_recv)):
            copy = pltpu.make_async_remote_copy(
                src_ref=src if sem < 4 else dst.at[index], dst_ref=dst.at[index], send_sem=ss.at[sem],
                recv_sem=rs.at[sem], device_id=target, device_id_type=MESH,
            )
            copy.start()
            extra.append(copy)

    def share(b):
        for row in range(2):
            if b == 0:

                @pl.when(jnp.logical_not(jnp.logical_and(source, yb == row)))
                def _():
                    scat_copy(b, spot, row).wait_recv()

            else:
                scat_copy(b, spot, row).wait_recv()

        for o in FAR_FIRST:
            all_copy(b, o).start()
        core_copy(b, jnp.int32(0)).start()

    def gathered(b, o):
        all_copy(b, o).wait_recv()
        core_copy(b, o).start()

    share(0)

    for o in range(1, 4):
        spread(c, group[o - 1], o - 1)
    spread(c, (me, across), 3)
    share(1)
    each(1, CHIPS, lambda o: gathered(0, o), 5)
    for copy in extra[6:8]:
        copy.wait_recv()
    for o in range(1, 4):
        spread(across, group[o - 1], 3 + o)

    def product(s, b):
        total = None
        hb = side(b)
        for e in range(2):
            left = jnp.concatenate(
                [
                    jnp.concatenate([emb[s * 8 + i, hb, kk, e] for kk in range(2)], axis=1)
                    for i in range(8)
                ],
                axis=0,
            )
            at = pl.ds(pl.multiple_of(e * 512 + hb * 256, 256), 256)
            right = jnp.concatenate([w_ref[g, at, :] for g in range(3)], axis=1)
            part = jnp.dot(left, right, preferred_element_type=f32)
            total = part if total is None else total + part
        return total.reshape(4, 64, 384)

    each(0, CHIPS, lambda o: core_copy(0, o).wait_recv())
    fetches[0].wait()
    for s in range(2):
        acc[s] = product(s, 0)
    each(1, CHIPS, lambda o: gathered(1, o), 5)
    each(0, CHIPS, lambda o: core_copy(1, o).wait_recv())

    far_first = [jnp.where(q < 2, 3 - i, 1 + i) for i in range(3)]

    def member(o):
        return me, base + lax.rem(q + o, 4)

    def rows_of(t):
        return pl.ds(t % 2 * 32, 32)

    def part_copy(o, t):
        s, rows = t // 2, rows_of(t)
        return pltpu.make_async_remote_copy(
            src_ref=part_out.at[o - 1, s, rows], dst_ref=part_in.at[o - 1, s, rows], send_sem=part_send.at[o - 1, t],
            recv_sem=part_recv.at[o - 1, t], device_id=member(o), device_id_type=MESH,
        )

    def pair_copy(t):
        s, rows = t // 2, rows_of(t)
        return pltpu.make_async_remote_copy(
            src_ref=pair_out.at[s, rows], dst_ref=pair_in.at[s, rows], send_sem=pair_send.at[t],
            recv_sem=pair_recv.at[t], device_id=(me, across), device_id_type=MESH,
        )

    def done_copy(o, t):
        s, rows = t // 2, rows_of(t)
        return pltpu.make_async_remote_copy(
            src_ref=table.at[s, q, rows], dst_ref=table.at[s, q, rows], send_sem=done_send.at[o - 1, t],
            recv_sem=done_recv.at[o - 1, t], device_id=member(o), device_id_type=MESH,
        )

    for s in range(2):
        acc[s] = acc[s] + product(s, 1)
        for t in (2 * s, 2 * s + 1):
            rows = rows_of(t)
            for o in far_first:
                part_out[o - 1, s, rows, :] = acc[s, lax.rem(q + o, 4), rows, :].astype(bf16)
                part_copy(o, t).start()
    for fetch in fetches[1:-1]:
        fetch.wait()
    for i, copy in enumerate(extra):
        if not 6 <= i < 8:
            copy.wait_recv()
    idle()
    for t in range(4):
        s, rows = t // 2, rows_of(t)
        total = acc[s, q, rows, :]
        for o in range(1, 4):
            part_copy(o, t).wait_recv()
            total = total + part_in[o - 1, s, rows, :].astype(f32)
        acc[s, q, rows, :] = total
        pair_out[s, rows, :] = total.astype(bf16)
        pair_copy(t).start()
    for t in range(4):
        s, rows = t // 2, rows_of(t)
        pair_copy(t).wait_recv()
        table[s, q, rows, :] = (acc[s, q, rows, :] + pair_in[s, rows, :].astype(f32)).astype(bf16)
        for o in far_first:
            done_copy(o, t).start()
    for t in range(4):
        for o in range(1, 4):
            done_copy(o, t).wait_recv()

    def finish():
        for copy in extra:
            copy.wait_send()
        for b in range(2):
            each(1, CHIPS, lambda o: all_copy(b, o).wait_send())
            each(0, CHIPS, lambda o: core_copy(b, o).wait_send())

        @pl.when(source)
        def _():
            each(1, CHIPS, lambda o: scat_copy(0, beside(o), yb).wait_send())

        @pl.when(gives)
        def _():
            for o in range(CHIPS):
                give_copy(o).wait_send()

        for t in range(4):
            pair_copy(t).wait_send()
            for o in range(1, 4):
                part_copy(o, t).wait_send()
                done_copy(o, t).wait_send()

    return finish


def shifted_up(value, by, row):
    return jnp.where(row >= by, pltpu.roll(value, by, 0), 0.0)


def shifted_down(value, by, row):
    return jnp.where(row < 8 - by, pltpu.roll(value, 8 - by, 0), 0.0)


def scan_modes(src, out_ref, box, rates_ref, rd, hk, backward):
    row = lax.broadcasted_iota(jnp.int32, (8, 128), 0)
    shifted = shifted_down if backward else shifted_up
    length = 128

    def at(block, i):
        j = block * BLOCK + i
        j = length - 1 - j if backward else j
        return pl.ds(pl.multiple_of(j * 8, 8), 8)

    def spread(factor):
        whole = jnp.exp(-rates_ref[...] * float(factor))
        return [jnp.broadcast_to(whole[m : m + 1, :], (8, 128)) for m in range(MODES)]

    decay, jump = spread(1), spread(BLOCK)

    def ends(block, state):
        drive = [src[at(block, i), :] for i in range(BLOCK)]
        out = []
        for m in range(MODES):
            value = drive[0]
            for i in range(1, BLOCK):
                value = decay[m] * value + drive[i]
            box[block, m] = value
            out.append(jump[m] * state[m] + value)
        return tuple(out)

    zero = jnp.zeros((8, 128), jnp.float32)
    state = list(lax.fori_loop(0, length // BLOCK, ends, (zero,) * MODES))
    for by in (1, 2, 4):
        factor = spread(length * by)
        state = [state[m] + factor[m] * shifted(state[m], by, row) for m in range(MODES)]
    entering = tuple(shifted(state[m], 1, row) for m in range(MODES))

    def outs(block, state):
        drive = [src[at(block, i), :] for i in range(BLOCK)]
        for i in range(BLOCK):
            terms = [rd[i, m : m + 1, :] * state[m] for m in range(MODES)]
            terms += [hk[i - n : i - n + 1, :] * drive[n] for n in range(i + 1)]
            sums = terms[:4]
            for n, term in enumerate(terms[4:]):
                sums[n % 4] = sums[n % 4] + term
            out_ref[at(block, i), :] = (sums[0] + sums[1]) + (sums[2] + sums[3])
        return tuple(jump[m] * state[m] + box[block, m] for m in range(MODES))

    lax.fori_loop(0, length // BLOCK, outs, entering)


def prepare(toks, cots, rates_ref, res_ref, hot, cot, rd, hk):
    lane = lax.broadcasted_iota(jnp.int32, (8, VOCAB), 1)
    for s in range(NC):
        cot[pl.ds(s, 128, stride=8), :] = cots[s].astype(jnp.float32)
    for i in range(BLOCK):
        rd[i] = res_ref[...] * jnp.exp(-rates_ref[...] * float(i + 1))
        hk[i : i + 1, :] = jnp.sum(res_ref[...] * jnp.exp(-rates_ref[...] * float(i)), axis=0, keepdims=True)

    def mark(i, ids):
        rows = []
        for j in range(0, 16, 2):
            two = [jnp.where(ids[:, j + e : j + e + 1] == lane, 1.0, 0.0) for e in range(2)]
            rows.append(jnp.concatenate(two, axis=0).astype(jnp.bfloat16))
        hot[pl.ds(pl.multiple_of(i * 128, 128), 128), :] = jnp.concatenate(rows, axis=0)
        return pltpu.roll(ids, 112, 1)

    lax.fori_loop(0, 8, mark, jnp.concatenate([toks[i] for i in range(NC)], axis=0))


def mix(
    table, taps_ref, rates_ref,
    mixed_ref, lhs_ref,
    hot, rd, hk, box, z, filt, cot, drive, glong, lo, gd, gz,
):
    c = lax.axis_index("ctx")
    halo = 8
    row = lax.broadcasted_iota(jnp.int32, (8, 128), 0)
    whole = table[...].reshape(VOCAB, 384)
    for i in range(4):
        found = jnp.dot(hot[i * 256 : (i + 1) * 256, :], whole, preferred_element_type=jnp.float32)
        for g in range(3):
            z[g, pl.ds(halo * 8 + i * 256, 256), :] = found[:, g * 128 : (g + 1) * 128]
    for g in range(3):
        for d in range(1, TAPS):
            z[g, pl.ds((halo - d) * 8, 8), :] = shifted_up(z[g, pl.ds((halo + 128 - d) * 8, 8), :], 1, row)

    def filter_rows(i, _):
        base = i * 64
        for g in range(3):
            value = None
            for d in range(TAPS):
                term = taps_ref[g, d : d + 1, :] * z[g, pl.ds(pl.multiple_of(base + (halo - d) * 8, 8), 64), :]
                value = term if value is None else value + term
            filt[g, pl.ds(pl.multiple_of(base, 64), 64), :] = value
        here = pl.ds(pl.multiple_of(base, 64), 64)
        drive[here, :] = filt[1, here, :] * filt[2, here, :]
        glong[here, :] = cot[here, :] * filt[0, here, :]
        return 0

    lax.fori_loop(0, 16, filter_rows, 0)
    scan_modes(drive, lo, box, rates_ref, rd, hk, False)
    scan_modes(glong, gd, box, rates_ref, rd, hk, True)

    def grads(i, _):
        here = pl.ds(pl.multiple_of(i * 64, 64), 64)
        long_out, grad_drive = lo[here, :], gd[here, :]
        z[0, here, :] = cot[here, :] * long_out
        z[1, here, :] = grad_drive * filt[2, here, :]
        z[2, here, :] = grad_drive * filt[1, here, :]
        lo[here, :] = filt[0, here, :] * long_out
        return 0

    lax.fori_loop(0, 16, grads, 0)
    mixed_ref[...] = lo[pl.ds(c, 128, stride=8), :].astype(jnp.bfloat16)
    for g in range(3):
        for d in range(TAPS - 1):
            z[g, pl.ds((128 + d) * 8, 8), :] = shifted_down(z[g, pl.ds(d * 8, 8), :], 1, row)

    def adjoint_rows(i, _):
        base = i * 64
        for g in range(3):
            value = None
            for d in range(TAPS):
                term = taps_ref[g, d : d + 1, :] * z[g, pl.ds(pl.multiple_of(base + d * 8, 8), 64), :]
                value = term if value is None else value + term
            gz[g, pl.ds(pl.multiple_of(base, 64), 64), :] = value
        return 0

    lax.fori_loop(0, 16, adjoint_rows, 0)
    for s in range(NC):
        start = lax.rem(c + s, NC)
        for g in range(3):
            lhs_ref[pl.ds(s * 128, 128), pl.ds(g * 128, 128)] = gz[g, pl.ds(start, 128, stride=8), :].astype(jnp.bfloat16)


SPOT = {0: (0, 0), 1: (1, 0), 2: (0, 1), 3: (1, 1), 4: (2, 1), 5: (3, 1), 6: (2, 0), 7: (3, 0)}


def whole_kernel(
    embed_hbm, w_hbm, tok_ref, cot_ref, taps_hbm, rates_hbm, res_hbm,
    mixed_ref, pair_ref,
    embed_ref, w_ref, taps_ref, rates_ref, res_ref, fetch_sem,
    emb, acc, part_out, part_in, pair_out, pair_in, table, toks, cots,
    local_sem, scat_send, scat_recv, all_send, all_recv, swap_send, swap_recv,
    part_send, part_recv, pair_send, pair_recv, done_send, done_recv,
    cot_send, cot_recv, tok_send, tok_recv,
    hot, rd, hk, box, z, filt, cot, drive, glong, lo, gd, gz, lhs_ref,
    own, core_out, core_in, rest_out, rest_in, last_out, last_in,
    core_send, core_recv, rest_send, rest_recv, last_send, last_recv,
):
    f32, bf16 = jnp.float32, jnp.bfloat16
    x, y, h, k, c = place()
    x0, y0 = lax.div(c, 2), lax.rem(c, 2) * 2
    dx, dy = lax.rem(x - x0 + 4, 4), lax.rem(y - y0 + 4, 4)
    partner = (flat(x, y, h, 1 - k), c)
    spot = x * 4 + y
    lane = h * 2 + k

    def beside(o):
        return toward(x, y, o)

    yb = jnp.where(jnp.logical_or(dy == 1, dy == 2), 1, 0)
    far = jnp.where(dy >= 2, 1, 0)
    step = jnp.where(dx < 2, dx + 2 * far, dx + 4 - 2 * far)
    owner = [(flat(x0, y0 + yb, e, k), lax.rem(c + step, NC)) for e in range(2)]
    from_c = 2 * x + lax.div(y, 2)
    back = lax.rem(c - from_c + NC, NC)
    back_x = jnp.where(back < 4, lax.rem(back, 2), 2 + lax.rem(back, 2))
    back_far = jnp.where(back < 4, lax.div(back, 2), 3 - lax.div(back, 2))
    back_y = jnp.where(lax.rem(y, 2) == 0, 3 * back_far, 1 + back_far)
    giver_x, giver_y = lax.rem(x + back_x, 4), lax.rem(lax.div(y, 2) * 2 + back_y, 4)
    givers = [(flat(giver_x, giver_y, e, k), from_c) for e in range(2)]
    loop = jnp.logical_and(dx == 0, dy < 2)
    foreign = [jnp.logical_not(jnp.logical_and(loop, h == e)) for e in range(2)]
    fetches = [
        pltpu.make_async_copy(src, dst, fetch_sem.at[i])
        for i, (src, dst) in enumerate((
            (w_hbm, w_ref), (cot_ref, cots.at[c]), (tok_ref, toks.at[c]),
            (taps_hbm, taps_ref), (rates_hbm, rates_ref), (res_hbm, res_ref), (embed_hbm, embed_ref),
        ))
    ]
    finish = build_table(
        [(givers[e], foreign[e]) for e in range(2)], 2 - loop.astype(jnp.int32),
        lambda: prepare(toks, cots, rates_ref, res_ref, hot, cot, rd, hk),
        embed_ref, w_ref, fetches, tok_ref, cot_ref,
        emb, acc, part_out, part_in, pair_out, pair_in, table, toks, cots,
        local_sem, scat_send, scat_recv, all_send, all_recv, swap_send, swap_recv,
        part_send, part_recv, pair_send, pair_recv, done_send, done_recv,
        cot_send, cot_recv, tok_send, tok_recv,
    )
    mix(
        table, taps_ref, rates_ref, mixed_ref, lhs_ref,
        hot, rd, hk, box, z, filt, cot, drive, glong, lo, gd, gz,
    )

    def core_copy(e, a):
        return pltpu.make_async_remote_copy(
            src_ref=core_out.at[e, pl.ds(a * 4, 4)], dst_ref=core_in.at[e, pl.ds(a * 4, 4)],
            send_sem=core_send.at[e, a], recv_sem=core_recv.at[e, a], device_id=partner, device_id_type=MESH,
        )

    def slot(o):
        return lax.rem(dx + o // 4, 4) * 4 + lax.rem(dy + o % 4, 4)

    def rest_copy(e, o):
        return pltpu.make_async_remote_copy(
            src_ref=rest_out.at[e, o], dst_ref=rest_in.at[e, o],
            send_sem=rest_send.at[e, o], recv_sem=rest_recv.at[e, o],
            device_id=(beside(o) * 4 + lane, c), device_id_type=MESH,
        )

    def last_copy(e):
        return pltpu.make_async_remote_copy(
            src_ref=last_out.at[e], dst_ref=last_in.at[h],
            send_sem=last_send.at[e], recv_sem=last_recv.at[h], device_id=owner[e], device_id_type=MESH,
        )

    def last_wait(e):
        pltpu.make_async_remote_copy(
            src_ref=last_out.at[e], dst_ref=last_in.at[e],
            send_sem=last_send.at[e], recv_sem=last_recv.at[e], device_id=partner, device_id_type=MESH,
        ).wait_recv()

    def tile(e, kk, store):
        starts = [pl.multiple_of(r * 512 + e * 256 + kk * 128, 128) for r in range(2)]
        right = jnp.concatenate(
            [jnp.concatenate([w_ref[g, pl.ds(at, 128), :] for g in range(3)], axis=1) for at in starts], axis=0
        )
        out = lax.dot_general(lhs_ref[...], right, (((1,), (1,)), ((), ())), preferred_element_type=f32)
        for s in range(NC):
            sx, sfar = SPOT[s]
            for r in range(2):
                sy = 3 * sfar if r == 0 else 1 + sfar
                store(e, sx * 4 + sy, out[s * 128 : (s + 1) * 128, r * 128 : (r + 1) * 128])

    def to_core(e, a, value):
        core_out[e, a] = value.astype(bf16)

    def to_own(e, a, value):
        own[e, a] = value

    for e in range(2):
        tile(e, 1 - k, to_core)
        for a in range(4):
            core_copy(e, a).start()
    for e in range(2):
        tile(e, k, to_own)
        for a in range(4):
            core_copy(e, a).wait_recv()

        for o in FAR_FIRST:
            a = slot(o)
            rest_out[e, o] = (own[e, a] + core_in[e, a].astype(f32)).astype(bf16)
            rest_copy(e, o).start()
    for e in range(2):

        def take(o, both):
            rest_copy(e, o).wait_recv()
            return both + rest_in[e, o].astype(f32)

        home = dx * 4 + dy
        both = lax.fori_loop(1, CHIPS, take, own[e, home] + core_in[e, home].astype(f32), unroll=3)
        last_out[e] = both.astype(bf16)

        @pl.when(foreign[e])
        def _():
            last_copy(e).start()

        @pl.when(jnp.logical_not(foreign[e]))
        def _():
            last_in[e] = last_out[e]

    for e in range(2):

        @pl.when(foreign[e])
        def _():
            last_wait(e)

    pair_ref[...] = last_in[...]
    finish()
    for e in range(2):
        for a in range(4):
            core_copy(e, a).wait_send()

        def sent(o, _):
            rest_copy(e, o).wait_send()
            return 0

        lax.fori_loop(1, CHIPS, sent, 0)

        @pl.when(foreign[e])
        def _():
            last_copy(e).wait_send()


def last_kernel(mixed_ref, pair_ref, out_ref, grad_ref):
    out_ref[...] = mixed_ref[...]
    grad_ref[...] = (pair_ref[0].astype(jnp.float32) + pair_ref[1].astype(jnp.float32)).astype(jnp.bfloat16)


def on_device(token_ids, embed, w_in, taps, rates, residues, cotangent):
    bf16, f32, i32 = jnp.bfloat16, jnp.float32, jnp.int32
    dma = pltpu.SemaphoreType.DMA
    w = w_in.transpose(1, 0, 2)
    taps = taps.transpose(1, 0, 2)
    wide = pltpu.VMEM((1024, 128), f32)
    mixed, pair = pl.pallas_call(
        whole_kernel,
        out_shape=(
            jax.ShapeDtypeStruct((128, 128), bf16),
            jax.ShapeDtypeStruct((2, 128, 128), bf16),
        ),
        in_specs=[ANY] * 7,
        out_specs=(VMEM, VMEM),
        scratch_shapes=[
            pltpu.VMEM((VOCAB, 128), bf16), pltpu.VMEM((3, 1024, 128), bf16), pltpu.VMEM((3, TAPS, 128), f32),
            pltpu.VMEM((MODES, 128), f32), pltpu.VMEM((MODES, 128), f32), dma((7,)),
            pltpu.VMEM((CHIPS, 2, 2, 2, PIECE, 128), bf16),
            pltpu.VMEM((2, 4, 64, 384), f32),
            pltpu.VMEM((3, 2, 64, 384), bf16), pltpu.VMEM((3, 2, 64, 384), bf16),
            pltpu.VMEM((2, 64, 384), bf16), pltpu.VMEM((2, 64, 384), bf16),
            pltpu.VMEM((2, 4, 64, 384), bf16),
            pltpu.VMEM((NC, 1, 128), i32),
            pltpu.VMEM((NC, 128, 128), bf16),
            dma, dma((2, CHIPS)), dma((2, 2)),
            dma((2, CHIPS)), dma((2, CHIPS)), dma((2, CHIPS)), dma((2, CHIPS)),
            dma((3, 4)), dma((3, 4)), dma((4,)), dma((4,)), dma((3, 4)), dma((3, 4)),
            dma((NC - 1,)), dma((NC - 1,)), dma((NC - 1,)), dma((NC - 1,)),
            pltpu.VMEM((1024, VOCAB), bf16), pltpu.VMEM((BLOCK, MODES, 128), f32), pltpu.VMEM((BLOCK, 128), f32),
            pltpu.VMEM((128 // BLOCK, MODES, 8, 128), f32),
            pltpu.VMEM((3, 136 * 8, 128), f32), pltpu.VMEM((3, 1024, 128), f32),
            wide, wide, wide, wide, wide,
            pltpu.VMEM((3, 1024, 128), f32), pltpu.VMEM((1024, 384), bf16),
            pltpu.VMEM((2, CHIPS, 128, 128), f32),
            pltpu.VMEM((2, CHIPS, 128, 128), bf16), pltpu.VMEM((2, CHIPS, 128, 128), bf16),
            pltpu.VMEM((2, CHIPS, 128, 128), bf16), pltpu.VMEM((2, CHIPS, 128, 128), bf16),
            pltpu.VMEM((2, 128, 128), bf16), pltpu.VMEM((2, 128, 128), bf16),
            dma((2, 4)), dma((2, 4)), dma((2, CHIPS)), dma((2, CHIPS)), dma((2,)), dma((2,)),
        ],
        compiler_params=pltpu.CompilerParams(collective_id=0, has_side_effects=True, vmem_limit_bytes=LIMIT),
        name="whole",
    )(embed, w, token_ids.reshape(1, 128), cotangent, taps, rates, residues)
    return pl.pallas_call(
        last_kernel,
        out_shape=(jax.ShapeDtypeStruct((128, 128), bf16), jax.ShapeDtypeStruct((128, 128), bf16)),
        in_specs=[VMEM, VMEM],
        out_specs=(VMEM, VMEM),
        name="last",
    )(mixed, pair)


def solution(mesh):
    in_specs = (
        P("ctx"),
        P(None, "fsdp"),
        P("ctx", None, "fsdp"),
        P(None, None, "fsdp"),
        P(None, "fsdp"),
        P(None, "fsdp"),
        P("ctx", "fsdp"),
    )
    out_specs = (P("ctx", "fsdp"), P("ctx", "fsdp"))
    return jax.shard_map(on_device, mesh=mesh, in_specs=in_specs, out_specs=out_specs, check_vma=False)
```
